32 devices in a mesh: dp: 4 (over y, x), fsdp: 8 (over z, core).
Axes of the slice: x: 2, y: 2, z: 4, core: 2. Of those that a mesh axis runs over, the one named last changes fastest.
Arguments:
- tokens: bfloat16 [32, 512, 768], P(('dp', 'fsdp')), may hold values from -6 to 6
- lengths: int32 [32], P(('dp', 'fsdp')), may hold values from 30 to 512, as said below
- cotangent: bfloat16 [32, 512, 768], P(('dp', 'fsdp')), may hold values from -6 to 6
- query_weight: bfloat16 [768, 768], P('fsdp'), may hold values from -0.21875 to 0.21875
- query_bias: bfloat16 [768], P('fsdp'), may hold values from -3 to 3
- key_weight: bfloat16 [768, 768], P('fsdp'), may hold values from -0.21875 to 0.21875
- value_weight: bfloat16 [768, 768], P('fsdp'), may hold values from -0.21875 to 0.21875
- value_bias: bfloat16 [768], P('fsdp'), may hold values from -3 to 3
- output_weight: bfloat16 [768, 768], P('fsdp'), may hold values from -3.5 to 3.5
- output_bias: bfloat16 [768], P('fsdp'), may hold values from -3 to 3
- first_gain: bfloat16 [768], P('fsdp'), may hold values from 0.25 to 1.75
- first_shift: bfloat16 [768], P('fsdp'), may hold values from -3 to 3
- inner_weight: bfloat16 [768, 3072], P('fsdp'), may hold values from -0.21875 to 0.21875
- inner_bias: bfloat16 [3072], P('fsdp'), may hold values from -3 to 3
- outer_weight: bfloat16 [3072, 768], P('fsdp'), may hold values from -0.109375 to 0.109375
- outer_bias: bfloat16 [768], P('fsdp'), may hold values from -3 to 3
- second_gain: bfloat16 [768], P('fsdp'), may hold values from 0.25 to 1.75
- second_shift: bfloat16 [768], P('fsdp'), may hold values from -3 to 3
Outputs:
- block_output: bfloat16 [32, 512, 768], P(('dp', 'fsdp'))
- input_grad: float32 [32, 512, 768], P(('dp', 'fsdp'))
- query_weight_grad: float32 [768, 768], P('fsdp')
- query_bias_grad: float32 [768], P('fsdp')
- key_weight_grad: float32 [768, 768], P('fsdp')
- value_weight_grad: float32 [768, 768], P('fsdp')
- value_bias_grad: float32 [768], P('fsdp')
- output_weight_grad: float32 [768, 768], P('fsdp')
- output_bias_grad: float32 [768], P('fsdp')
- first_gain_grad: float32 [768], P('fsdp')
- first_shift_grad: float32 [768], P('fsdp')
- inner_weight_grad: float32 [768, 3072], P('fsdp')
- inner_bias_grad: float32 [3072], P('fsdp')
- outer_weight_grad: float32 [3072, 768], P('fsdp')
- outer_bias_grad: float32 [768], P('fsdp')
- second_gain_grad: float32 [768], P('fsdp')
- second_shift_grad: float32 [768], P('fsdp')
The draws below stay inside these ranges and needn't reach their ends.
Inputs may be any that keep to these rules, and one draw needn't show every extreme that they name: Document i holds its true tokens in slots 0 to lengths[i] - 1, the rest is padding; in every draw some document has exactly 512 and another exactly 30.
All inputs are finite; a program needn't handle non-finite values.
Results may differ from the reference program's by a relative error of at most 0.015.
Values may be sent and summed in bfloat16 or wider, within the bound.
No kernel may reach another device: no remote copies, remote signals or barrier semaphores. Data moves between devices by JAX's collectives and lax.ppermute only.
A program may use at most 192 MiB of HBM per device.

```python
import math
import jax
import jax.numpy as jnp
from jax import lax

D = 768
H = 12
HD = 64
FF = 3072
SEQ = 512
MIN_LEN = 30
DOCS = 32


def draw_lengths(key, part):
    key_drawn = jax.random.fold_in(key, 11)
    key_longest = jax.random.fold_in(key, 12)
    key_offset = jax.random.fold_in(key, 13)
    drawn = jax.random.randint(key_drawn, (DOCS,), MIN_LEN, SEQ + 1)
    longest = jax.random.randint(key_longest, (), 0, DOCS)
    offset = jax.random.randint(key_offset, (), 1, DOCS)
    shortest = (longest + offset) % DOCS
    positions = jnp.arange(DOCS, dtype=jnp.int32)
    drawn = jnp.where(positions == longest, SEQ, drawn)
    drawn = jnp.where(positions == shortest, MIN_LEN, drawn)
    return drawn.astype(jnp.int32)


def block_levels(key, dims, cuts, smallest, largest):
    gain = 1.0
    for position, parts in cuts:
        heights = jax.random.uniform(jax.random.fold_in(jax.random.fold_in(key, 6), position), (parts,), jnp.float32, smallest / len(cuts), largest / len(cuts))
        gain = gain * jnp.repeat(jnp.exp(heights), dims[position] // parts).reshape((-1,) + (1,) * (len(dims) - 1 - position))
    return gain


def scatter_about(rng, shape, scale, bound, shards=(), kind=jnp.bfloat16):
    factor_of = block_levels(rng, shape, shards, -0.22, 0.18) if shards else 1.0
    entries = jax.random.normal(rng, shape, jnp.float32) * scale * factor_of
    return jnp.minimum(jnp.maximum(entries, -bound), bound).astype(kind)


def setup_inputs(seed: int = 0) -> dict:
    streams_of = jax.random.split(jax.random.key(seed), 19)
    return {
        "tokens": scatter_about(streams_of[0], (DOCS, SEQ, D), 1.0, 6.0, ((0, 32),)),
        "lengths": draw_lengths(jax.random.fold_in(streams_of[18], 71), 0),
        "cotangent": scatter_about(streams_of[2], (DOCS, SEQ, D), 1.0, 6.0, ((0, 32),)),
        "query_weight": scatter_about(streams_of[3], (D, D), D ** -0.5, 0.21875, ((0, 8),)),
        "query_bias": scatter_about(streams_of[4], (D,), 0.5, 3.0, ((0, 8),)),
        "key_weight": scatter_about(streams_of[5], (D, D), D ** -0.5, 0.21875, ((0, 8),)),
        "value_weight": scatter_about(streams_of[6], (D, D), D ** -0.5, 0.21875, ((0, 8),)),
        "value_bias": scatter_about(streams_of[7], (D,), 0.5, 3.0, ((0, 8),)),
        "output_weight": scatter_about(streams_of[8], (D, D), (max(2 * D // SEQ, 1)) ** -0.5, 3.5, ((0, 8),)),
        "output_bias": scatter_about(streams_of[9], (D,), 0.5, 3.0, ((0, 8),)),
        "first_gain": jnp.clip(1.0 + 0.15 * jax.random.normal(streams_of[10], (D,), jnp.float32), 0.25, 1.75).astype(jnp.bfloat16),
        "first_shift": scatter_about(streams_of[11], (D,), 0.5, 3.0, ((0, 8),)),
        "inner_weight": scatter_about(streams_of[12], (D, FF), D ** -0.5, 0.21875, ((0, 8),)),
        "inner_bias": scatter_about(streams_of[13], (FF,), 0.5, 3.0, ((0, 8),)),
        "outer_weight": scatter_about(streams_of[14], (FF, D), FF ** -0.5, 0.109375, ((0, 8),)),
        "outer_bias": scatter_about(streams_of[15], (D,), 0.5, 3.0, ((0, 8),)),
        "second_gain": jnp.clip(1.0 + 0.15 * jax.random.normal(streams_of[16], (D,), jnp.float32), 0.25, 1.75).astype(jnp.bfloat16),
        "second_shift": scatter_about(streams_of[17], (D,), 0.5, 3.0, ((0, 8),)),
    }


@jax.custom_vjp
def low(v):
    return lax.optimization_barrier(v.astype(jnp.bfloat16)).astype(jnp.float32)

@jax.custom_vjp
def low_back(v):
    return v

def low_keep(v):
    return (low(v), None)

def low_pass(kept, grad):
    return (grad,)

def back_keep(v):
    return (v, None)

def back_low(kept, grad):
    return (low(grad),)
low.defvjp(low_keep, low_pass)
low_back.defvjp(back_keep, back_low)
epsilon = 1e-12
masked_score = -1e+30

def matmul(left, right):
    return jnp.dot(left, right, precision=lax.Precision.HIGHEST)

def normalize(values):
    center = values - lax.optimization_barrier(jnp.mean(values, axis=-1, keepdims=True))
    spread = lax.optimization_barrier(jnp.mean(center * center, axis=-1, keepdims=True))
    return center * lax.rsqrt(spread + epsilon)

def attend(pieces):
    queries, keysets, values, length = pieces
    scores = jnp.einsum('qhd,khd->hqk', queries, keysets, precision=lax.Precision.HIGHEST) * (1.0 / math.sqrt(HD))
    allowed = jnp.arange(SEQ, dtype=jnp.int32) < length
    scores = jnp.where(allowed[None, None, :], scores, masked_score)
    scores = low_back(scores)
    highest = lax.optimization_barrier(jnp.max(scores, axis=-1, keepdims=True))
    exponent = jnp.exp(scores - highest)
    probs = low(exponent / lax.optimization_barrier(jnp.sum(exponent, axis=-1, keepdims=True)))
    mixture = jnp.einsum('hqk,khd->qhd', probs, values, precision=lax.Precision.HIGHEST)
    return mixture.reshape(SEQ, H * HD)

def forward(params, inputs, doc_lengths):
    query_weight, query_bias, key_weight, value_weight, value_bias, output_weight, output_bias, first_gain, first_shift, inner_weight, inner_bias, outer_weight, outer_bias, second_gain, second_shift = params
    doc_count = inputs.shape[0]
    flat_in = inputs.reshape(doc_count * SEQ, D)
    low_in = low(flat_in)
    queries = low(low_back(matmul(low_in, query_weight) + query_bias))
    keysets = low(low_back(matmul(low_in, key_weight)))
    values = low(low_back(matmul(low_in, value_weight) + value_bias))
    shaped = (doc_count, SEQ, H, HD)
    attended = lax.map(jax.checkpoint(attend), (queries.reshape(shaped), keysets.reshape(shaped), values.reshape(shaped), doc_lengths))
    attended = low(low_back(attended.reshape(doc_count * SEQ, D)))
    branch = low_back(matmul(attended, output_weight) + output_bias)
    first_sum = flat_in + branch
    hidden = normalize(first_sum) * first_gain + first_shift
    inner = low_back(matmul(low(hidden), inner_weight) + inner_bias)
    activated = low(inner * 0.5 * (1.0 + lax.erf(inner / math.sqrt(2.0))))
    outer = low_back(matmul(activated, outer_weight) + outer_bias)
    second_sum = hidden + outer
    result = normalize(second_sum) * second_gain + second_shift
    valid = (jnp.arange(SEQ, dtype=jnp.int32)[None, :] < doc_lengths[:, None]).astype(jnp.float32)
    result = result * valid.reshape(doc_count * SEQ, 1)
    return result.reshape(doc_count, SEQ, D)

def reference(tokens, lengths, cotangent, query_weight, query_bias, key_weight, value_weight, value_bias, output_weight, output_bias, first_gain, first_shift, inner_weight, inner_bias, outer_weight, outer_bias, second_gain, second_shift):
    params = tuple((item.astype(jnp.float32) for item in (query_weight, query_bias, key_weight, value_weight, value_bias, output_weight, output_bias, first_gain, first_shift, inner_weight, inner_bias, outer_weight, outer_bias, second_gain, second_shift)))
    group_size = math.gcd(DOCS, max(1, 4096 // SEQ))
    group_count = DOCS // group_size
    grouped_in = tokens.astype(jnp.float32).reshape(group_count, group_size, SEQ, D)
    grouped_cot = cotangent.astype(jnp.float32).reshape(group_count, group_size, SEQ, D)
    grouped_len = lengths.reshape(group_count, group_size)

    def one_group(running, pieces):
        block_in, block_cot, block_len = pieces

        def apply(params_in, inputs):
            return forward(params_in, inputs, block_len)
        result, pullback = jax.vjp(apply, params, block_in)
        param_grads, block_grad = pullback(block_cot)
        running = tuple((summed + added for summed, added in zip(running, param_grads)))
        return (running, (result.astype(jnp.bfloat16), block_grad))
    starting = tuple((jnp.zeros(item.shape, jnp.float32) for item in params))
    summed_grads, (outputs, input_grads) = lax.scan(one_group, starting, (grouped_in, grouped_cot, grouped_len))
    return (outputs.reshape(DOCS, SEQ, D), input_grads.reshape(DOCS, SEQ, D), summed_grads[0], summed_grads[1], summed_grads[2], summed_grads[3], summed_grads[4], summed_grads[5], summed_grads[6], summed_grads[7], summed_grads[8], summed_grads[9], summed_grads[10], summed_grads[11], summed_grads[12], summed_grads[13], summed_grads[14])
```

```python
import functools
import math

import jax
import jax.numpy as jnp
from jax import lax
from jax.experimental import pallas as pl
from jax.experimental.pallas import tpu as pltpu
from jax.sharding import PartitionSpec as P

F32 = jnp.float32
BF16 = jnp.bfloat16
HD = 64
MASKED = -1e30
SCALE = HD ** -0.5
EPSILON = 1e-12
ROOT_HALF = math.sqrt(0.5)
INV_ROOT_TWO_PI = 1.0 / math.sqrt(2.0 * math.pi)

VM = pl.BlockSpec(memory_space=pltpu.VMEM)
SM = pl.BlockSpec(memory_space=pltpu.SMEM)
HB = pl.BlockSpec(memory_space=pl.ANY)


def shape(*dims, dtype=BF16):
    return jax.ShapeDtypeStruct(dims, dtype)


def dot_nn(a, b):
    return lax.dot_general(a, b, (((1,), (0,)), ((), ())), preferred_element_type=F32)


def dot_nt(a, b):
    return lax.dot_general(a, b, (((1,), (1,)), ((), ())), preferred_element_type=F32)


def flip(value):
    return value.astype(F32).T.astype(BF16)


def column_sum(value):
    return jnp.sum(value.astype(F32), axis=0, keepdims=True)


def row_mean(value):
    return jnp.mean(value, axis=-1, keepdims=True)


def aligned(start, size):
    return pl.ds(pl.multiple_of(start, size), size)


class Pieces:
    def __init__(self, arrays, own, sibling, far, far_sibling, stacked):
        self.arrays, self.own, self.sibling = arrays, own, sibling
        self.far, self.far_sibling, self.stacked = far, far_sibling, stacked

    def count(self, blocks):
        return 2 * len(blocks) + 2 * 5 * 3

    def copies(self, refs, me_ref, target, sems, base, blocks):
        i, z, c = me_ref[0], me_ref[1], me_ref[2]
        done = []

        def place(block, z_at, c_at, offset, rows):
            if self.stacked:
                start = (2 * z_at + c_at) * 96 + offset
                return target.at[block, aligned_rows(start, rows), :]
            start = (2 * z_at + c_at) * 384 + block * 96 + offset
            return target.at[aligned_rows(start, rows), :]

        def add(source, where):
            done.append(pltpu.make_async_copy(source, where, sems.at[base + len(done)]))

        for c_at, near, far in ((c, self.own, self.far), (1 - c, self.sibling, self.far_sibling)):
            for block in blocks:
                position, row, lane = near[block]
                add(refs[position].at[pl.ds(row, 96), pl.ds(lane, 768)], place(block, z, c_at, 0, 96))
            for j in range(1, 4):
                for away in range(3):
                    add(refs[far[away]].at[j - 1], place(i ^ away, z ^ j, c_at, 0, 96))
                add(refs[far[3]].at[j - 1], place(i ^ 3, z ^ j, c_at, 0, 48))
                add(refs[far[4]].at[j - 1], place(i ^ 3, z ^ j, c_at, 48, 48))
        return done


def aligned_rows(start, rows):
    return pl.ds(pl.multiple_of(start, 16), rows)


class Whole:
    def __init__(self, arrays, spots, stacked):
        self.arrays, self.spots, self.stacked = arrays, spots, stacked

    def count(self, blocks):
        return len(blocks)

    def copies(self, refs, me_ref, target, sems, base, blocks):
        done = []
        for block in blocks:
            position, row, lane = self.spots[block]
            where = target.at[block] if self.stacked else target.at[pl.ds(block * 768, 768), :]
            source = refs[position].at[pl.ds(row, 768), pl.ds(lane, 768)]
            done.append(pltpu.make_async_copy(source, where, sems.at[base + block]))
        return done


def start_all(copies):
    for copy in copies:
        copy.start()


def wait_all(copies):
    for copy in copies:
        copy.wait()


def pair_masks(dims, axis):
    spot = lax.broadcasted_iota(jnp.int32, dims, axis)
    return spot < HD, spot >= HD


def keep(mask, value):
    return jnp.where(mask, value, jnp.zeros_like(value))


def attend_forward_body(group, me_ref, len_ref, x_ref, vec_ref, *refs):
    sources = refs[: len(group.arrays)]
    q_ref, k_ref, v_ref, att_ref, left_ref, lse_ref, w_ref, sems = refs[len(group.arrays) :]
    seq, width = x_ref.shape
    tile = min(256, seq)
    loads = group.copies(sources, me_ref, w_ref, sems, 0, (0, 1, 2))
    start_all(loads)
    for p in range(width // 128):
        left_ref[0, p * 128 : (p + 1) * 128, :] = flip(x_ref[:, p * 128 : (p + 1) * 128])
    wait_all(loads)

    def project(r, carry):
        rows = aligned(r * tile, tile)
        x = x_ref[rows, :]
        q_ref[rows, :] = (dot_nn(x, w_ref[0]) + vec_ref[0:1, :]).astype(BF16)
        k_ref[rows, :] = dot_nn(x, w_ref[1]).astype(BF16)
        v_ref[rows, :] = (dot_nn(x, w_ref[2]) + vec_ref[1:2, :]).astype(BF16)
        return carry

    lax.fori_loop(0, seq // tile, project, 0)
    length = len_ref[0]

    def pair(p, carry):
        lanes = aligned(p * 128, 128)
        k_pair = k_ref[:, lanes]
        q_t = (q_ref[:, lanes].astype(F32) * SCALE).T.astype(BF16)
        v_t = flip(v_ref[:, lanes])
        masks = pair_masks((128, seq), 0)
        allowed = lax.broadcasted_iota(jnp.int32, (seq, seq), 0) < length
        for e in range(2):
            s = dot_nn(k_pair, keep(masks[e], q_t))
            s = jnp.where(allowed, s, MASKED)
            top = jnp.max(s, axis=0, keepdims=True)
            p_t = jnp.exp(s - top)
            total = jnp.sum(p_t, axis=0, keepdims=True)
            o_t = dot_nn(v_t[e * HD : (e + 1) * HD, :], p_t.astype(BF16)) / total
            left_ref[1, aligned(p * 128 + e * HD, HD), :] = o_t.astype(BF16)
            lse_ref[pl.ds(p * 2 + e, 1), :] = top + jnp.log(total)
        att_ref[:, lanes] = flip(left_ref[1, aligned(p * 128, 128), :])
        return carry

    lax.fori_loop(0, width // 128, pair, 0)


def attend_forward(group, me, length, x, vec):
    seq, width = x.shape
    heads = width // HD
    return pl.pallas_call(
        functools.partial(attend_forward_body, group),
        out_shape=(shape(seq, width),) * 4 + (shape(2, width, seq), shape(-(-heads // 8) * 8, seq, dtype=F32)),
        in_specs=[SM, SM, VM, VM] + [HB] * len(group.arrays),
        out_specs=[VM] * 6,
        scratch_shapes=[pltpu.VMEM((4, width, width), BF16), pltpu.SemaphoreType.DMA((group.count((0, 1, 2)),))],
        cost_estimate=pl.CostEstimate(flops=12_000_000_000, bytes_accessed=20_000_000, transcendentals=3_200_000),
        name="attend_forward",
    )(me, length, x, vec, *group.arrays)


def attend_backward_body(len_ref, q_ref, k_ref, v_ref, do_ref, lse_ref, branch_ref, g_ref, sum_ref):
    seq, width = q_ref.shape
    length = len_ref[0]

    def pair(p, carry):
        lanes = aligned(p * 128, 128)
        q_pair = (q_ref[:, lanes].astype(F32) * SCALE).astype(BF16)
        k_pair = k_ref[:, lanes]
        v_pair = v_ref[:, lanes]
        do_pair = do_ref[:, lanes]
        q_t = flip(q_pair)
        k_t = (k_pair.astype(F32) * SCALE).T.astype(BF16)
        do_t = flip(do_pair)
        sub_masks = pair_masks((128, seq), 0)
        lane_masks = pair_masks((seq, 128), 1)
        allowed = lax.broadcasted_iota(jnp.int32, (seq, seq), 0) < length
        dk = jnp.zeros((seq, 128), F32)
        dv = jnp.zeros((seq, 128), F32)
        dq_t = []
        for e in range(2):
            s = dot_nn(k_pair, keep(sub_masks[e], q_t))
            s = jnp.where(allowed, s, MASKED)
            p_t = jnp.exp(s - lse_ref[pl.ds(p * 2 + e, 1), :])
            dp = dot_nn(v_pair, keep(sub_masks[e], do_t))
            dv = dv + dot_nn(p_t.astype(BF16), keep(lane_masks[e], do_pair))
            t = p_t * dp
            row = jnp.sum(t, axis=0, keepdims=True)
            ds = (t - p_t * row).astype(BF16)
            dk = dk + dot_nn(ds, keep(lane_masks[e], q_pair))
            dq_t.append(dot_nn(k_t[e * HD : (e + 1) * HD, :], ds))
        dq = jnp.concatenate(dq_t, axis=0).T.astype(BF16)
        dv = dv.astype(BF16)
        g_ref[0, :, lanes] = dq
        g_ref[1, :, lanes] = dk.astype(BF16)
        g_ref[2, :, lanes] = dv
        g_ref[3, :, lanes] = branch_ref[:, lanes]
        sum_ref[0:1, lanes] = column_sum(dq)
        sum_ref[1:2, lanes] = column_sum(dv)
        return carry

    lax.fori_loop(0, width // 128, pair, 0)


def attend_backward(length, q, k, v, do, lse, branch):
    seq, width = q.shape
    return pl.pallas_call(
        attend_backward_body,
        out_shape=(shape(4, seq, width), shape(8, width, dtype=F32)),
        in_specs=[SM] + [VM] * 6,
        out_specs=[VM] * 2,
        cost_estimate=pl.CostEstimate(flops=16_000_000_000, bytes_accessed=9_000_000, transcendentals=3_200_000),
        name="attend_backward",
    )(length, q, k, v, do, lse, branch)


def gelu_parts(inner):
    cumulative = 0.5 * (1.0 + lax.erf(inner * ROOT_HALF))
    density = jnp.exp(-0.5 * inner * inner) * INV_ROOT_TWO_PI
    return inner * cumulative, cumulative + inner * density


def middle_forward_body(groups, me_ref, len_ref, x_ref, att_ref, cot_ref, vec_ref, ib_ref, *refs):
    counts = [len(g.arrays) for g in groups]
    sources = [refs[sum(counts[:n]) : sum(counts[: n + 1])] for n in range(3)]
    (out_ref, ssg_ref, low_ref, actT_ref, slope_ref, norm_ref, rstd_ref, hidT_ref, sum_ref, wa, wi, wu, sems) = refs[sum(counts) :]
    seq, width = x_ref.shape
    blocks = wi.shape[0]
    tile = min(256, seq)
    spots = [0, groups[0].count((3,)), groups[0].count((3,)) + groups[1].count(range(blocks))]
    load_a = groups[0].copies(sources[0], me_ref, wa, sems, spots[0], (3,))
    load_i = groups[1].copies(sources[1], me_ref, wi, sems, spots[1], range(blocks))
    load_u = groups[2].copies(sources[2], me_ref, wu, sems, spots[2], range(blocks))
    start_all(load_a + load_i + load_u)
    length = len_ref[0]
    sum_ref[...] = jnp.zeros_like(sum_ref)
    wait_all(load_a + load_i + load_u)

    def rows_step(r, carry):
        rows = aligned(r * tile, tile)
        first = x_ref[rows, :].astype(F32) + dot_nn(att_ref[rows, :], wa[3]) + vec_ref[2:3, :]
        center = first - row_mean(first)
        rstd = lax.rsqrt(row_mean(center * center) + EPSILON)
        normed = center * rstd
        norm_ref[rows, :] = normed
        rstd_ref[rows, :] = rstd
        hidden = normed * vec_ref[3:4, :] + vec_ref[4:5, :]
        low = hidden.astype(BF16)
        hidT_ref[:, rows] = low.astype(F32).T.astype(BF16)

        def block(f, second):
            inner = dot_nn(low, wi[f]) + ib_ref[pl.ds(f, 1), :]
            active, slope = gelu_parts(inner)
            active = active.astype(BF16)
            spot = aligned(f * width, width)
            slope_ref[rows, spot] = slope.astype(BF16)
            actT_ref[spot, rows] = flip(active)
            return second + dot_nn(active, wu[spot, :])

        second = lax.fori_loop(0, blocks, block, hidden + vec_ref[5:6, :])
        center = second - row_mean(second)
        rstd = lax.rsqrt(row_mean(center * center) + EPSILON)
        normed = center * rstd
        spot = r * tile + lax.broadcasted_iota(jnp.int32, (tile, width), 0)
        valid = spot < length
        result = normed * vec_ref[6:7, :] + vec_ref[7:8, :]
        out_ref[rows, :] = jnp.where(valid, result, 0.0).astype(BF16)
        grad = jnp.where(valid, cot_ref[rows, :].astype(F32), 0.0)
        sum_ref[7:8, :] += column_sum(grad)
        sum_ref[6:7, :] += column_sum(grad * normed)
        grad = grad * vec_ref[6:7, :]
        grad = rstd * (grad - row_mean(grad) - normed * row_mean(grad * normed))
        ssg_ref[rows, :] = grad
        low = grad.astype(BF16)
        low_ref[rows, :] = low
        sum_ref[5:6, :] += column_sum(low)
        return carry

    lax.fori_loop(0, seq // tile, rows_step, 0)


def middle_forward(groups, me, length, x, att, cot, vec, ib):
    seq, width = x.shape
    blocks = ib.shape[0]
    count = groups[0].count((3,)) + groups[1].count(range(blocks)) + groups[2].count(range(blocks))
    arrays = [a for g in groups for a in g.arrays]
    return pl.pallas_call(
        functools.partial(middle_forward_body, groups),
        out_shape=(
            shape(seq, width),
            shape(seq, width, dtype=F32),
            shape(seq, width),
            shape(blocks * width, seq),
            shape(seq, blocks * width),
            shape(seq, width, dtype=F32),
            shape(seq, 1, dtype=F32),
            shape(width, seq),
            shape(8, width, dtype=F32),
        ),
        in_specs=[SM, SM] + [VM] * 5 + [HB] * len(arrays),
        out_specs=[VM] * 9,
        scratch_shapes=[
            pltpu.VMEM((4, width, width), BF16),
            pltpu.VMEM((blocks, width, width), BF16),
            pltpu.VMEM((blocks * width, width), BF16),
            pltpu.SemaphoreType.DMA((count,)),
        ],
        cost_estimate=pl.CostEstimate(flops=12_000_000_000, bytes_accessed=30_000_000, transcendentals=3_200_000),
        name="middle_forward",
    )(me, length, x, att, cot, vec, ib, *arrays)


def middle_backward_body(groups, me_ref, low_ref, ssg_ref, slope_ref, norm_ref, rstd_ref, vec_ref, *refs):
    counts = [len(g.arrays) for g in groups]
    sources = [refs[sum(counts[:n]) : sum(counts[: n + 1])] for n in range(3)]
    (igl_ref, fsg_ref, branch_ref, att_ref, ib_ref, sum_ref, wa, wi, wu, sems) = refs[sum(counts) :]
    seq, width = low_ref.shape
    blocks = wi.shape[0]
    tile = min(256, seq)
    spots = [0, groups[0].count((3,)), groups[0].count((3,)) + groups[1].count(range(blocks))]
    load_a = groups[0].copies(sources[0], me_ref, wa, sems, spots[0], (3,))
    load_i = groups[1].copies(sources[1], me_ref, wi, sems, spots[1], range(blocks))
    load_u = groups[2].copies(sources[2], me_ref, wu, sems, spots[2], range(blocks))
    start_all(load_u + load_i + load_a)
    sum_ref[...] = jnp.zeros_like(sum_ref)
    ib_ref[...] = jnp.zeros_like(ib_ref)
    wait_all(load_u + load_i + load_a)

    def rows_step(r, carry):
        rows = aligned(r * tile, tile)
        low = low_ref[rows, :]

        def block(f, grad):
            spot = aligned(f * width, width)
            inner = (dot_nt(low, wu[spot, :]) * slope_ref[rows, spot].astype(F32)).astype(BF16)
            igl_ref[f, rows, :] = inner
            ib_ref[pl.ds(f, 1), :] += column_sum(inner)
            return grad + dot_nt(inner, wi[f])

        grad = lax.fori_loop(0, blocks, block, ssg_ref[rows, :])
        normed = norm_ref[rows, :]
        sum_ref[4:5, :] += column_sum(grad)
        sum_ref[3:4, :] += column_sum(grad * normed)
        grad = grad * vec_ref[3:4, :]
        grad = rstd_ref[rows, :] * (grad - row_mean(grad) - normed * row_mean(grad * normed))
        fsg_ref[rows, :] = grad
        branch = grad.astype(BF16)
        branch_ref[rows, :] = branch
        sum_ref[2:3, :] += column_sum(branch)
        att_ref[rows, :] = dot_nt(branch, wa[3]).astype(BF16)
        return carry

    lax.fori_loop(0, seq // tile, rows_step, 0)


def middle_backward(groups, me, low, ssg, slope, norm, rstd, vec, blocks):
    seq, width = low.shape
    count = groups[0].count((3,)) + groups[1].count(range(blocks)) + groups[2].count(range(blocks))
    arrays = [a for g in groups for a in g.arrays]
    return pl.pallas_call(
        functools.partial(middle_backward_body, groups),
        out_shape=(
            shape(blocks, seq, width),
            shape(seq, width, dtype=F32),
            shape(seq, width),
            shape(seq, width),
            shape(blocks, width, dtype=F32),
            shape(8, width, dtype=F32),
        ),
        in_specs=[SM] + [VM] * 6 + [HB] * len(arrays),
        out_specs=[VM] * 6,
        scratch_shapes=[
            pltpu.VMEM((4, width, width), BF16),
            pltpu.VMEM((blocks, width, width), BF16),
            pltpu.VMEM((blocks * width, width), BF16),
            pltpu.SemaphoreType.DMA((count,)),
        ],
        cost_estimate=pl.CostEstimate(flops=9_000_000_000, bytes_accessed=25_000_000, transcendentals=0),
        name="middle_backward",
    )(me, low, ssg, slope, norm, rstd, vec, *arrays)


def input_grad_body(group, me_ref, g_ref, fsg_ref, *refs):
    sources = refs[: len(group.arrays)]
    out_ref, w_ref, sems = refs[len(group.arrays) :]
    seq, width = fsg_ref.shape
    tile = min(256, seq)
    loads = group.copies(sources, me_ref, w_ref, sems, 0, (0, 1, 2))
    start_all(loads)
    wait_all(loads)

    def rows_step(r, carry):
        rows = aligned(r * tile, tile)
        total = fsg_ref[rows, :]
        for n in range(3):
            total = total + dot_nt(g_ref[n, rows, :], w_ref[n])
        out_ref[rows, :] = total
        return carry

    lax.fori_loop(0, seq // tile, rows_step, 0)


def input_grad(group, me, g, fsg):
    seq, width = fsg.shape
    return pl.pallas_call(
        functools.partial(input_grad_body, group),
        out_shape=shape(seq, width, dtype=F32),
        in_specs=[SM, VM, VM] + [HB] * len(group.arrays),
        out_specs=VM,
        scratch_shapes=[pltpu.VMEM((4, width, width), BF16), pltpu.SemaphoreType.DMA((group.count((0, 1, 2)),))],
        cost_estimate=pl.CostEstimate(flops=4_000_000_000, bytes_accessed=10_000_000, transcendentals=0),
        name="input_grad",
    )(me, g, fsg, *group.arrays)


Z_ORDER = (0, 2, 1, 3)


def weight_grad_body(kind, orders, sibling, summed, me_ref, left_ref, g_ref, *refs):
    if summed:
        add_ref, refs = refs[0], refs[1:]
    outs, left = refs[:-1], refs[-1]
    i, z, c = me_ref[0], me_ref[1], me_ref[2]
    c_at = (1 - c) if sibling else c
    for out_ref, order in zip(outs, orders, strict=True):
        for spot, away in enumerate(order):
            block = i ^ away
            for n, j in enumerate(Z_ORDER):
                z_at = z ^ j
                if kind == "outer":
                    rows = left_ref[aligned_rows((2 * z_at + c_at) * 384 + block * 96, 96), :]
                elif kind == "inner":
                    rows = left_ref[aligned_rows((2 * z_at + c_at) * 96, 96), :]
                else:
                    rows = left_ref[block // 3, aligned_rows((2 * z_at + c_at) * 96, 96), :]
                left[n * 96 : (n + 1) * 96, :] = rows
            right = g_ref[...] if kind == "outer" else g_ref[block]
            total = dot_nn(left[...], right).reshape(4, 96, 768)
            if summed:
                total = total + add_ref[away].astype(F32)
            out_ref[spot] = total.astype(BF16)


def weight_grad(kind, orders, sibling, me, left, g, add=None):
    summed = add is not None
    return pl.pallas_call(
        functools.partial(weight_grad_body, kind, orders, sibling, summed),
        out_shape=tuple(shape(len(order), 4, 96, 768) for order in orders),
        in_specs=[SM, VM, VM] + [VM] * summed,
        out_specs=[VM] * len(orders),
        scratch_shapes=[pltpu.VMEM((384, left.shape[-1]), BF16)],
        cost_estimate=pl.CostEstimate(flops=2_000_000_000, bytes_accessed=6_000_000, transcendentals=0),
        name=f"weight_grad_{kind}",
    )(*((me, left, g) + ((add,) if summed else ())))


def swap(value, axis, size, mask):
    return lax.ppermute(value, axis, [(n, n ^ mask) for n in range(size)])


def gather_group(piece, fsdp, dp):
    far = [swap(piece, "fsdp", fsdp, 2 * j) for j in (1, 2, 3)]
    mine = jnp.stack(far)
    over_x = swap(mine, "dp", dp, 1)
    over_y = swap(mine, "dp", dp, 2)
    half_a = swap(over_x[:, :48], "dp", dp, 2)
    half_b = swap(over_y[:, 48:], "dp", dp, 1)
    near = (mine, over_x, over_y, half_a, half_b)
    return near, tuple(swap(v, "fsdp", fsdp, 1) for v in near)


def add_low(a, b):
    return (a.astype(F32) + b.astype(F32)).astype(BF16)


def scatter_planes(send, held, first, fsdp, dp):
    got = swap(send, "dp", dp, first)
    onward = swap(add_low(held[1], got[1]), "dp", dp, 3 - first)
    return (held[0].astype(F32) + got[0].astype(F32) + onward.astype(F32)).astype(BF16)


def scatter_z(value, fsdp):
    got = swap(value[2:], "fsdp", fsdp, 2)
    onward = swap(add_low(value[1], got[1]), "fsdp", fsdp, 4)
    return (value[0].astype(F32) + got[0].astype(F32) + onward.astype(F32)).astype(BF16)


def spread(value, dp):
    return (value,) + tuple(swap(value, "dp", dp, m) for m in (1, 2, 3))


def pick(pieces, index):
    return jnp.where(index == 0, pieces[0], jnp.where(index == 1, pieces[1], jnp.where(index == 2, pieces[2], pieces[3])))


def in_order(pieces, i):
    return [pick(pieces, n ^ i) for n in range(4)]


def on_device(
    sizes,
    tokens,
    lengths,
    cotangent,
    query_weight,
    query_bias,
    key_weight,
    value_weight,
    value_bias,
    output_weight,
    output_bias,
    first_gain,
    first_shift,
    inner_weight,
    inner_bias,
    outer_weight,
    outer_bias,
    second_gain,
    second_shift,
):
    dp, fsdp = sizes
    docs, seq, width = tokens.shape
    blocks = inner_weight.shape[1] // width
    direct = dp == 4 and fsdp == 8 and docs == 1 and query_weight.shape == (96, 768) and blocks == 4
    i = lax.axis_index("dp")
    f = lax.axis_index("fsdp")
    me = jnp.stack([i, f // 2, f % 2, jnp.zeros_like(i)]).astype(jnp.int32)

    small = (query_bias, value_bias, output_bias, first_gain, first_shift, outer_bias, second_gain, second_shift, inner_bias)
    part = query_bias.shape[0]
    packed = lax.all_gather(jnp.concatenate(small), "fsdp", axis=0, tiled=False).astype(F32)
    vec = packed[:, : 8 * part].reshape(fsdp, 8, part).transpose(1, 0, 2).reshape(8, width)
    ib = packed[:, 8 * part :].reshape(blocks, width)

    if direct:
        mine = (query_weight, key_weight, value_weight, output_weight)
        near_a, far_a = gather_group(pick(mine, i), fsdp, dp)
        near_i, far_i = gather_group(lax.dynamic_slice(inner_weight, (0, i * 768), (96, 768)), fsdp, dp)
        near_u, far_u = gather_group(lax.dynamic_slice(outer_weight, (i * 96, 0), (96, 768)), fsdp, dp)
        theirs = tuple(swap(w, "fsdp", fsdp, 1) for w in mine)
        inner_other = swap(inner_weight, "fsdp", fsdp, 1)
        outer_other = swap(outer_weight, "fsdp", fsdp, 1)
        four = range(4)
        group_a = Pieces(
            mine + theirs + near_a + far_a,
            [(n, 0, 0) for n in four],
            [(4 + n, 0, 0) for n in four],
            tuple(range(8, 13)),
            tuple(range(13, 18)),
            True,
        )
        group_i = Pieces(
            (inner_weight, inner_other) + near_i + far_i,
            [(0, 0, 768 * n) for n in four],
            [(1, 0, 768 * n) for n in four],
            tuple(range(2, 7)),
            tuple(range(7, 12)),
            True,
        )
        group_u = Pieces(
            (outer_weight, outer_other) + near_u + far_u,
            [(0, 96 * n, 0) for n in four],
            [(1, 96 * n, 0) for n in four],
            tuple(range(2, 7)),
            tuple(range(7, 12)),
            False,
        )
    else:
        whole = tuple(
            lax.all_gather(w, "fsdp", axis=0, tiled=True)
            for w in (query_weight, key_weight, value_weight, output_weight, inner_weight, outer_weight)
        )
        group_a = Whole(whole[:4], [(n, 0, 0) for n in range(4)], True)
        group_i = Whole(whole[4:5], [(0, 0, width * n) for n in range(blocks)], True)
        group_u = Whole(whole[5:6], [(0, width * n, 0) for n in range(blocks)], False)

    x = tokens.reshape(seq, width)
    cot = cotangent.reshape(seq, width)
    groups = (group_a, group_i, group_u)
    q, k, v, att, left_a, lse = attend_forward(group_a, me, lengths, x, vec)
    out, ssg, low, act_t, slope, norm, rstd, hid_t, sum_one = middle_forward(groups, me, lengths, x, att, cot, vec, ib)

    if direct:
        (sent_u,) = weight_grad("outer", ((0, 1, 2, 3),), True, me, act_t, low)
        got_u = swap(sent_u, "fsdp", fsdp, 1)
        send_u, held_u = weight_grad("outer", ((1, 3), (0, 2)), False, me, act_t, low, got_u)
        plane_u = scatter_planes(send_u, held_u, 1, fsdp, dp)
    igl, fsg, branch, att_g, ib_sum, sum_two = middle_backward(groups, me, low, ssg, slope, norm, rstd, vec, blocks)
    if direct:
        (sent_i,) = weight_grad("inner", ((0, 1, 2, 3),), True, me, hid_t, igl)
        got_i = swap(sent_i, "fsdp", fsdp, 1)
        send_i, held_i = weight_grad("inner", ((2, 3), (0, 1)), False, me, hid_t, igl, got_i)
        plane_i = scatter_planes(send_i, held_i, 2, fsdp, dp)
    g, sum_three = attend_backward(lengths, q, k, v, att_g, lse, branch)
    in_grad = input_grad(group_a, me, g, fsg)

    vec_sum = jnp.concatenate([sum_three[:2], sum_two[2:5], sum_one[5:8]])
    vec_sum = vec_sum.reshape(8, fsdp, part).transpose(1, 0, 2).reshape(fsdp, 8 * part)
    small_sum = jnp.concatenate([vec_sum, ib_sum.reshape(fsdp, blocks * part)], axis=1)
    small_sum = lax.psum(small_sum, ("dp", "fsdp"))
    small_own = lax.dynamic_index_in_dim(small_sum, f, 0, keepdims=False)
    small_grads = [small_own[n * part : (n + 1) * part] for n in range(8)] + [small_own[8 * part :]]

    if direct:
        (sent_a,) = weight_grad("attend", ((0, 1, 2, 3),), True, me, left_a, g)
        got_a = swap(sent_a, "fsdp", fsdp, 1)
        send_a, held_a = weight_grad("attend", ((1, 3), (0, 2)), False, me, left_a, g, got_a)
        plane_a = scatter_planes(send_a, held_a, 1, fsdp, dp)
        own = [in_order(spread(scatter_z(p, fsdp), dp), i) for p in (plane_a, plane_i, plane_u)]
        q_g, k_g, v_g, o_g = (w.astype(F32) for w in own[0])
        i_g = jnp.concatenate(own[1], axis=1).astype(F32)
        u_g = jnp.concatenate(own[2], axis=0).astype(F32)
    else:
        x_t, att_t = left_a[0], left_a[1]
        locals_ = (
            dot_nn(x_t, g[0]),
            dot_nn(x_t, g[1]),
            dot_nn(x_t, g[2]),
            dot_nn(att_t, g[3]),
            jnp.concatenate([dot_nn(hid_t, igl[n]) for n in range(blocks)], axis=1),
            dot_nn(act_t, low),
        )
        owned = [lax.psum_scatter(w, "fsdp", scatter_dimension=0, tiled=True) for w in locals_]
        q_g, k_g, v_g, o_g, i_g, u_g = (lax.psum(w.astype(BF16), "dp").astype(F32) for w in owned)

    qb, vb, ob, g1, s1, ub, g2, s2, ibg = small_grads
    return (
        out.reshape(docs, seq, width),
        in_grad.reshape(docs, seq, width),
        q_g,
        qb,
        k_g,
        v_g,
        vb,
        o_g,
        ob,
        g1,
        s1,
        i_g,
        ibg,
        u_g,
        ub,
        g2,
        s2,
    )


def solution(mesh):
    rows, row = P("fsdp", None), P("fsdp")
    docs = P(("dp", "fsdp"), None, None)
    in_specs = (docs, P(("dp", "fsdp")), docs, rows, row, rows, rows, row, rows, row, row, row, rows, row, rows, row, row, row)
    out_specs = (docs, docs, rows, row, rows, rows, row, rows, row, row, row, rows, row, rows, row, row, row)
    sizes = (mesh.shape["dp"], mesh.shape["fsdp"])
    return jax.shard_map(
        functools.partial(on_device, sizes), mesh=mesh, in_specs=in_specs, out_specs=out_specs, check_vma=False
    )
```

```python
import functools
import math

import jax
import jax.numpy as jnp
from jax import lax
from jax.experimental import pallas as pl
from jax.experimental.pallas import tpu as pltpu
from jax.sharding import PartitionSpec as P

F32 = jnp.float32
BF16 = jnp.bfloat16
HD = 64
MASKED = -1e30
SCALE = HD ** -0.5
EPSILON = 1e-12
ROOT_HALF = math.sqrt(0.5)
INV_ROOT_TWO_PI = 1.0 / math.sqrt(2.0 * math.pi)

VM = pl.BlockSpec(memory_space=pltpu.VMEM)
SM = pl.BlockSpec(memory_space=pltpu.SMEM)
HB = pl.BlockSpec(memory_space=pl.ANY)


def shape(*dims, dtype=BF16):
    return jax.ShapeDtypeStruct(dims, dtype)


def local(*dims, dtype=BF16):
    return pltpu.VMEM(dims, dtype)


def stay(*values):
    return tuple(pltpu.with_memory_space_constraint(v, pltpu.VMEM) for v in values)


def far_off(*values):
    return tuple(pltpu.with_memory_space_constraint(v, pltpu.HBM) for v in values)


def limit(mebibytes):
    return pltpu.CompilerParams(vmem_limit_bytes=mebibytes << 20)


def dot_nn(a, b):
    return lax.dot_general(a, b, (((1,), (0,)), ((), ())), preferred_element_type=F32)


def dot_nt(a, b):
    return lax.dot_general(a, b, (((1,), (1,)), ((), ())), preferred_element_type=F32)


def flip(value):
    return value.astype(F32).T.astype(BF16)


def column_sum(value):
    return jnp.sum(value.astype(F32), axis=0, keepdims=True)


def row_mean(value):
    return jnp.mean(value, axis=-1, keepdims=True)


def aligned(start, size):
    return pl.ds(pl.multiple_of(start, size), size)


class Pieces:
    def __init__(self, held, arrays, own, sibling, far, far_sibling, stacked, packs=()):
        self.held, self.arrays, self.own, self.sibling, self.packs = held, arrays, own, sibling, packs
        self.far, self.far_sibling, self.stacked = far, far_sibling, stacked

    def count(self):
        return len(self.own)

    def place(self, target, block, z_at, c_at, offset, rows):
        if self.stacked:
            return target.at[block, aligned_rows((2 * z_at + c_at) * 96 + offset, rows), :]
        return target.at[aligned_rows((2 * z_at + c_at) * 384 + block * 96 + offset, rows), :]

    def copies(self, held, me_ref, target, sems, base):
        z, c = me_ref[1], me_ref[2]
        done = []
        for block, (position, row, lane) in enumerate(self.own):
            where = self.place(target, block, z, c, 0, 96)
            source = held[position].at[pl.ds(row, 96), pl.ds(lane, 768)]
            done.append(pltpu.make_async_copy(source, where, sems.at[base + block]))
        return done

    def fill(self, refs, me_ref, target):
        i, z, c = me_ref[0], me_ref[1], me_ref[2]
        for block, (position, row, lane) in enumerate(self.sibling):
            self.place(target, block, z, 1 - c, 0, 96)[...] = refs[position][row : row + 96, lane : lane + 768]
        for c_at, far in ((c, self.far), (1 - c, self.far_sibling)):
            for away, parts in enumerate(far):
                for position, row, rows, offset in parts:
                    for j in range(1, 4):
                        where = self.place(target, i ^ away, z ^ j, c_at, offset, rows)
                        where[...] = refs[position][j - 1, row : row + rows, :]

    def vectors(self, refs, me_ref, target):
        z, c = me_ref[1], me_ref[2]
        for c_at, spot, far in ((c, self.packs[0], self.far), (1 - c, self.packs[1], self.far_sibling)):
            target[2 * z + c_at] = refs[spot][96:104, :].astype(F32)
            for j in range(1, 4):
                target[2 * (z ^ j) + c_at] = refs[far[0][0][0]][j - 1, 96:104, :].astype(F32)


def aligned_rows(start, rows):
    return pl.ds(pl.multiple_of(start, 16), rows)


class Whole:
    def __init__(self, held, arrays, spots, stacked):
        self.held, self.arrays, self.spots, self.stacked = held, arrays, spots, stacked

    def count(self):
        return len(self.spots)

    def copies(self, held, me_ref, target, sems, base):
        done = []
        for block, (position, row, lane) in enumerate(self.spots):
            where = target.at[block] if self.stacked else target.at[pl.ds(block * 768, 768), :]
            source = held[position].at[pl.ds(row, 768), pl.ds(lane, 768)]
            done.append(pltpu.make_async_copy(source, where, sems.at[base + block]))
        return done

    def fill(self, refs, me_ref, target):
        pass

    def vectors(self, refs, me_ref, target):
        target[...] = refs[0][...].astype(F32)


def start_all(copies):
    for copy in copies:
        copy.start()


def wait_all(copies):
    for copy in copies:
        copy.wait()


def pair_masks(dims, axis):
    spot = lax.broadcasted_iota(jnp.int32, dims, axis)
    return spot < HD, spot >= HD


def keep(mask, value):
    return jnp.where(mask, value, jnp.zeros_like(value))


def attend_forward_body(group, part, me_ref, len_ref, x_ref, *refs):
    held, refs = refs[: len(group.held)], refs[len(group.held) :]
    sources = refs[: len(group.arrays)]
    q_ref, k_ref, v_ref, att_ref, left_ref, lse_ref, w_ref, vec_ref, ib_ref, packed, sems = refs[len(group.arrays) :]
    seq, width = x_ref.shape
    tile = min(256, seq)
    loads = group.copies(held, me_ref, w_ref, sems, 0)
    start_all(loads)
    group.fill(sources, me_ref, w_ref)
    group.vectors(sources, me_ref, packed)
    for f in range(packed.shape[0]):
        pack = packed[f]
        vec_ref[:, f * part : (f + 1) * part] = pack[:, :part]
        row, lane = divmod(f * 4 * part, width)
        ib_ref[row : row + 1, lane : lane + 4 * part] = pack[:1, 128 : 128 + 4 * part]
    for p in range(width // 128):
        left_ref[0, p * 128 : (p + 1) * 128, :] = flip(x_ref[:, p * 128 : (p + 1) * 128])
    wait_all(loads)

    def project(r, carry):
        rows = aligned(r * tile, tile)
        x = x_ref[rows, :]
        q_ref[rows, :] = (dot_nn(x, w_ref[0]) + vec_ref[0:1, :]).astype(BF16)
        k_ref[rows, :] = dot_nn(x, w_ref[1]).astype(BF16)
        v_ref[rows, :] = (dot_nn(x, w_ref[2]) + vec_ref[1:2, :]).astype(BF16)
        return carry

    lax.fori_loop(0, seq // tile, project, 0)
    length = len_ref[0]

    def pair(p, carry):
        lanes = aligned(p * 128, 128)
        k_pair = k_ref[:, lanes]
        q_t = (q_ref[:, lanes].astype(F32) * SCALE).T.astype(BF16)
        v_t = flip(v_ref[:, lanes])
        masks = pair_masks((128, seq), 0)
        allowed = lax.broadcasted_iota(jnp.int32, (seq, seq), 0) < length
        for e in range(2):
            s = dot_nn(k_pair, keep(masks[e], q_t))
            s = jnp.where(allowed, s, MASKED)
            top = jnp.max(s, axis=0, keepdims=True)
            p_t = jnp.exp(s - top)
            total = jnp.sum(p_t, axis=0, keepdims=True)
            o_t = dot_nn(v_t[e * HD : (e + 1) * HD, :], p_t.astype(BF16)) / total
            left_ref[1, aligned(p * 128 + e * HD, HD), :] = o_t.astype(BF16)
            lse_ref[pl.ds(p * 2 + e, 1), :] = top + jnp.log(total)
        att_ref[:, lanes] = flip(left_ref[1, aligned(p * 128, 128), :])
        return carry

    lax.fori_loop(0, width // 128, pair, 0)


def attend_forward(group, shards, blocks, me, length, x):
    seq, width = x.shape
    heads = width // HD
    return pl.pallas_call(
        functools.partial(attend_forward_body, group, width // shards),
        out_shape=(local(seq, width),) * 4
        + (local(2, width, seq), local(-(-heads // 8) * 8, seq, dtype=F32), local(4, width, width))
        + (local(8, width, dtype=F32), local(blocks, width, dtype=F32)),
        in_specs=[SM, SM, VM] + [HB] * len(group.held) + [VM] * len(group.arrays),
        out_specs=[VM] * 9,
        scratch_shapes=[pltpu.VMEM((shards, 8, width), F32), pltpu.SemaphoreType.DMA((group.count(),))],
        compiler_params=limit(10),
        cost_estimate=pl.CostEstimate(flops=12_000_000_000, bytes_accessed=20_000_000, transcendentals=3_200_000),
        name="attend_forward",
    )(me, length, x, *far_off(*group.held), *stay(*group.arrays))


def attend_backward_body(first, last, len_ref, q_ref, k_ref, v_ref, do_ref, lse_ref, branch_ref, *refs):
    g_ref, sum_ref = refs[-2:]
    seq, width = q_ref.shape
    length = len_ref[0]

    def pair(p, carry):
        lanes = aligned(p * 128, 128)
        q_pair = (q_ref[:, lanes].astype(F32) * SCALE).astype(BF16)
        k_pair = k_ref[:, lanes]
        v_pair = v_ref[:, lanes]
        do_pair = do_ref[:, lanes]
        q_t = flip(q_pair)
        k_t = (k_pair.astype(F32) * SCALE).T.astype(BF16)
        do_t = flip(do_pair)
        sub_masks = pair_masks((128, seq), 0)
        lane_masks = pair_masks((seq, 128), 1)
        allowed = lax.broadcasted_iota(jnp.int32, (seq, seq), 0) < length
        dk = jnp.zeros((seq, 128), F32)
        dv = jnp.zeros((seq, 128), F32)
        dq_t = []
        for e in range(2):
            s = dot_nn(k_pair, keep(sub_masks[e], q_t))
            s = jnp.where(allowed, s, MASKED)
            p_t = jnp.exp(s - lse_ref[pl.ds(p * 2 + e, 1), :])
            dp = dot_nn(v_pair, keep(sub_masks[e], do_t))
            dv = dv + dot_nn(p_t.astype(BF16), keep(lane_masks[e], do_pair))
            t = p_t * dp
            row = jnp.sum(t, axis=0, keepdims=True)
            ds = (t - p_t * row).astype(BF16)
            dk = dk + dot_nn(ds, keep(lane_masks[e], q_pair))
            dq_t.append(dot_nn(k_t[e * HD : (e + 1) * HD, :], ds))
        dq = jnp.concatenate(dq_t, axis=0).T.astype(BF16)
        dv = dv.astype(BF16)
        g_ref[0, :, lanes] = dq
        g_ref[1, :, lanes] = dk.astype(BF16)
        g_ref[2, :, lanes] = dv
        g_ref[3, :, lanes] = branch_ref[:, lanes]
        sum_ref[0:1, lanes] = column_sum(dq)
        sum_ref[1:2, lanes] = column_sum(dv)
        return carry

    lax.fori_loop(first, last, pair, 0)


def attend_backward(first, last, length, q, k, v, do, lse, branch, before=()):
    seq, width = q.shape
    return pl.pallas_call(
        functools.partial(attend_backward_body, first, last),
        out_shape=(local(4, seq, width), local(8, width, dtype=F32)),
        in_specs=[SM] + [VM] * 6 + [HB] * len(before),
        out_specs=[VM] * 2,
        input_output_aliases={7 + n: n for n in range(len(before))},
        compiler_params=limit(10),
        cost_estimate=pl.CostEstimate(flops=16_000_000_000, bytes_accessed=9_000_000, transcendentals=3_200_000),
        name="attend_backward",
    )(length, *stay(q, k, v, do, lse, branch, *before))


def gelu_parts(inner):
    cumulative = 0.5 * (1.0 + lax.erf(inner * ROOT_HALF))
    density = jnp.exp(-0.5 * inner * inner) * INV_ROOT_TWO_PI
    return inner * cumulative, cumulative + inner * density


def fill_body(groups, me_ref, *refs):
    sources = []
    for n, group in enumerate(groups):
        sources.append((refs[: len(group.held)], refs[len(group.held) : len(group.held) + len(group.arrays)]))
        refs = refs[len(group.held) + len(group.arrays) :]
    wi, wu, sems = refs
    loads, base = [], 0
    for group, (held, _), target in zip(groups, sources, (wi, wu), strict=True):
        loads += group.copies(held, me_ref, target, sems, base)
        base += group.count()
    start_all(loads)
    for group, (_, near), target in zip(groups, sources, (wi, wu), strict=True):
        group.fill(near, me_ref, target)
    wait_all(loads)


def fill(groups, me, width, blocks):
    operands, specs = [], []
    for g in groups:
        operands += [*far_off(*g.held), *stay(*g.arrays)]
        specs += [HB] * len(g.held) + [VM] * len(g.arrays)
    return pl.pallas_call(
        functools.partial(fill_body, groups),
        out_shape=(local(blocks, width, width), local(blocks * width, width)),
        in_specs=[SM] + specs,
        out_specs=[VM] * 2,
        scratch_shapes=[pltpu.SemaphoreType.DMA((sum(g.count() for g in groups),))],
        compiler_params=limit(2),
        cost_estimate=pl.CostEstimate(flops=0, bytes_accessed=9_000_000, transcendentals=0),
        name="fill",
    )(me, *operands)


def middle_forward_body(
    len_ref,
    x_ref,
    att_ref,
    cot_ref,
    vec_ref,
    ib_ref,
    wa,
    wi,
    wu,
    out_ref,
    ssg_ref,
    low_ref,
    actT_ref,
    slope_ref,
    norm_ref,
    rstd_ref,
    hidT_ref,
    sum_ref,
):
    seq, width = x_ref.shape
    blocks = wi.shape[0]
    tile = min(256, seq)
    length = len_ref[0]
    sum_ref[...] = jnp.zeros_like(sum_ref)

    def rows_step(r, carry):
        rows = aligned(r * tile, tile)
        first = x_ref[rows, :].astype(F32) + dot_nn(att_ref[rows, :], wa[3]) + vec_ref[2:3, :]
        center = first - row_mean(first)
        rstd = lax.rsqrt(row_mean(center * center) + EPSILON)
        normed = center * rstd
        norm_ref[rows, :] = normed
        rstd_ref[rows, :] = rstd
        hidden = normed * vec_ref[3:4, :] + vec_ref[4:5, :]
        low = hidden.astype(BF16)
        hidT_ref[:, rows] = low.astype(F32).T.astype(BF16)

        def block(f, second):
            inner = dot_nn(low, wi[f]) + ib_ref[pl.ds(f, 1), :]
            active, slope = gelu_parts(inner)
            active = active.astype(BF16)
            spot = aligned(f * width, width)
            slope_ref[rows, spot] = slope.astype(BF16)
            actT_ref[spot, rows] = flip(active)
            return second + dot_nn(active, wu[spot, :])

        second = lax.fori_loop(0, blocks, block, hidden + vec_ref[5:6, :])
        center = second - row_mean(second)
        rstd = lax.rsqrt(row_mean(center * center) + EPSILON)
        normed = center * rstd
        spot = r * tile + lax.broadcasted_iota(jnp.int32, (tile, width), 0)
        valid = spot < length
        result = normed * vec_ref[6:7, :] + vec_ref[7:8, :]
        out_ref[rows, :] = jnp.where(valid, result, 0.0).astype(BF16)
        grad = jnp.where(valid, cot_ref[rows, :].astype(F32), 0.0)
        sum_ref[7:8, :] += column_sum(grad)
        sum_ref[6:7, :] += column_sum(grad * normed)
        grad = grad * vec_ref[6:7, :]
        grad = rstd * (grad - row_mean(grad) - normed * row_mean(grad * normed))
        ssg_ref[rows, :] = grad
        low = grad.astype(BF16)
        low_ref[rows, :] = low
        sum_ref[5:6, :] += column_sum(low)
        return carry

    lax.fori_loop(0, seq // tile, rows_step, 0)


def middle_forward(length, x, att, cot, vec, ib, wa, wi, wu):
    seq, width = x.shape
    blocks = ib.shape[0]
    return pl.pallas_call(
        middle_forward_body,
        out_shape=(
            shape(seq, width),
            local(seq, width, dtype=F32),
            local(seq, width),
            local(blocks * width, seq),
            local(seq, blocks * width),
            local(seq, width, dtype=F32),
            local(seq, 1, dtype=F32),
            local(width, seq),
            local(8, width, dtype=F32),
        ),
        in_specs=[SM] + [VM] * 8,
        out_specs=[VM] * 9,
        compiler_params=limit(12),
        cost_estimate=pl.CostEstimate(flops=12_000_000_000, bytes_accessed=30_000_000, transcendentals=3_200_000),
        name="middle_forward",
    )(length, x, *stay(att), cot, *stay(vec, ib, wa, wi, wu))


def middle_backward_body(
    low_ref, ssg_ref, slope_ref, norm_ref, rstd_ref, vec_ref, wa, wi, wu, igl_ref, fsg_ref, branch_ref, att_ref, ib_ref, sum_ref
):
    seq, width = low_ref.shape
    blocks = wi.shape[0]
    tile = min(256, seq)
    sum_ref[...] = jnp.zeros_like(sum_ref)
    ib_ref[...] = jnp.zeros_like(ib_ref)

    def rows_step(r, carry):
        rows = aligned(r * tile, tile)
        low = low_ref[rows, :]

        def block(f, grad):
            spot = aligned(f * width, width)
            inner = (dot_nt(low, wu[spot, :]) * slope_ref[rows, spot].astype(F32)).astype(BF16)
            igl_ref[f, rows, :] = inner
            ib_ref[pl.ds(f, 1), :] += column_sum(inner)
            return grad + dot_nt(inner, wi[f])

        grad = lax.fori_loop(0, blocks, block, ssg_ref[rows, :])
        normed = norm_ref[rows, :]
        sum_ref[4:5, :] += column_sum(grad)
        sum_ref[3:4, :] += column_sum(grad * normed)
        grad = grad * vec_ref[3:4, :]
        grad = rstd_ref[rows, :] * (grad - row_mean(grad) - normed * row_mean(grad * normed))
        fsg_ref[rows, :] = grad
        branch = grad.astype(BF16)
        branch_ref[rows, :] = branch
        sum_ref[2:3, :] += column_sum(branch)
        att_ref[rows, :] = dot_nt(branch, wa[3]).astype(BF16)
        return carry

    lax.fori_loop(0, seq // tile, rows_step, 0)


def middle_backward(low, ssg, slope, norm, rstd, vec, wa, wi, wu):
    seq, width = low.shape
    blocks = wi.shape[0]
    return pl.pallas_call(
        middle_backward_body,
        out_shape=(
            local(blocks, seq, width),
            local(seq, width, dtype=F32),
            local(seq, width),
            local(seq, width),
            local(blocks, width, dtype=F32),
            local(8, width, dtype=F32),
        ),
        in_specs=[VM] * 9,
        out_specs=[VM] * 6,
        compiler_params=limit(10),
        cost_estimate=pl.CostEstimate(flops=9_000_000_000, bytes_accessed=25_000_000, transcendentals=0),
        name="middle_backward",
    )(*stay(low, ssg, slope, norm, rstd, vec, wa, wi, wu))


def input_grad_body(g_ref, fsg_ref, w_ref, out_ref):
    seq, width = fsg_ref.shape
    tile = min(256, seq)

    def rows_step(r, carry):
        rows = aligned(r * tile, tile)
        total = fsg_ref[rows, :]
        for n in range(3):
            total = total + dot_nt(g_ref[n, rows, :], w_ref[n])
        out_ref[rows, :] = total
        return carry

    lax.fori_loop(0, seq // tile, rows_step, 0)


def input_grad(g, fsg, wa):
    seq, width = fsg.shape
    return pl.pallas_call(
        input_grad_body,
        out_shape=shape(seq, width, dtype=F32),
        in_specs=[VM] * 3,
        out_specs=VM,
        compiler_params=limit(8),
        cost_estimate=pl.CostEstimate(flops=4_000_000_000, bytes_accessed=10_000_000, transcendentals=0),
        name="input_grad",
    )(*stay(g, fsg, wa))


Z_ORDER = (0, 2, 1, 3)


def weight_grad_body(kind, order, z_order, me_ref, left_ref, g_ref, *refs):
    sums, refs = (refs[:4], refs[4:]) if kind == "attend" else ((), refs)
    outs, left = refs[:2], refs[2]
    i, z, c = me_ref[0], me_ref[1], me_ref[2]
    part = 96
    if kind == "attend":
        extra = refs[3]
        one, two, three, ib = (r[...] for r in sums)
        row = lax.broadcasted_iota(jnp.int32, one.shape, 0)
        every = jnp.where(row < 2, three, jnp.where(row < 5, two, one))
        for f in range(8):
            extra[f] = jnp.zeros_like(extra[f])
            extra[f, :, :part] = every[:, f * part : (f + 1) * part]
            extra[f, 0:1, 128 : 128 + 4 * part] = ib[f // 2 : f // 2 + 1, f % 2 * 4 * part : (f % 2 + 1) * 4 * part]

    for c_at, out_ref in zip((1 - c, c), outs, strict=True):

        def block_step(spot, carry):
            block = i ^ pick(order, spot)
            for n, j in enumerate(z_order):
                f_at = 2 * (z ^ j) + c_at
                if kind == "outer":
                    rows = left_ref[aligned_rows(f_at * 384 + block * 96, 96), :]
                elif kind == "inner":
                    rows = left_ref[aligned_rows(f_at * 96, 96), :]
                else:
                    rows = left_ref[block // 3, aligned_rows(f_at * 96, 96), :]
                left[n * 96 : (n + 1) * 96, :] = rows
            right = g_ref[...] if kind == "outer" else g_ref[block]
            out_ref[spot, :, :96, :] = dot_nn(left[...], right).reshape(4, 96, 768).astype(BF16)
            if kind == "attend":
                for n, j in enumerate(z_order):
                    out_ref[spot, n, 96:104, :] = extra[2 * (z ^ j) + c_at].astype(BF16)
            return carry

        lax.fori_loop(0, 4, block_step, 0)


def weight_grad(kind, order, z_order, me, left, g, sums=()):
    rows = 104 if kind == "attend" else 96
    return pl.pallas_call(
        functools.partial(weight_grad_body, kind, order, z_order),
        out_shape=(local(4, 4, rows, 768),) * 2,
        in_specs=[SM] + [VM] * (2 + len(sums)),
        out_specs=[VM] * 2,
        scratch_shapes=[pltpu.VMEM((384, left.shape[-1]), BF16)] + [pltpu.VMEM((8, 8, 768), F32)] * (kind == "attend"),
        compiler_params=limit(6),
        cost_estimate=pl.CostEstimate(flops=4_000_000_000, bytes_accessed=6_000_000, transcendentals=0),
        name=f"weight_grad_{kind}",
    )(me, *stay(left, g, *sums))


def prepare_body(me_ref, *refs):
    vectors, weights = refs[:9], refs[9:15]
    first_ref, second_ref, pack_ref, *rows, sems = refs[15:]
    i = me_ref[0]
    part = vectors[0].shape[0]
    copies = [
        pltpu.make_async_copy(
            weights[4].at[:, pl.ds(pl.multiple_of(i * 768, 768), 768)], second_ref.at[pl.ds(0, 96), :], sems.at[0]
        ),
        pltpu.make_async_copy(weights[5].at[aligned_rows(i * 96, 96), :], second_ref.at[pl.ds(96, 96), :], sems.at[1]),
    ]
    for n in range(9):
        copies.append(pltpu.make_async_copy(vectors[n], rows[n], sems.at[3 + n]))
    for n in range(4):

        @pl.when(i == n)
        def _():
            pltpu.make_async_copy(weights[n], first_ref.at[pl.ds(0, 96), :], sems.at[2]).start()

    start_all(copies)
    pack_ref[...] = jnp.zeros_like(pack_ref)
    wait_all(copies[2:])
    for n in range(8):
        pack_ref[n : n + 1, :part] = rows[n][...].astype(F32).reshape(1, part)
    pack_ref[0:1, 128 : 128 + 4 * part] = rows[8][...].astype(F32).reshape(1, 4 * part)
    first_ref[96:104, :] = pack_ref[...].astype(BF16)
    pltpu.make_async_copy(weights[0], first_ref.at[pl.ds(0, 96), :], sems.at[2]).wait()
    wait_all(copies[:2])


def prepare(me, vectors, weights):
    return pl.pallas_call(
        prepare_body,
        out_shape=(local(104, 768), local(192, 768)),
        in_specs=[SM] + [HB] * 15,
        out_specs=[VM] * 2,
        scratch_shapes=[pltpu.VMEM((8, 768), F32)]
        + [pltpu.VMEM(v.shape, BF16) for v in vectors]
        + [pltpu.SemaphoreType.DMA((12,))],
        compiler_params=limit(2),
        cost_estimate=pl.CostEstimate(flops=0, bytes_accessed=1_000_000, transcendentals=0),
        name="prepare",
    )(me, *far_off(*vectors, *weights))


def after(value, *others):
    def body(*refs):
        pass

    return pl.pallas_call(
        body,
        out_shape=jax.ShapeDtypeStruct(value.shape, value.dtype),
        in_specs=[HB] * (1 + len(others)),
        out_specs=HB,
        input_output_aliases={0: 0},
        compiler_params=limit(1),
        cost_estimate=pl.CostEstimate(flops=0, bytes_accessed=0, transcendentals=0),
        name="after",
    )(value, *others)


def swap(value, axis, size, mask):
    return lax.ppermute(value, axis, [(n, n ^ mask) for n in range(size)])


def gather_z(piece, fsdp):
    return [swap(piece, "fsdp", fsdp, 2 * j) for j in (1, 2, 3)]


def gather_plane(mine, dp):
    over_x = swap(mine, "dp", dp, 1)
    over_y = swap(mine, "dp", dp, 2)
    return over_x, over_y


def total(*terms):
    result = terms[0].astype(F32)
    for term in terms[1:]:
        result = result + term.astype(F32)
    return result.astype(BF16)


def scatter_z(value, fsdp):
    got = swap(value[2:], "fsdp", fsdp, 2)
    onward = swap(total(value[1], got[1]), "fsdp", fsdp, 4)
    return total(value[0], got[0], onward)


def direct_z(value, fsdp):
    return total(value[0], *[swap(value[j], "fsdp", fsdp, 2 * j) for j in (1, 2, 3)])


def spread(value, dp):
    return (value,) + tuple(swap(value, "dp", dp, m) for m in (1, 2, 3))


def pick(pieces, index):
    return jnp.where(index == 0, pieces[0], jnp.where(index == 1, pieces[1], jnp.where(index == 2, pieces[2], pieces[3])))


def in_order(pieces, i):
    return [pick(pieces, n ^ i) for n in range(4)]


def on_device(
    sizes,
    tokens,
    lengths,
    cotangent,
    query_weight,
    query_bias,
    key_weight,
    value_weight,
    value_bias,
    output_weight,
    output_bias,
    first_gain,
    first_shift,
    inner_weight,
    inner_bias,
    outer_weight,
    outer_bias,
    second_gain,
    second_shift,
):
    dp, fsdp = sizes
    docs, seq, width = tokens.shape
    blocks = inner_weight.shape[1] // width
    direct = dp == 4 and fsdp == 8 and docs == 1 and query_weight.shape == (96, 768) and blocks == 4
    i = lax.axis_index("dp")
    f = lax.axis_index("fsdp")
    me = jnp.stack([i, f // 2, f % 2, jnp.zeros_like(i)]).astype(jnp.int32)

    small = (query_bias, value_bias, output_bias, first_gain, first_shift, outer_bias, second_gain, second_shift, inner_bias)
    part = query_bias.shape[0]

    if direct:
        mine = (query_weight, key_weight, value_weight, output_weight)
        piece_a, piece_m = prepare(me, small, mine + (inner_weight, outer_weight))
        z_a = gather_z(piece_a, fsdp)
        theirs = tuple(swap(w, "fsdp", fsdp, 1) for w in mine + (piece_a,))
        mine_a = jnp.stack(z_a)
        plane_a = gather_plane(mine_a, dp)
        z_m = gather_z(after(piece_m, mine_a), fsdp)
        parts_a = (plane_a[0][:, :48], plane_a[1][:, 48:96])
        rest_a = (swap(parts_a[0], "dp", dp, 2), swap(parts_a[1], "dp", dp, 1))
        near_a = (mine_a,) + plane_a + rest_a
        far_a = tuple(swap(w, "fsdp", fsdp, 1) for w in near_a)
        z_m[0] = after(z_m[0], *parts_a)
        mine_m = jnp.stack(z_m)
        plane_m = gather_plane(mine_m, dp)
        inner_other = swap(inner_weight, "fsdp", fsdp, 1)
        outer_other = swap(outer_weight, "fsdp", fsdp, 1)

        def far_at(base, row, halves):
            return [[(base + n, row, 96, 0)] for n in range(3)] + [[(base + n, 0, rows, off) for n, rows, off in halves]]

        split = ((3, 48, 0), (4, 48, 48))
        group_a = Pieces(
            mine,
            theirs + near_a + far_a + (piece_a,),
            [(n, 0, 0) for n in range(4)],
            [(n, 0, 0) for n in range(4)],
            far_at(5, 0, split),
            far_at(10, 0, split),
            True,
            (15, 4),
        )
        x = tokens.reshape(seq, width)
        q, k, v, att, left_a, lse, wa, vec, ib = attend_forward(group_a, fsdp, blocks, me, lengths, after(x, mine_m))
        plane_m = (after(plane_m[0], att), after(plane_m[1], att))
        rest_m = (swap(plane_m[0][:, :96], "dp", dp, 2), swap(plane_m[1][:, 96:], "dp", dp, 1))
        near_m = (mine_m,) + plane_m + rest_m
        far_m = tuple(swap(w, "fsdp", fsdp, 1) for w in near_m)
        group_i = Pieces(
            (inner_weight,),
            (inner_other,) + near_m[:4] + far_m[:4],
            [(0, 0, 768 * n) for n in range(4)],
            [(0, 0, 768 * n) for n in range(4)],
            far_at(1, 0, ((3, 96, 0),)),
            far_at(5, 0, ((3, 96, 0),)),
            True,
        )
        group_u = Pieces(
            (outer_weight,),
            (outer_other,) + near_m[:3] + near_m[4:] + far_m[:3] + far_m[4:],
            [(0, 96 * n, 0) for n in range(4)],
            [(0, 96 * n, 0) for n in range(4)],
            far_at(1, 96, ((3, 96, 0),)),
            far_at(5, 96, ((3, 96, 0),)),
            False,
        )
    else:
        whole = tuple(
            lax.all_gather(w, "fsdp", axis=0, tiled=True)
            for w in (query_weight, key_weight, value_weight, output_weight, inner_weight, outer_weight)
        )
        packs = jnp.pad(jnp.stack(small[:8]), ((0, 0), (0, width - part)))
        packs = packs + jnp.pad(inner_bias[None], ((0, 7), (128, width - 128 - 4 * part)))
        packs = lax.all_gather(packs, "fsdp", axis=0, tiled=False)
        group_a = Whole(whole[:4], (packs,), [(n, 0, 0) for n in range(4)], True)
        group_i = Whole(whole[4:5], (), [(0, 0, width * n) for n in range(blocks)], True)
        group_u = Whole(whole[5:6], (), [(0, width * n, 0) for n in range(blocks)], False)
        x = tokens.reshape(seq, width)
        q, k, v, att, left_a, lse, wa, vec, ib = attend_forward(group_a, fsdp, blocks, me, lengths, x)

    cot = cotangent.reshape(seq, width)
    wi, wu = fill((group_i, group_u), me, width, blocks)
    out, ssg, low, act_t, slope, norm, rstd, hid_t, sum_one = middle_forward(lengths, x, att, cot, vec, ib, wa, wi, wu)
    pairs = width // 128
    attend = functools.partial(attend_backward, length=lengths, q=q, k=k, v=v, lse=lse)
    if direct:
        sent_u, kept_u = weight_grad("outer", (1, 3, 0, 2), Z_ORDER, me, act_t, low)
        got_u = swap(sent_u, "fsdp", fsdp, 1)
        low = after(low, sent_u)
    igl, fsg, branch, att_g, ib_sum, sum_two = middle_backward(low, ssg, slope, norm, rstd, vec, wa, wi, wu)
    if direct:
        first_u = total(kept_u[:2], got_u[:2])
        over_u = swap(first_u, "dp", dp, 1)
        sent_i, kept_i = weight_grad("inner", (2, 3, 0, 1), Z_ORDER, me, hid_t, after(igl, first_u))
        got_i = swap(sent_i, "fsdp", fsdp, 1)
        half = attend(0, pairs // 2, do=after(att_g, sent_i), branch=branch)
        first_i = total(kept_i[:2], got_i[:2])
        over_i = swap(first_i, "dp", dp, 2)
        g, sum_three = attend(pairs // 2, pairs, do=after(att_g, first_i), branch=branch, before=half)
    else:
        g, sum_three = attend(0, pairs, do=att_g, branch=branch)
        in_grad = input_grad(g, fsg, wa)

    if direct:
        sent_a, kept_a = weight_grad(
            "attend", (0, 1, 2, 3), (0, 1, 2, 3), me, left_a, g, (sum_one, sum_two, sum_three, ib_sum)
        )
        got_a = swap(sent_a, "fsdp", fsdp, 1)
        in_grad = input_grad(g, after(fsg, sent_a), wa)
        ready_a = [total(kept_a[m], got_a[m]) for m in (1, 2, 3)]
        over_a = [swap(ready_a[m - 1], "dp", dp, m) for m in (1, 2, 3)]
        over_u = after(over_u, *ready_a)
        onward_u = swap(total(kept_u[3], got_u[3], over_u[1]), "dp", dp, 2)
        onward_i = swap(total(kept_i[3], got_i[3], over_i[1]), "dp", dp, 1)
        plane_u = total(kept_u[2], got_u[2], over_u[0], onward_u)
        plane_i = total(kept_i[2], got_i[2], over_i[0], onward_i)
        plane_m = jnp.concatenate([plane_u, plane_i], axis=1)
        over_a[0] = after(over_a[0], plane_m)
        own_a = direct_z(total(kept_a[0], got_a[0], *over_a), fsdp)
        both = spread(scatter_z(plane_m, fsdp), dp)
        small_own = own_a[96:104].astype(F32)
        small_grads = [small_own[n, :part] for n in range(8)] + [small_own[0, 128 : 128 + blocks * part]]
        q_g, k_g, v_g, o_g = (w.astype(F32) for w in in_order(spread(own_a[:96], dp), i))
        u_g = jnp.concatenate(in_order([w[:96] for w in both], i), axis=0).astype(F32)
        i_g = jnp.concatenate(in_order([w[96:] for w in both], i), axis=1).astype(F32)
    else:
        vec_sum = jnp.concatenate([sum_three[:2], sum_two[2:5], sum_one[5:8]])
        vec_sum = vec_sum.reshape(8, fsdp, part).transpose(1, 0, 2).reshape(fsdp, 8 * part)
        ib_part = ib_sum.reshape(fsdp, blocks * part)
        small_sum = lax.psum(jnp.concatenate([vec_sum, ib_part], axis=1), ("dp", "fsdp"))
        small_own = lax.dynamic_index_in_dim(small_sum, f, 0, keepdims=False)
        small_grads = [small_own[n * part : (n + 1) * part] for n in range(8)] + [small_own[8 * part :]]
        x_t, att_t = left_a[0], left_a[1]
        locals_ = (
            dot_nn(x_t, g[0]),
            dot_nn(x_t, g[1]),
            dot_nn(x_t, g[2]),
            dot_nn(att_t, g[3]),
            jnp.concatenate([dot_nn(hid_t, igl[n]) for n in range(blocks)], axis=1),
            dot_nn(act_t, low),
        )
        owned = [lax.psum_scatter(w, "fsdp", scatter_dimension=0, tiled=True) for w in locals_]
        q_g, k_g, v_g, o_g, i_g, u_g = (lax.psum(w.astype(BF16), "dp").astype(F32) for w in owned)

    qb, vb, ob, g1, s1, ub, g2, s2, ibg = small_grads
    return (
        out.reshape(docs, seq, width),
        in_grad.reshape(docs, seq, width),
        q_g,
        qb,
        k_g,
        v_g,
        vb,
        o_g,
        ob,
        g1,
        s1,
        i_g,
        ibg,
        u_g,
        ub,
        g2,
        s2,
    )


def solution(mesh):
    rows, row = P("fsdp", None), P("fsdp")
    docs = P(("dp", "fsdp"), None, None)
    in_specs = (docs, P(("dp", "fsdp")), docs, rows, row, rows, rows, row, rows, row, row, row, rows, row, rows, row, row, row)
    out_specs = (docs, docs, rows, row, rows, rows, row, rows, row, row, row, rows, row, rows, row, row, row)
    sizes = (mesh.shape["dp"], mesh.shape["fsdp"])
    return jax.shard_map(
        functools.partial(on_device, sizes), mesh=mesh, in_specs=in_specs, out_specs=out_specs, check_vma=False
    )
```

```python
import functools
import math

import jax
import jax.numpy as jnp
from jax import lax
from jax.experimental import pallas as pl
from jax.experimental.pallas import tpu as pltpu
from jax.sharding import PartitionSpec as P

F32 = jnp.float32
BF16 = jnp.bfloat16
HD = 64
MASKED = -1e30
SCALE = HD ** -0.5
EPSILON = 1e-12
ROOT_HALF = math.sqrt(0.5)
INV_ROOT_TWO_PI = 1.0 / math.sqrt(2.0 * math.pi)

VM = pl.BlockSpec(memory_space=pltpu.VMEM)
SM = pl.BlockSpec(memory_space=pltpu.SMEM)
HB = pl.BlockSpec(memory_space=pl.ANY)
FREE = pl.CostEstimate(flops=0, bytes_accessed=0, transcendentals=0)


def shape(*dims, dtype=BF16):
    return jax.ShapeDtypeStruct(dims, dtype)


def local(*dims, dtype=BF16):
    return pltpu.VMEM(dims, dtype)


def stay(*values):
    return tuple(pltpu.with_memory_space_constraint(v, pltpu.VMEM) for v in values)


def far_off(*values):
    return tuple(pltpu.with_memory_space_constraint(v, pltpu.HBM) for v in values)


def limit(mebibytes):
    return pltpu.CompilerParams(vmem_limit_bytes=mebibytes << 20)


def dot_nn(a, b):
    return lax.dot_general(a, b, (((1,), (0,)), ((), ())), preferred_element_type=F32)


def dot_nt(a, b):
    return lax.dot_general(a, b, (((1,), (1,)), ((), ())), preferred_element_type=F32)


def flip(value):
    return value.astype(F32).T.astype(BF16)


def column_sum(value):
    return jnp.sum(value.astype(F32), axis=0, keepdims=True)


def row_mean(value):
    return jnp.mean(value, axis=-1, keepdims=True)


def aligned(start, size):
    return pl.ds(pl.multiple_of(start, size), size)


class Pieces:
    def __init__(self, held, arrays, own, sibling, far, far_sibling, stacked, packs=()):
        self.held, self.arrays, self.own, self.sibling, self.packs = held, arrays, own, sibling, packs
        self.far, self.far_sibling, self.stacked = far, far_sibling, stacked

    def count(self):
        return len(self.own)

    def place(self, target, block, z_at, c_at, offset, rows):
        if self.stacked:
            return target.at[block, aligned_rows((2 * z_at + c_at) * 96 + offset, rows), :]
        return target.at[aligned_rows((2 * z_at + c_at) * 384 + block * 96 + offset, rows), :]

    def copies(self, held, me_ref, target, sems, base):
        z, c = me_ref[1], me_ref[2]
        done = []
        for block, (position, row, lane) in enumerate(self.own):
            where = self.place(target, block, z, c, 0, 96)
            source = held[position].at[pl.ds(row, 96), pl.ds(lane, 768)]
            done.append(pltpu.make_async_copy(source, where, sems.at[base + block]))
        return done

    def fill(self, refs, me_ref, target):
        i, z, c = me_ref[0], me_ref[1], me_ref[2]
        for block, (position, tile) in enumerate(self.sibling):
            self.place(target, block, z, 1 - c, 0, 96)[...] = refs[position][tile]
        for c_at, far in ((c, self.far), (1 - c, self.far_sibling)):
            for away, parts in enumerate(far):
                for position, tile, row, rows, offset in parts:
                    for j in range(1, 4):
                        where = self.place(target, i ^ away, z ^ j, c_at, offset, rows)
                        where[...] = refs[position][tile + j - 1, row : row + rows, :]

    def vectors(self, refs, me_ref, target):
        z, c = me_ref[1], me_ref[2]
        own, mine, other = (refs[n] for n in self.packs)
        for j in range(4):
            target[2 * (z ^ j) + c] = (mine[j - 1, 96:104, :] if j else own[96:104, :]).astype(F32)
            target[2 * (z ^ j) + 1 - c] = other[13, 8 * j : 8 * j + 8, :].astype(F32)


def bundle_body(group_count, held, me_ref, *refs):
    sources, near = refs[: len(held)], refs[len(held) : -2]
    out_ref, sems = refs[-2:]
    own = [(n, row, lane) for n, spots in enumerate(held) for row, lane in spots]
    loads = []
    for tile, (n, row, lane) in enumerate(own):
        source = sources[n].at[pl.ds(row, 96), pl.ds(lane, 768)]
        loads.append(pltpu.make_async_copy(source, out_ref.at[tile], sems.at[tile]))
    start_all(loads)
    tile = len(own)
    for away in range(3):
        for group in range(group_count):
            for j in range(3):
                out_ref[tile] = near[away][j, group * 96 : (group + 1) * 96, :]
                tile += 1
    if group_count == 1:
        out_ref[tile, 0:8, :] = near[3][96:104, :]
        for j in range(3):
            out_ref[tile, 8 * j + 8 : 8 * j + 16, :] = near[0][j, 96:104, :]
        out_ref[tile, 32:, :] = jnp.zeros((64, 768), BF16)
    wait_all(loads)


def bundle(group_count, sources, held, near):
    own = sum(len(spots) for spots in held)
    tiles = own + 9 * group_count + (group_count == 1)
    return pl.pallas_call(
        functools.partial(bundle_body, group_count, held),
        out_shape=local(tiles, 96, 768),
        in_specs=[SM] + [HB] * len(sources) + [VM] * len(near),
        out_specs=VM,
        scratch_shapes=[pltpu.SemaphoreType.DMA((own,))],
        compiler_params=limit(2),
        cost_estimate=FREE,
        name="bundle",
    )(jnp.zeros((1,), jnp.int32), *far_off(*sources), *stay(*near))


def aligned_rows(start, rows):
    return pl.ds(pl.multiple_of(start, 16), rows)


class Whole:
    def __init__(self, held, arrays, spots, stacked):
        self.held, self.arrays, self.spots, self.stacked = held, arrays, spots, stacked

    def count(self):
        return len(self.spots)

    def copies(self, held, me_ref, target, sems, base):
        done = []
        for block, (position, row, lane) in enumerate(self.spots):
            where = target.at[block] if self.stacked else target.at[pl.ds(block * 768, 768), :]
            source = held[position].at[pl.ds(row, 768), pl.ds(lane, 768)]
            done.append(pltpu.make_async_copy(source, where, sems.at[base + block]))
        return done

    def fill(self, refs, me_ref, target):
        pass

    def vectors(self, refs, me_ref, target):
        target[...] = refs[0][...].astype(F32)


def start_all(copies):
    for copy in copies:
        copy.start()


def wait_all(copies):
    for copy in copies:
        copy.wait()


def pair_masks(dims, axis):
    spot = lax.broadcasted_iota(jnp.int32, dims, axis)
    return spot < HD, spot >= HD


def keep(mask, value):
    return jnp.where(mask, value, jnp.zeros_like(value))


def attend_forward_body(group, part, me_ref, len_ref, x_ref, *refs):
    held, refs = refs[: len(group.held)], refs[len(group.held) :]
    sources = refs[: len(group.arrays)]
    q_ref, k_ref, v_ref, att_ref, left_ref, lse_ref, w_ref, vec_ref, ib_ref, packed, sems = refs[len(group.arrays) :]
    seq, width = x_ref.shape
    tile = min(256, seq)
    loads = group.copies(held, me_ref, w_ref, sems, 0)
    start_all(loads)
    group.fill(sources, me_ref, w_ref)
    group.vectors(sources, me_ref, packed)
    for f in range(packed.shape[0]):
        pack = packed[f]
        vec_ref[:, f * part : (f + 1) * part] = pack[:, :part]
        row, lane = divmod(f * 4 * part, width)
        ib_ref[row : row + 1, lane : lane + 4 * part] = pack[:1, 128 : 128 + 4 * part]
    for p in range(width // 128):
        left_ref[0, p * 128 : (p + 1) * 128, :] = flip(x_ref[:, p * 128 : (p + 1) * 128])
    wait_all(loads)

    def project(r, carry):
        rows = aligned(r * tile, tile)
        x = x_ref[rows, :]
        q_ref[rows, :] = (dot_nn(x, w_ref[0]) + vec_ref[0:1, :]).astype(BF16)
        k_ref[rows, :] = dot_nn(x, w_ref[1]).astype(BF16)
        v_ref[rows, :] = (dot_nn(x, w_ref[2]) + vec_ref[1:2, :]).astype(BF16)
        return carry

    lax.fori_loop(0, seq // tile, project, 0)
    length = len_ref[0]

    def pair(p, carry):
        lanes = aligned(p * 128, 128)
        k_pair = k_ref[:, lanes]
        q_t = (q_ref[:, lanes].astype(F32) * SCALE).T.astype(BF16)
        v_t = flip(v_ref[:, lanes])
        masks = pair_masks((128, seq), 0)
        allowed = lax.broadcasted_iota(jnp.int32, (seq, seq), 0) < length
        for e in range(2):
            s = dot_nn(k_pair, keep(masks[e], q_t))
            s = jnp.where(allowed, s, MASKED)
            top = jnp.max(s, axis=0, keepdims=True)
            p_t = jnp.exp(s - top)
            total = jnp.sum(p_t, axis=0, keepdims=True)
            o_t = dot_nn(v_t[e * HD : (e + 1) * HD, :], p_t.astype(BF16)) / total
            left_ref[1, aligned(p * 128 + e * HD, HD), :] = o_t.astype(BF16)
            lse_ref[pl.ds(p * 2 + e, 1), :] = top + jnp.log(total)
        att_ref[:, lanes] = flip(left_ref[1, aligned(p * 128, 128), :])
        return carry

    lax.fori_loop(0, width // 128, pair, 0)


def attend_forward(group, shards, blocks, me, length, x):
    seq, width = x.shape
    heads = width // HD
    return pl.pallas_call(
        functools.partial(attend_forward_body, group, width // shards),
        out_shape=(local(seq, width),) * 4
        + (local(2, width, seq), local(-(-heads // 8) * 8, seq, dtype=F32), local(4, width, width))
        + (local(8, width, dtype=F32), local(blocks, width, dtype=F32)),
        in_specs=[SM, SM, VM] + [HB] * len(group.held) + [VM] * len(group.arrays),
        out_specs=[VM] * 9,
        scratch_shapes=[pltpu.VMEM((shards, 8, width), F32), pltpu.SemaphoreType.DMA((group.count(),))],
        compiler_params=limit(10),
        cost_estimate=FREE,
        name="attend_forward",
    )(me, length, x, *far_off(*group.held), *stay(*group.arrays))


def attend_backward_body(first, last, len_ref, q_ref, k_ref, v_ref, do_ref, lse_ref, branch_ref, *refs):
    g_ref, sum_ref = refs[-2:]
    seq, width = q_ref.shape
    length = len_ref[0]

    def pair(p, carry):
        lanes = aligned(p * 128, 128)
        q_pair = (q_ref[:, lanes].astype(F32) * SCALE).astype(BF16)
        k_pair = k_ref[:, lanes]
        v_pair = v_ref[:, lanes]
        do_pair = do_ref[:, lanes]
        q_t = flip(q_pair)
        k_t = (k_pair.astype(F32) * SCALE).T.astype(BF16)
        do_t = flip(do_pair)
        sub_masks = pair_masks((128, seq), 0)
        lane_masks = pair_masks((seq, 128), 1)
        allowed = lax.broadcasted_iota(jnp.int32, (seq, seq), 0) < length
        dk = jnp.zeros((seq, 128), F32)
        dv = jnp.zeros((seq, 128), F32)
        dq_t = []
        for e in range(2):
            s = dot_nn(k_pair, keep(sub_masks[e], q_t))
            s = jnp.where(allowed, s, MASKED)
            p_t = jnp.exp(s - lse_ref[pl.ds(p * 2 + e, 1), :])
            dp = dot_nn(v_pair, keep(sub_masks[e], do_t))
            dv = dv + dot_nn(p_t.astype(BF16), keep(lane_masks[e], do_pair))
            t = p_t * dp
            row = jnp.sum(t, axis=0, keepdims=True)
            ds = (t - p_t * row).astype(BF16)
            dk = dk + dot_nn(ds, keep(lane_masks[e], q_pair))
            dq_t.append(dot_nn(k_t[e * HD : (e + 1) * HD, :], ds))
        dq = jnp.concatenate(dq_t, axis=0).T.astype(BF16)
        dv = dv.astype(BF16)
        g_ref[0, :, lanes] = dq
        g_ref[1, :, lanes] = dk.astype(BF16)
        g_ref[2, :, lanes] = dv
        g_ref[3, :, lanes] = branch_ref[:, lanes]
        sum_ref[0:1, lanes] = column_sum(dq)
        sum_ref[1:2, lanes] = column_sum(dv)
        return carry

    lax.fori_loop(first, last, pair, 0)


def attend_backward(first, last, length, q, k, v, do, lse, branch, before=()):
    seq, width = q.shape
    return pl.pallas_call(
        functools.partial(attend_backward_body, first, last),
        out_shape=(local(4, seq, width), local(8, width, dtype=F32)),
        in_specs=[SM] + [VM] * 6 + [HB] * len(before),
        out_specs=[VM] * 2,
        input_output_aliases={7 + n: n for n in range(len(before))},
        compiler_params=limit(10),
        cost_estimate=FREE,
        name="attend_backward",
    )(length, *stay(q, k, v, do, lse, branch, *before))


def gelu_parts(inner):
    cumulative = 0.5 * (1.0 + lax.erf(inner * ROOT_HALF))
    density = jnp.exp(-0.5 * inner * inner) * INV_ROOT_TWO_PI
    return inner * cumulative, cumulative + inner * density


def fill_body(group, me_ref, *refs):
    held, near = refs[: len(group.held)], refs[len(group.held) : len(group.held) + len(group.arrays)]
    target, sems = refs[-2:]
    loads = group.copies(held, me_ref, target, sems, 0)
    start_all(loads)
    group.fill(near, me_ref, target)
    wait_all(loads)


def fill(group, me, *dims):
    return pl.pallas_call(
        functools.partial(fill_body, group),
        out_shape=local(*dims),
        in_specs=[SM] + [HB] * len(group.held) + [VM] * len(group.arrays),
        out_specs=VM,
        scratch_shapes=[pltpu.SemaphoreType.DMA((group.count(),))],
        compiler_params=limit(2),
        cost_estimate=FREE,
        name="fill",
    )(me, *far_off(*group.held), *stay(*group.arrays))


def middle_forward_body(
    len_ref,
    x_ref,
    att_ref,
    cot_ref,
    vec_ref,
    ib_ref,
    wa,
    wi,
    wu,
    out_ref,
    ssg_ref,
    low_ref,
    actT_ref,
    slope_ref,
    norm_ref,
    rstd_ref,
    hidT_ref,
    sum_ref,
):
    seq, width = x_ref.shape
    blocks = wi.shape[0]
    tile = min(256, seq)
    length = len_ref[0]
    sum_ref[...] = jnp.zeros_like(sum_ref)

    def rows_step(r, carry):
        rows = aligned(r * tile, tile)
        first = x_ref[rows, :].astype(F32) + dot_nn(att_ref[rows, :], wa[3]) + vec_ref[2:3, :]
        center = first - row_mean(first)
        rstd = lax.rsqrt(row_mean(center * center) + EPSILON)
        normed = center * rstd
        norm_ref[rows, :] = normed
        rstd_ref[rows, :] = rstd
        hidden = normed * vec_ref[3:4, :] + vec_ref[4:5, :]
        low = hidden.astype(BF16)
        hidT_ref[:, rows] = low.astype(F32).T.astype(BF16)

        def block(f, second):
            inner = dot_nn(low, wi[f]) + ib_ref[pl.ds(f, 1), :]
            active, slope = gelu_parts(inner)
            active = active.astype(BF16)
            spot = aligned(f * width, width)
            slope_ref[rows, spot] = slope.astype(BF16)
            actT_ref[spot, rows] = flip(active)
            return second + dot_nn(active, wu[spot, :])

        second = lax.fori_loop(0, blocks, block, hidden + vec_ref[5:6, :])
        center = second - row_mean(second)
        rstd = lax.rsqrt(row_mean(center * center) + EPSILON)
        normed = center * rstd
        spot = r * tile + lax.broadcasted_iota(jnp.int32, (tile, width), 0)
        valid = spot < length
        result = normed * vec_ref[6:7, :] + vec_ref[7:8, :]
        out_ref[rows, :] = jnp.where(valid, result, 0.0).astype(BF16)
        grad = jnp.where(valid, cot_ref[rows, :].astype(F32), 0.0)
        sum_ref[7:8, :] += column_sum(grad)
        sum_ref[6:7, :] += column_sum(grad * normed)
        grad = grad * vec_ref[6:7, :]
        grad = rstd * (grad - row_mean(grad) - normed * row_mean(grad * normed))
        ssg_ref[rows, :] = grad
        low = grad.astype(BF16)
        low_ref[rows, :] = low
        sum_ref[5:6, :] += column_sum(low)
        return carry

    lax.fori_loop(0, seq // tile, rows_step, 0)


def middle_forward(length, x, att, cot, vec, ib, wa, wi, wu):
    seq, width = x.shape
    blocks = ib.shape[0]
    return pl.pallas_call(
        middle_forward_body,
        out_shape=(
            shape(seq, width),
            local(seq, width, dtype=F32),
            local(seq, width),
            local(blocks * width, seq),
            local(seq, blocks * width),
            local(seq, width, dtype=F32),
            local(seq, 1, dtype=F32),
            local(width, seq),
            local(8, width, dtype=F32),
        ),
        in_specs=[SM] + [VM] * 8,
        out_specs=[VM] * 9,
        compiler_params=limit(12),
        cost_estimate=FREE,
        name="middle_forward",
    )(length, x, *stay(att), cot, *stay(vec, ib, wa, wi, wu))


def middle_backward_body(
    low_ref, ssg_ref, slope_ref, norm_ref, rstd_ref, vec_ref, wa, wi, wu, igl_ref, fsg_ref, branch_ref, att_ref, ib_ref, sum_ref
):
    seq, width = low_ref.shape
    blocks = wi.shape[0]
    tile = min(256, seq)
    sum_ref[...] = jnp.zeros_like(sum_ref)
    ib_ref[...] = jnp.zeros_like(ib_ref)

    def rows_step(r, carry):
        rows = aligned(r * tile, tile)
        low = low_ref[rows, :]

        def block(f, grad):
            spot = aligned(f * width, width)
            inner = (dot_nt(low, wu[spot, :]) * slope_ref[rows, spot].astype(F32)).astype(BF16)
            igl_ref[f, rows, :] = inner
            ib_ref[pl.ds(f, 1), :] += column_sum(inner)
            return grad + dot_nt(inner, wi[f])

        grad = lax.fori_loop(0, blocks, block, ssg_ref[rows, :])
        normed = norm_ref[rows, :]
        sum_ref[4:5, :] += column_sum(grad)
        sum_ref[3:4, :] += column_sum(grad * normed)
        grad = grad * vec_ref[3:4, :]
        grad = rstd_ref[rows, :] * (grad - row_mean(grad) - normed * row_mean(grad * normed))
        fsg_ref[rows, :] = grad
        branch = grad.astype(BF16)
        branch_ref[rows, :] = branch
        sum_ref[2:3, :] += column_sum(branch)
        att_ref[rows, :] = dot_nt(branch, wa[3]).astype(BF16)
        return carry

    lax.fori_loop(0, seq // tile, rows_step, 0)


def middle_backward(low, ssg, slope, norm, rstd, vec, wa, wi, wu):
    seq, width = low.shape
    blocks = wi.shape[0]
    return pl.pallas_call(
        middle_backward_body,
        out_shape=(
            local(blocks, seq, width),
            local(seq, width, dtype=F32),
            local(seq, width),
            local(seq, width),
            local(blocks, width, dtype=F32),
            local(8, width, dtype=F32),
        ),
        in_specs=[VM] * 9,
        out_specs=[VM] * 6,
        compiler_params=limit(10),
        cost_estimate=FREE,
        name="middle_backward",
    )(*stay(low, ssg, slope, norm, rstd, vec, wa, wi, wu))


def input_grad_body(g_ref, fsg_ref, w_ref, out_ref):
    seq, width = fsg_ref.shape
    tile = min(256, seq)

    def rows_step(r, carry):
        rows = aligned(r * tile, tile)
        total = fsg_ref[rows, :]
        for n in range(3):
            total = total + dot_nt(g_ref[n, rows, :], w_ref[n])
        out_ref[rows, :] = total
        return carry

    lax.fori_loop(0, seq // tile, rows_step, 0)


def input_grad(g, fsg, wa):
    seq, width = fsg.shape
    return pl.pallas_call(
        input_grad_body,
        out_shape=shape(seq, width, dtype=F32),
        in_specs=[VM] * 3,
        out_specs=VM,
        compiler_params=limit(8),
        cost_estimate=FREE,
        name="input_grad",
    )(*stay(g, fsg, wa))


Z_ORDER = (0, 2, 1, 3)


def weight_grad_body(kind, order, z_order, me_ref, left_ref, g_ref, *refs):
    sums, refs = (refs[:4], refs[4:]) if kind == "attend" else ((), refs)
    sent = len(order) if kind == "attend" else 1
    outs, left = refs[: sent + 1], refs[sent + 1]
    i, z, c = me_ref[0], me_ref[1], me_ref[2]
    part = 96
    if kind == "attend":
        extra = refs[sent + 2]
        one, two, three, ib = (r[...] for r in sums)
        row = lax.broadcasted_iota(jnp.int32, one.shape, 0)
        every = jnp.where(row < 2, three, jnp.where(row < 5, two, one))
        for f in range(8):
            extra[f] = jnp.zeros_like(extra[f])
            extra[f, :, :part] = every[:, f * part : (f + 1) * part]
            extra[f, 0:1, 128 : 128 + 4 * part] = ib[f // 2 : f // 2 + 1, f % 2 * 4 * part : (f % 2 + 1) * 4 * part]

    def one_block(spot, away, c_at, out_ref):
        block = i ^ away
        for n, j in enumerate(z_order):
            f_at = 2 * (z ^ j) + c_at
            if kind == "outer":
                rows = left_ref[aligned_rows(f_at * 384 + block * 96, 96), :]
            elif kind == "inner":
                rows = left_ref[aligned_rows(f_at * 96, 96), :]
            else:
                rows = left_ref[block // 3, aligned_rows(f_at * 96, 96), :]
            left[n * 96 : (n + 1) * 96, :] = rows
        right = g_ref[...] if kind == "outer" else g_ref[block]
        grads = dot_nn(left[...], right).reshape(4, 96, 768).astype(BF16)
        if kind == "outer":
            out_ref[:, spot] = grads
        else:
            out_ref[spot, :, :96, :] = grads
        if kind == "attend":
            for n, j in enumerate(z_order):
                out_ref[spot, n, 96:104, :] = extra[2 * (z ^ j) + c_at].astype(BF16)

    def block_step(c_at, out_ref, spot, carry):
        one_block(spot, pick(order, spot), c_at, out_ref)
        return carry

    if kind == "attend":
        for spot, away in enumerate(order):
            one_block(0, away, 1 - c, outs[spot])
    else:
        lax.fori_loop(0, 4, functools.partial(block_step, 1 - c, outs[0]), 0)
    lax.fori_loop(0, 4, functools.partial(block_step, c, outs[-1]), 0)


def weight_grad(kind, order, z_order, me, left, g, sums=()):
    rows = 104 if kind == "attend" else 96
    sent = (local(1, 4, rows, 768),) * 4 if kind == "attend" else (local(4, 4, rows, 768),)
    return pl.pallas_call(
        functools.partial(weight_grad_body, kind, order, z_order),
        out_shape=sent + (local(4, 4, rows, 768),),
        in_specs=[SM] + [VM] * (2 + len(sums)),
        out_specs=[VM] * (len(sent) + 1),
        scratch_shapes=[pltpu.VMEM((384, left.shape[-1]), BF16)] + [pltpu.VMEM((8, 8, 768), F32)] * (kind == "attend"),
        compiler_params=limit(6),
        cost_estimate=FREE,
        name=f"weight_grad_{kind}",
    )(me, *stay(left, g, *sums))


def prepare_body(me_ref, *refs):
    vectors, weights = refs[:9], refs[9:15]
    first_ref, second_ref, pack_ref, *rows, sems = refs[15:]
    i = me_ref[0]
    part = vectors[0].shape[0]
    copies = [
        pltpu.make_async_copy(
            weights[4].at[:, pl.ds(pl.multiple_of(i * 768, 768), 768)], second_ref.at[pl.ds(0, 96), :], sems.at[0]
        ),
        pltpu.make_async_copy(weights[5].at[aligned_rows(i * 96, 96), :], second_ref.at[pl.ds(96, 96), :], sems.at[1]),
    ]
    for n in range(9):
        copies.append(pltpu.make_async_copy(vectors[n], rows[n], sems.at[3 + n]))
    for n in range(4):

        @pl.when(i == n)
        def _():
            pltpu.make_async_copy(weights[n], first_ref.at[pl.ds(0, 96), :], sems.at[2]).start()

    start_all(copies)
    pack_ref[...] = jnp.zeros_like(pack_ref)
    wait_all(copies[2:])
    for n in range(8):
        pack_ref[n : n + 1, :part] = rows[n][...].astype(F32).reshape(1, part)
    pack_ref[0:1, 128 : 128 + 4 * part] = rows[8][...].astype(F32).reshape(1, 4 * part)
    first_ref[96:104, :] = pack_ref[...].astype(BF16)
    pltpu.make_async_copy(weights[0], first_ref.at[pl.ds(0, 96), :], sems.at[2]).wait()
    wait_all(copies[:2])


def prepare(me, vectors, weights):
    return pl.pallas_call(
        prepare_body,
        out_shape=(local(104, 768), local(192, 768)),
        in_specs=[SM] + [HB] * 15,
        out_specs=[VM] * 2,
        scratch_shapes=[pltpu.VMEM((8, 768), F32)]
        + [pltpu.VMEM(v.shape, BF16) for v in vectors]
        + [pltpu.SemaphoreType.DMA((12,))],
        compiler_params=limit(2),
        cost_estimate=FREE,
        name="prepare",
    )(me, *far_off(*vectors, *weights))


def after(value, *others):
    def body(*refs):
        pass

    return pl.pallas_call(
        body,
        out_shape=jax.ShapeDtypeStruct(value.shape, value.dtype),
        in_specs=[HB] * (1 + len(others)),
        out_specs=HB,
        input_output_aliases={0: 0},
        compiler_params=limit(1),
        cost_estimate=FREE,
        name="after",
    )(value, *others)


def swap(value, axis, size, mask):
    return lax.ppermute(value, axis, [(n, n ^ mask) for n in range(size)])


def gather_z(piece, fsdp):
    return [swap(piece, "fsdp", fsdp, 2 * j) for j in (1, 2, 3)]


def combine(*outs):
    arrays = []
    for _, _, *lists in outs:
        for terms in lists:
            arrays += [a for n, (a, _) in enumerate(terms) if not any(a is b for b in arrays)]

    def find(array):
        return next(n for n, b in enumerate(arrays) if b is array)

    def body(*refs):
        for out_ref, (lead, rows, *lists) in zip(refs[len(arrays) :], outs, strict=True):
            size = rows // len(lists)

            def tile(index):
                for n, terms in enumerate(lists):
                    if len(terms) == 1:
                        value = refs[find(terms[0][0])][terms[0][1](*index)]
                    else:
                        value = sum(refs[find(array)][at(*index)].astype(F32) for array, at in terms).astype(BF16)
                    out_ref[(*index, slice(n * size, (n + 1) * size), slice(None))] = value

            def step(front, last, carry):
                tile((*front, last))
                return carry

            if not lead:
                tile(())
            elif len(lead) == 1:
                lax.fori_loop(0, lead[0], functools.partial(step, ()), 0)
            else:
                for front in range(lead[0]):
                    lax.fori_loop(0, lead[1], functools.partial(step, (front,)), 0)

    return pl.pallas_call(
        body,
        out_shape=tuple(local(*lead, rows, 768) for lead, rows, *_ in outs),
        in_specs=[VM] * len(arrays),
        out_specs=[VM] * len(outs),
        compiler_params=limit(2),
        cost_estimate=FREE,
        name="combine",
    )(*stay(*arrays))


def stack_three(parts):
    rows = parts[0].shape[0]

    def body(*refs):
        for n in range(3):
            refs[3][n] = refs[n][...]

    return pl.pallas_call(
        body,
        out_shape=local(3, rows, 768),
        in_specs=[VM] * 3,
        out_specs=VM,
        compiler_params=limit(2),
        cost_estimate=FREE,
        name="stack_three",
    )(*stay(*parts))


def halves(over_x, over_y):
    return (
        combine(((3,), 48, [(over_x, lambda n: (n, slice(0, 48)))]))[0],
        combine(((3,), 48, [(over_y, lambda n: (n, slice(48, 96)))]))[0],
    )


def first_sum(kept, got):
    at = lambda a, b: (2 + a, b)
    return combine(((2, 4), 96, [(kept, at), (got, at)]))[0]


def second_sum(kept, got, over):
    here, there = (lambda b: (1, b)), (lambda b: (1, b))
    return combine(((4,), 96, [(kept, here), (got, here), (over, there)]))[0]


def finish(terms, beside):
    def body(*refs):
        terms, (beside_ref, own_ref, small_ref) = refs[:-3], refs[-3:]
        value = sum(r[...].astype(F32) for r in terms)
        own_ref[:96, :] = value[:96].astype(BF16)
        own_ref[96:, :] = beside_ref[...]
        small_ref[...] = value[96:]

    return pl.pallas_call(
        body,
        out_shape=(local(192, 768), local(8, 768, dtype=F32)),
        in_specs=[VM] * (len(terms) + 1),
        out_specs=[VM] * 2,
        compiler_params=limit(2),
        cost_estimate=FREE,
        name="finish",
    )(*stay(*terms, beside))


def spread(value, dp):
    return (value,) + tuple(swap(value, "dp", dp, m) for m in (1, 2, 3))


def pick(pieces, index):
    return jnp.where(index == 0, pieces[0], jnp.where(index == 1, pieces[1], jnp.where(index == 2, pieces[2], pieces[3])))


def in_order(pieces, i):
    return [pick(pieces, n ^ i) for n in range(4)]


def on_device(
    sizes,
    tokens,
    lengths,
    cotangent,
    query_weight,
    query_bias,
    key_weight,
    value_weight,
    value_bias,
    output_weight,
    output_bias,
    first_gain,
    first_shift,
    inner_weight,
    inner_bias,
    outer_weight,
    outer_bias,
    second_gain,
    second_shift,
):
    dp, fsdp = sizes
    docs, seq, width = tokens.shape
    blocks = inner_weight.shape[1] // width
    direct = dp == 4 and fsdp == 8 and docs == 1 and query_weight.shape == (96, 768) and blocks == 4
    i = lax.axis_index("dp")
    f = lax.axis_index("fsdp")
    me = jnp.stack([i, f // 2, f % 2, jnp.zeros_like(i)]).astype(jnp.int32)

    small = (query_bias, value_bias, output_bias, first_gain, first_shift, outer_bias, second_gain, second_shift, inner_bias)
    part = query_bias.shape[0]

    if direct:
        mine = (query_weight, key_weight, value_weight, output_weight)
        piece_a, piece_m = prepare(me, small, mine + (inner_weight, outer_weight))
        z_a = gather_z(piece_a, fsdp)
        z_m = gather_z(piece_m, fsdp)
        mine_a = stack_three(z_a)
        plane_a = (swap(mine_a, "dp", dp, 1), swap(mine_a, "dp", dp, 2))
        parts_a = halves(*plane_a)
        rest_a = (swap(parts_a[0], "dp", dp, 2), swap(parts_a[1], "dp", dp, 1))
        z_m[0] = after(z_m[0], *rest_a)
        mine_m = stack_three(z_m)
        plane_m = (swap(mine_m, "dp", dp, 1), swap(mine_m, "dp", dp, 2))
        near_a = bundle(1, mine, ((((0, 0)),),) * 4, (after(mine_a, mine_m),) + plane_a + (piece_a,))
        far_a = (swap(near_a, "fsdp", fsdp, 1),) + tuple(swap(v, "fsdp", fsdp, 1) for v in rest_a)

        def far_at(base, row=0):
            return [[(base + n, 0, row, 96, 0)] for n in range(3)]

        group_a = Pieces(
            mine,
            (mine_a,) + plane_a + rest_a + far_a + (piece_a,),
            [(n, 0, 0) for n in range(4)],
            [(5, n) for n in range(4)],
            far_at(0) + [[(3, 0, 0, 48, 0), (4, 0, 0, 48, 48)]],
            [[(5, 4 + 3 * n, 0, 96, 0)] for n in range(3)] + [[(6, 0, 0, 48, 0), (7, 0, 0, 48, 48)]],
            True,
            (8, 0, 5),
        )
        x = tokens.reshape(seq, width)
        q, k, v, att, left_a, lse, wa, vec, ib = attend_forward(group_a, fsdp, blocks, me, lengths, after(x, mine_m))
        plane_m = (after(plane_m[0], att), after(plane_m[1], att))
        parts_m = (
            combine(((3,), 96, [(plane_m[0], lambda n: (n, slice(0, 96)))]))[0],
            combine(((3,), 96, [(plane_m[1], lambda n: (n, slice(96, 192)))]))[0],
        )
        rest_m = (swap(parts_m[0], "dp", dp, 2), swap(parts_m[1], "dp", dp, 1))
        spots = (tuple((0, 768 * n) for n in range(4)), tuple((96 * n, 0) for n in range(4)))
        near_m = bundle(2, (inner_weight, outer_weight), spots, (mine_m,) + plane_m)
        far_m = (swap(near_m, "fsdp", fsdp, 1),) + tuple(swap(v, "fsdp", fsdp, 1) for v in rest_m)
        group_i = Pieces(
            (inner_weight,),
            (mine_m,) + plane_m + (rest_m[0], far_m[0], far_m[1]),
            [(0, 0, 768 * n) for n in range(4)],
            [(4, n) for n in range(4)],
            far_at(0) + [[(3, 0, 0, 96, 0)]],
            [[(4, 8 + 6 * n, 0, 96, 0)] for n in range(3)] + [[(5, 0, 0, 96, 0)]],
            True,
        )
        group_u = Pieces(
            (outer_weight,),
            (mine_m,) + plane_m + (rest_m[1], far_m[0], far_m[2]),
            [(0, 96 * n, 0) for n in range(4)],
            [(4, 4 + n) for n in range(4)],
            far_at(0, 96) + [[(3, 0, 0, 96, 0)]],
            [[(4, 11 + 6 * n, 0, 96, 0)] for n in range(3)] + [[(5, 0, 0, 96, 0)]],
            False,
        )
    else:
        whole = tuple(
            lax.all_gather(w, "fsdp", axis=0, tiled=True)
            for w in (query_weight, key_weight, value_weight, output_weight, inner_weight, outer_weight)
        )
        packs = jnp.pad(jnp.stack(small[:8]), ((0, 0), (0, width - part)))
        packs = packs + jnp.pad(inner_bias[None], ((0, 7), (128, width - 128 - 4 * part)))
        packs = lax.all_gather(packs, "fsdp", axis=0, tiled=False)
        group_a = Whole(whole[:4], (packs,), [(n, 0, 0) for n in range(4)], True)
        group_i = Whole(whole[4:5], (), [(0, 0, width * n) for n in range(blocks)], True)
        group_u = Whole(whole[5:6], (), [(0, width * n, 0) for n in range(blocks)], False)
        x = tokens.reshape(seq, width)
        q, k, v, att, left_a, lse, wa, vec, ib = attend_forward(group_a, fsdp, blocks, me, lengths, x)

    cot = cotangent.reshape(seq, width)
    wi = fill(group_i, me, blocks, width, width)
    wu = fill(group_u, me, blocks * width, width)
    out, ssg, low, act_t, slope, norm, rstd, hid_t, sum_one = middle_forward(lengths, x, att, cot, vec, ib, wa, wi, wu)
    pairs = width // 128
    attend = functools.partial(attend_backward, length=lengths, q=q, k=k, v=v, lse=lse)
    if direct:
        sent_u, kept_u = weight_grad("outer", (0, 1, 2, 3), Z_ORDER, me, act_t, low)
        got_u = swap(sent_u, "fsdp", fsdp, 1)
        low = after(low, sent_u)
    igl, fsg, branch, att_g, ib_sum, sum_two = middle_backward(low, ssg, slope, norm, rstd, vec, wa, wi, wu)
    if direct:
        first_u = first_sum(kept_u, got_u)
        over_u = swap(first_u, "fsdp", fsdp, 2)
        sent_i, kept_i = weight_grad("inner", (0, 1, 2, 3), Z_ORDER, me, hid_t, after(igl, first_u))
        got_i = swap(sent_i, "fsdp", fsdp, 1)
        half = attend(0, pairs // 2, do=after(att_g, sent_i), branch=branch)
        got_i = after(got_i, half[0])
        upper, lower = slice(0, 48), slice(48, 96)
        (first_x,) = combine(((2, 4), 48, [(v, lambda a, b: (2 * a + 1, b, upper)) for v in (kept_i, got_i)]))
        (first_y,) = combine(((2, 4), 48, [(v, lambda a, b: (a + 2, b, lower)) for v in (kept_i, got_i)]))
        over_x, over_y = swap(first_x, "dp", dp, 1), swap(first_y, "dp", dp, 2)
        do = after(att_g, first_x, first_y)
        g, sum_three = attend(pairs // 2, pairs, do=do, branch=branch, before=half)
    else:
        g, sum_three = attend(0, pairs, do=att_g, branch=branch)
        in_grad = input_grad(g, fsg, wa)

    if direct:
        *sent_a, kept_a = weight_grad(
            "attend", (1, 2, 3, 0), (0, 1, 2, 3), me, left_a, g, (sum_one, sum_two, sum_three, ib_sum)
        )
        over_x = after(over_x, kept_a)
        (second_x,) = combine(
            ((4,), 48, [(v, lambda b: (2, b, upper)) for v in (kept_i, got_i)] + [(over_x, lambda b: (1, b))])
        )
        (second_y,) = combine(
            ((4,), 48, [(v, lambda b: (1, b, lower)) for v in (kept_i, got_i)] + [(over_y, lambda b: (1, b))])
        )
        onward_x, onward_y = swap(second_x, "dp", dp, 2), swap(second_y, "dp", dp, 1)
        over_u = after(over_u, second_x, second_y)
        second_u = second_sum(kept_u, got_u, over_u)
        onward_u = swap(second_u, "fsdp", fsdp, 4)
        sent_a[3] = after(sent_a[3], second_x)
        got_a = [swap(v, "fsdp", fsdp, 1) for v in sent_a]
        got_a[0] = after(got_a[0], second_u)
        ready_a = [combine(((4,), 104, [(kept_a, lambda b, n=n: (n, b)), (got_a[n], lambda b: (0, b))]))[0] for n in range(4)]
        over_a = [swap(ready_a[m - 1], "dp", dp, m) for m in (1, 2, 3)]
        in_grad = input_grad(g, after(fsg, *ready_a), wa)

        tile, front, here = (lambda b: (b,)), (lambda b: (0, b)), (lambda: ())

        def plane_at(first):
            def terms(rows, over, onward):
                held = [(v, lambda b: (0, first + b, rows)) for v in (kept_i, got_i)]
                return held + [(over, lambda b: (0, first + b)), (onward, lambda b: (first + b,))]

            return (2,), 96, terms(upper, over_x, onward_x), terms(lower, over_y, onward_y)

        onward_x = after(onward_x, in_grad)
        keep_i, send_i = combine(plane_at(0), plane_at(2))
        near_i = swap(send_i, "fsdp", fsdp, 2)

        onward_u = after(onward_u, keep_i)
        (line_u,) = combine(((4,), 96, [(kept_u, front), (got_u, front), (over_u, front), (onward_u, tile)]))
        beside_u = swap(line_u, "dp", dp, 1)

        near_i = after(near_i, line_u)
        (next_i,) = combine(((), 96, [(keep_i, lambda: (1,)), (near_i, lambda: (1,))]))
        last_i = swap(next_i, "fsdp", fsdp, 4)

        over_a[0] = after(over_a[0], next_i)
        whole_a = combine(
            *[((), 104, [(ready_a[3], lambda j=j: (j,))] + [(v, lambda j=j: (j,)) for v in over_a]) for j in range(4)]
        )
        far_a = [swap(whole_a[j], "fsdp", fsdp, 2 * j) for j in (1, 2, 3)]

        beside_u = after(beside_u, whole_a[0])
        (pair_u,) = combine(((4,), 96, [(line_u, tile), (beside_u, lambda b: (b ^ 1,))]))
        across_u = swap(pair_u, "dp", dp, 2)

        last_i = after(last_i, pair_u)
        (own_i,) = combine(((), 96, [(keep_i, lambda: (0,)), (near_i, lambda: (0,)), (last_i, here)]))

        far_a[0] = after(far_a[0], own_i)
        own, small_rows = finish((whole_a[0], *far_a), own_i)
        every = spread(own, dp)
        all_a = [v[:96] for v in every]
        all_i = [v[96:] for v in every]

        across_u = after(across_u, *every)
        (all_u,) = combine(((4,), 96, [(pair_u, tile), (across_u, lambda b: (b ^ 2,))]))
        small_own = small_rows
        small_grads = [small_own[n, :part] for n in range(8)] + [small_own[0, 128 : 128 + blocks * part]]
        q_g, k_g, v_g, o_g = (w.astype(F32) for w in in_order(all_a, i))
        i_g = jnp.concatenate(in_order(all_i, i), axis=1).astype(F32)
        u_g = jnp.concatenate(in_order([all_u[n] for n in range(4)], i), axis=0).astype(F32)
    else:
        vec_sum = jnp.concatenate([sum_three[:2], sum_two[2:5], sum_one[5:8]])
        vec_sum = vec_sum.reshape(8, fsdp, part).transpose(1, 0, 2).reshape(fsdp, 8 * part)
        ib_part = ib_sum.reshape(fsdp, blocks * part)
        small_sum = lax.psum(jnp.concatenate([vec_sum, ib_part], axis=1), ("dp", "fsdp"))
        small_own = lax.dynamic_index_in_dim(small_sum, f, 0, keepdims=False)
        small_grads = [small_own[n * part : (n + 1) * part] for n in range(8)] + [small_own[8 * part :]]
        x_t, att_t = left_a[0], left_a[1]
        locals_ = (
            dot_nn(x_t, g[0]),
            dot_nn(x_t, g[1]),
            dot_nn(x_t, g[2]),
            dot_nn(att_t, g[3]),
            jnp.concatenate([dot_nn(hid_t, igl[n]) for n in range(blocks)], axis=1),
            dot_nn(act_t, low),
        )
        owned = [lax.psum_scatter(w, "fsdp", scatter_dimension=0, tiled=True) for w in locals_]
        q_g, k_g, v_g, o_g, i_g, u_g = (lax.psum(w.astype(BF16), "dp").astype(F32) for w in owned)

    qb, vb, ob, g1, s1, ub, g2, s2, ibg = small_grads
    return (
        out.reshape(docs, seq, width),
        in_grad.reshape(docs, seq, width),
        q_g,
        qb,
        k_g,
        v_g,
        vb,
        o_g,
        ob,
        g1,
        s1,
        i_g,
        ibg,
        u_g,
        ub,
        g2,
        s2,
    )


def solution(mesh):
    rows, row = P("fsdp", None), P("fsdp")
    docs = P(("dp", "fsdp"), None, None)
    in_specs = (docs, P(("dp", "fsdp")), docs, rows, row, rows, rows, row, rows, row, row, row, rows, row, rows, row, row, row)
    out_specs = (docs, docs, rows, row, rows, rows, row, rows, row, row, row, rows, row, rows, row, row, row)
    sizes = (mesh.shape["dp"], mesh.shape["fsdp"])
    return jax.shard_map(
        functools.partial(on_device, sizes), mesh=mesh, in_specs=in_specs, out_specs=out_specs, check_vma=False
    )
```

```python
import functools
import math

import jax
import jax.numpy as jnp
from jax import lax
from jax.experimental import pallas as pl
from jax.experimental.pallas import tpu as pltpu
from jax.sharding import PartitionSpec as P

F32 = jnp.float32
BF16 = jnp.bfloat16
HD = 64
MASKED = -1e30
SCALE = HD ** -0.5
EPSILON = 1e-12
ROOT_HALF = math.sqrt(0.5)
INV_ROOT_TWO_PI = 1.0 / math.sqrt(2.0 * math.pi)

VM = pl.BlockSpec(memory_space=pltpu.VMEM)
SM = pl.BlockSpec(memory_space=pltpu.SMEM)
HB = pl.BlockSpec(memory_space=pl.ANY)
FREE = pl.CostEstimate(flops=0, bytes_accessed=0, transcendentals=0)

LONG = pl.CostEstimate(flops=60_000_000_000, bytes_accessed=0, transcendentals=0)


def shape(*dims, dtype=BF16):
    return jax.ShapeDtypeStruct(dims, dtype)


def local(*dims, dtype=BF16):
    return pltpu.VMEM(dims, dtype)


def stay(*values):
    return tuple(pltpu.with_memory_space_constraint(v, pltpu.VMEM) for v in values)


def far_off(*values):
    return tuple(pltpu.with_memory_space_constraint(v, pltpu.HBM) for v in values)


def limit(mebibytes):
    return pltpu.CompilerParams(vmem_limit_bytes=mebibytes << 20)


def dot_nn(a, b):
    return lax.dot_general(a, b, (((1,), (0,)), ((), ())), preferred_element_type=F32)


def dot_nt(a, b):
    return lax.dot_general(a, b, (((1,), (1,)), ((), ())), preferred_element_type=F32)


def flip(value):
    return value.astype(F32).T.astype(BF16)


def column_sum(value):
    return jnp.sum(value.astype(F32), axis=0, keepdims=True)


def row_mean(value):
    return jnp.mean(value, axis=-1, keepdims=True)


def aligned(start, size):
    return pl.ds(pl.multiple_of(start, size), size)


class Pieces:
    def __init__(self, held, arrays, own, sibling, far, far_sibling, stacked, packs=()):
        self.held, self.arrays, self.own, self.sibling, self.packs = held, arrays, own, sibling, packs
        self.far, self.far_sibling, self.stacked = far, far_sibling, stacked

    def count(self):
        return len(self.own)

    def place(self, target, block, z_at, c_at, offset, rows):
        if self.stacked:
            return target.at[block, aligned_rows((2 * z_at + c_at) * 96 + offset, rows), :]
        return target.at[aligned_rows((2 * z_at + c_at) * 384 + block * 96 + offset, rows), :]

    def copies(self, held, me_ref, target, sems, base):
        z, c = me_ref[1], me_ref[2]
        done = []
        for block, (position, row, lane) in enumerate(self.own):
            where = self.place(target, block, z, c, 0, 96)
            source = held[position].at[pl.ds(row, 96), pl.ds(lane, 768)]
            done.append(pltpu.make_async_copy(source, where, sems.at[base + block]))
        return done

    def fill(self, refs, me_ref, target, rest=(0, 1, 2, 3)):
        i, z, c = me_ref[0], me_ref[1], me_ref[2]
        for block, (position, tile) in enumerate(self.sibling if 0 in rest else ()):
            self.place(target, block, z, 1 - c, 0, 96)[...] = refs[position][tile]
        for c_at, far in ((c, self.far), (1 - c, self.far_sibling)):
            for away in rest:
                parts = far[away]
                for position, tile, row, rows, offset in parts:
                    for j in range(1, 4):
                        where = self.place(target, i ^ away, z ^ j, c_at, offset, rows)
                        where[...] = refs[position][tile + j - 1, row : row + rows, :]

    def vectors(self, refs, me_ref, target):
        z, c = me_ref[1], me_ref[2]
        own, mine, other = (refs[n] for n in self.packs)
        for j in range(4):
            target[2 * (z ^ j) + c] = (mine[j - 1, 96:104, :] if j else own[96:104, :]).astype(F32)
            target[2 * (z ^ j) + 1 - c] = other[13, 8 * j : 8 * j + 8, :].astype(F32)


def bundle_body(group_count, held, me_ref, *refs):
    sources, near = refs[: len(held)], refs[len(held) : -2]
    out_ref, sems = refs[-2:]
    own = [(n, row, lane) for n, spots in enumerate(held) for row, lane in spots]
    loads = []
    for tile, (n, row, lane) in enumerate(own):
        source = sources[n].at[pl.ds(row, 96), pl.ds(lane, 768)]
        loads.append(pltpu.make_async_copy(source, out_ref.at[tile], sems.at[tile]))
    start_all(loads)
    tile = len(own)
    for away in range(3):
        for group in range(group_count):
            for j in range(3):
                out_ref[tile] = near[away][j, group * 96 : (group + 1) * 96, :]
                tile += 1
    if group_count == 1:
        out_ref[tile, 0:8, :] = near[3][96:104, :]
        for j in range(3):
            out_ref[tile, 8 * j + 8 : 8 * j + 16, :] = near[0][j, 96:104, :]
        out_ref[tile, 32:, :] = jnp.zeros((64, 768), BF16)
    wait_all(loads)


def bundle(group_count, sources, held, near):
    own = sum(len(spots) for spots in held)
    tiles = own + 9 * group_count + (group_count == 1)
    return pl.pallas_call(
        functools.partial(bundle_body, group_count, held),
        out_shape=local(tiles, 96, 768),
        in_specs=[SM] + [HB] * len(sources) + [VM] * len(near),
        out_specs=VM,
        scratch_shapes=[pltpu.SemaphoreType.DMA((own,))],
        compiler_params=limit(2),
        cost_estimate=FREE,
        name="bundle",
    )(jnp.zeros((1,), jnp.int32), *far_off(*sources), *stay(*near))


def aligned_rows(start, rows):
    return pl.ds(pl.multiple_of(start, 16), rows)


class Whole:
    def __init__(self, held, arrays, spots, stacked):
        self.held, self.arrays, self.spots, self.stacked = held, arrays, spots, stacked

    def count(self):
        return len(self.spots)

    def copies(self, held, me_ref, target, sems, base):
        done = []
        for block, (position, row, lane) in enumerate(self.spots):
            where = target.at[block] if self.stacked else target.at[pl.ds(block * 768, 768), :]
            source = held[position].at[pl.ds(row, 768), pl.ds(lane, 768)]
            done.append(pltpu.make_async_copy(source, where, sems.at[base + block]))
        return done

    def fill(self, refs, me_ref, target, rest=()):
        pass

    def vectors(self, refs, me_ref, target):
        target[...] = refs[0][...].astype(F32)


def start_all(copies):
    for copy in copies:
        copy.start()


def wait_all(copies):
    for copy in copies:
        copy.wait()


def pair_masks(dims, axis):
    spot = lax.broadcasted_iota(jnp.int32, dims, axis)
    return spot < HD, spot >= HD


def keep(mask, value):
    return jnp.where(mask, value, jnp.zeros_like(value))


def attend_forward_body(group, part, me_ref, len_ref, x_ref, *refs):
    held, refs = refs[: len(group.held)], refs[len(group.held) :]
    sources = refs[: len(group.arrays)]
    q_ref, k_ref, v_ref, att_ref, left_ref, lse_ref, w_ref, vec_ref, ib_ref, packed, sems = refs[len(group.arrays) :]
    seq, width = x_ref.shape
    tile = min(256, seq)
    loads = group.copies(held, me_ref, w_ref, sems, 0)
    start_all(loads)
    group.fill(sources, me_ref, w_ref)
    group.vectors(sources, me_ref, packed)
    for f in range(packed.shape[0]):
        pack = packed[f]
        vec_ref[:, f * part : (f + 1) * part] = pack[:, :part]
        row, lane = divmod(f * 4 * part, width)
        ib_ref[row : row + 1, lane : lane + 4 * part] = pack[:1, 128 : 128 + 4 * part]
    for p in range(width // 128):
        left_ref[0, p * 128 : (p + 1) * 128, :] = flip(x_ref[:, p * 128 : (p + 1) * 128])
    wait_all(loads)

    def project(r, carry):
        rows = aligned(r * tile, tile)
        x = x_ref[rows, :]
        q_ref[rows, :] = (dot_nn(x, w_ref[0]) + vec_ref[0:1, :]).astype(BF16)
        k_ref[rows, :] = dot_nn(x, w_ref[1]).astype(BF16)
        v_ref[rows, :] = (dot_nn(x, w_ref[2]) + vec_ref[1:2, :]).astype(BF16)
        return carry

    lax.fori_loop(0, seq // tile, project, 0)
    length = len_ref[0]

    def pair(p, carry):
        lanes = aligned(p * 128, 128)
        k_pair = k_ref[:, lanes]
        q_t = (q_ref[:, lanes].astype(F32) * SCALE).T.astype(BF16)
        v_t = flip(v_ref[:, lanes])
        masks = pair_masks((128, seq), 0)
        allowed = lax.broadcasted_iota(jnp.int32, (seq, seq), 0) < length
        for e in range(2):
            s = dot_nn(k_pair, keep(masks[e], q_t))
            s = jnp.where(allowed, s, MASKED)
            top = jnp.max(s, axis=0, keepdims=True)
            p_t = jnp.exp(s - top)
            total = jnp.sum(p_t, axis=0, keepdims=True)
            o_t = dot_nn(v_t[e * HD : (e + 1) * HD, :], p_t.astype(BF16)) / total
            left_ref[1, aligned(p * 128 + e * HD, HD), :] = o_t.astype(BF16)
            lse_ref[pl.ds(p * 2 + e, 1), :] = top + jnp.log(total)
        att_ref[:, lanes] = flip(left_ref[1, aligned(p * 128, 128), :])
        return carry

    lax.fori_loop(0, width // 128, pair, 0)


def attend_forward(group, shards, blocks, me, length, x):
    seq, width = x.shape
    heads = width // HD
    return pl.pallas_call(
        functools.partial(attend_forward_body, group, width // shards),
        out_shape=(local(seq, width),) * 4
        + (local(2, width, seq), local(-(-heads // 8) * 8, seq, dtype=F32), local(4, width, width))
        + (local(8, width, dtype=F32), local(blocks, width, dtype=F32)),
        in_specs=[SM, SM, VM] + [HB] * len(group.held) + [VM] * len(group.arrays),
        out_specs=[VM] * 9,
        scratch_shapes=[pltpu.VMEM((shards, 8, width), F32), pltpu.SemaphoreType.DMA((group.count(),))],
        compiler_params=limit(10),
        cost_estimate=FREE,
        name="attend_forward",
    )(me, length, x, *far_off(*group.held), *stay(*group.arrays))


def attend_backward_body(first, last, len_ref, q_ref, k_ref, v_ref, do_ref, lse_ref, branch_ref, *refs):
    g_ref, sum_ref = refs[-2:]
    seq, width = q_ref.shape
    length = len_ref[0]

    def pair(p, carry):
        lanes = aligned(p * 128, 128)
        q_pair = (q_ref[:, lanes].astype(F32) * SCALE).astype(BF16)
        k_pair = k_ref[:, lanes]
        v_pair = v_ref[:, lanes]
        do_pair = do_ref[:, lanes]
        q_t = flip(q_pair)
        k_t = (k_pair.astype(F32) * SCALE).T.astype(BF16)
        do_t = flip(do_pair)
        sub_masks = pair_masks((128, seq), 0)
        lane_masks = pair_masks((seq, 128), 1)
        allowed = lax.broadcasted_iota(jnp.int32, (seq, seq), 0) < length
        dk = jnp.zeros((seq, 128), F32)
        dv = jnp.zeros((seq, 128), F32)
        dq_t = []
        for e in range(2):
            s = dot_nn(k_pair, keep(sub_masks[e], q_t))
            s = jnp.where(allowed, s, MASKED)
            p_t = jnp.exp(s - lse_ref[pl.ds(p * 2 + e, 1), :])
            dp = dot_nn(v_pair, keep(sub_masks[e], do_t))
            dv = dv + dot_nn(p_t.astype(BF16), keep(lane_masks[e], do_pair))
            t = p_t * dp
            row = jnp.sum(t, axis=0, keepdims=True)
            ds = (t - p_t * row).astype(BF16)
            dk = dk + dot_nn(ds, keep(lane_masks[e], q_pair))
            dq_t.append(dot_nn(k_t[e * HD : (e + 1) * HD, :], ds))
        dq = jnp.concatenate(dq_t, axis=0).T.astype(BF16)
        dv = dv.astype(BF16)
        g_ref[0, :, lanes] = dq
        g_ref[1, :, lanes] = dk.astype(BF16)
        g_ref[2, :, lanes] = dv
        g_ref[3, :, lanes] = branch_ref[:, lanes]
        sum_ref[0:1, lanes] = column_sum(dq)
        sum_ref[1:2, lanes] = column_sum(dv)
        return carry

    lax.fori_loop(first, last, pair, 0)


def attend_backward(first, last, length, q, k, v, do, lse, branch, before=()):
    seq, width = q.shape
    return pl.pallas_call(
        functools.partial(attend_backward_body, first, last),
        out_shape=(local(4, seq, width), local(8, width, dtype=F32)),
        in_specs=[SM] + [VM] * 6 + [HB] * len(before),
        out_specs=[VM] * 2,
        input_output_aliases={7 + n: n for n in range(len(before))},
        compiler_params=limit(10),
        cost_estimate=FREE,
        name="attend_backward",
    )(length, *stay(q, k, v, do, lse, branch, *before))


def gelu_parts(inner):
    cumulative = 0.5 * (1.0 + lax.erf(inner * ROOT_HALF))
    density = jnp.exp(-0.5 * inner * inner) * INV_ROOT_TWO_PI
    return inner * cumulative, cumulative + inner * density


def fill_body(group, early, me_ref, *refs):
    held, near = refs[: len(group.held)], refs[len(group.held) : len(group.held) + len(group.arrays)]
    if not early:
        group.fill(near, me_ref, refs[-1], (3,))
        return
    target, sems = refs[-2:]
    loads = group.copies(held, me_ref, target, sems, 0)
    start_all(loads)
    group.fill(near, me_ref, target, (0, 1, 2))
    wait_all(loads)


def fill(group, me, *dims, before=None):
    early = before is None
    more = () if early else (before,)
    return pl.pallas_call(
        functools.partial(fill_body, group, early),
        out_shape=local(*dims),
        in_specs=[SM] + [HB] * len(group.held) + [VM] * len(group.arrays) + [HB] * len(more),
        out_specs=VM,
        scratch_shapes=[pltpu.SemaphoreType.DMA((group.count(),))] * early,
        input_output_aliases={} if early else {1 + len(group.held) + len(group.arrays): 0},
        compiler_params=limit(2),
        cost_estimate=FREE,
        name="fill",
    )(me, *far_off(*group.held), *stay(*group.arrays, *more))


def middle_forward_body(
    len_ref,
    x_ref,
    att_ref,
    cot_ref,
    vec_ref,
    ib_ref,
    wa,
    wi,
    wu,
    out_ref,
    ssg_ref,
    low_ref,
    actT_ref,
    slope_ref,
    norm_ref,
    rstd_ref,
    hidT_ref,
    sum_ref,
):
    seq, width = x_ref.shape
    blocks = wi.shape[0]
    tile = min(256, seq)
    length = len_ref[0]
    sum_ref[...] = jnp.zeros_like(sum_ref)

    def rows_step(r, carry):
        rows = aligned(r * tile, tile)
        first = x_ref[rows, :].astype(F32) + dot_nn(att_ref[rows, :], wa[3]) + vec_ref[2:3, :]
        center = first - row_mean(first)
        rstd = lax.rsqrt(row_mean(center * center) + EPSILON)
        normed = center * rstd
        norm_ref[rows, :] = normed
        rstd_ref[rows, :] = rstd
        hidden = normed * vec_ref[3:4, :] + vec_ref[4:5, :]
        low = hidden.astype(BF16)
        hidT_ref[:, rows] = low.astype(F32).T.astype(BF16)

        def block(f, second):
            inner = dot_nn(low, wi[f]) + ib_ref[pl.ds(f, 1), :]
            active, slope = gelu_parts(inner)
            active = active.astype(BF16)
            spot = aligned(f * width, width)
            slope_ref[rows, spot] = slope.astype(BF16)
            actT_ref[spot, rows] = flip(active)
            return second + dot_nn(active, wu[spot, :])

        second = lax.fori_loop(0, blocks, block, hidden + vec_ref[5:6, :])
        center = second - row_mean(second)
        rstd = lax.rsqrt(row_mean(center * center) + EPSILON)
        normed = center * rstd
        spot = r * tile + lax.broadcasted_iota(jnp.int32, (tile, width), 0)
        valid = spot < length
        result = normed * vec_ref[6:7, :] + vec_ref[7:8, :]
        out_ref[rows, :] = jnp.where(valid, result, 0.0).astype(BF16)
        grad = jnp.where(valid, cot_ref[rows, :].astype(F32), 0.0)
        sum_ref[7:8, :] += column_sum(grad)
        sum_ref[6:7, :] += column_sum(grad * normed)
        grad = grad * vec_ref[6:7, :]
        grad = rstd * (grad - row_mean(grad) - normed * row_mean(grad * normed))
        ssg_ref[rows, :] = grad
        low = grad.astype(BF16)
        low_ref[rows, :] = low
        sum_ref[5:6, :] += column_sum(low)
        return carry

    lax.fori_loop(0, seq // tile, rows_step, 0)


def middle_forward(length, x, att, cot, vec, ib, wa, wi, wu):
    seq, width = x.shape
    blocks = ib.shape[0]
    return pl.pallas_call(
        middle_forward_body,
        out_shape=(
            shape(seq, width),
            local(seq, width, dtype=F32),
            local(seq, width),
            local(blocks * width, seq),
            local(seq, blocks * width),
            local(seq, width, dtype=F32),
            local(seq, 1, dtype=F32),
            local(width, seq),
            local(8, width, dtype=F32),
        ),
        in_specs=[SM] + [VM] * 8,
        out_specs=[VM] * 9,
        compiler_params=limit(12),
        cost_estimate=FREE,
        name="middle_forward",
    )(length, x, *stay(att), cot, *stay(vec, ib, wa, wi, wu))


def middle_backward_body(
    low_ref, ssg_ref, slope_ref, norm_ref, rstd_ref, vec_ref, wa, wi, wu, igl_ref, fsg_ref, branch_ref, att_ref, ib_ref, sum_ref
):
    seq, width = low_ref.shape
    blocks = wi.shape[0]
    tile = min(256, seq)
    sum_ref[...] = jnp.zeros_like(sum_ref)
    ib_ref[...] = jnp.zeros_like(ib_ref)

    def rows_step(r, carry):
        rows = aligned(r * tile, tile)
        low = low_ref[rows, :]

        def block(f, grad):
            spot = aligned(f * width, width)
            inner = (dot_nt(low, wu[spot, :]) * slope_ref[rows, spot].astype(F32)).astype(BF16)
            igl_ref[f, rows, :] = inner
            ib_ref[pl.ds(f, 1), :] += column_sum(inner)
            return grad + dot_nt(inner, wi[f])

        grad = lax.fori_loop(0, blocks, block, ssg_ref[rows, :])
        normed = norm_ref[rows, :]
        sum_ref[4:5, :] += column_sum(grad)
        sum_ref[3:4, :] += column_sum(grad * normed)
        grad = grad * vec_ref[3:4, :]
        grad = rstd_ref[rows, :] * (grad - row_mean(grad) - normed * row_mean(grad * normed))
        fsg_ref[rows, :] = grad
        branch = grad.astype(BF16)
        branch_ref[rows, :] = branch
        sum_ref[2:3, :] += column_sum(branch)
        att_ref[rows, :] = dot_nt(branch, wa[3]).astype(BF16)
        return carry

    lax.fori_loop(0, seq // tile, rows_step, 0)


def middle_backward(low, ssg, slope, norm, rstd, vec, wa, wi, wu):
    seq, width = low.shape
    blocks = wi.shape[0]
    return pl.pallas_call(
        middle_backward_body,
        out_shape=(
            local(blocks, seq, width),
            local(seq, width, dtype=F32),
            local(seq, width),
            local(seq, width),
            local(blocks, width, dtype=F32),
            local(8, width, dtype=F32),
        ),
        in_specs=[VM] * 9,
        out_specs=[VM] * 6,
        compiler_params=limit(10),
        cost_estimate=FREE,
        name="middle_backward",
    )(*stay(low, ssg, slope, norm, rstd, vec, wa, wi, wu))


def input_grad_body(g_ref, fsg_ref, w_ref, out_ref, token_ref):
    seq, width = fsg_ref.shape
    token_ref[...] = jnp.zeros_like(token_ref)
    tile = min(256, seq)

    def rows_step(r, carry):
        rows = aligned(r * tile, tile)
        total = fsg_ref[rows, :]
        for n in range(3):
            total = total + dot_nt(g_ref[n, rows, :], w_ref[n])
        out_ref[rows, :] = total
        return carry

    lax.fori_loop(0, seq // tile, rows_step, 0)


def input_grad(g, fsg, wa):
    seq, width = fsg.shape
    return pl.pallas_call(
        input_grad_body,
        out_shape=(shape(seq, width, dtype=F32), local(8, 128, dtype=F32)),
        in_specs=[VM] * 3,
        out_specs=[VM] * 2,
        compiler_params=limit(8),
        cost_estimate=FREE,
        name="input_grad",
    )(*stay(g, fsg, wa))


Z_ORDER = (0, 2, 1, 3)


def weight_grad_body(kind, order, z_order, me_ref, left_ref, g_ref, *refs):
    sums, refs = (refs[:4], refs[4:]) if kind == "attend" else ((), refs)
    outs, left = refs[:2], refs[2]
    i, z, c = me_ref[0], me_ref[1], me_ref[2]
    part = 96
    if kind == "attend":
        extra = refs[3]
        one, two, three, ib = (r[...] for r in sums)
        row = lax.broadcasted_iota(jnp.int32, one.shape, 0)
        every = jnp.where(row < 2, three, jnp.where(row < 5, two, one))
        for f in range(8):
            extra[f] = jnp.zeros_like(extra[f])
            extra[f, :, :part] = every[:, f * part : (f + 1) * part]
            extra[f, 0:1, 128 : 128 + 4 * part] = ib[f // 2 : f // 2 + 1, f % 2 * 4 * part : (f % 2 + 1) * 4 * part]

    def one_block(spot, away, c_at, out_ref):
        block = i ^ away
        for n, j in enumerate(z_order):
            f_at = 2 * (z ^ j) + c_at
            if kind == "outer":
                rows = left_ref[aligned_rows(f_at * 384 + block * 96, 96), :]
            elif kind == "inner":
                rows = left_ref[aligned_rows(f_at * 96, 96), :]
            else:
                rows = left_ref[block // 3, aligned_rows(f_at * 96, 96), :]
            left[n * 96 : (n + 1) * 96, :] = rows
        right = g_ref[...] if kind == "outer" else g_ref[block]
        grads = dot_nn(left[...], right).reshape(4, 96, 768).astype(BF16)
        out_ref[spot, :, :96, :] = grads
        if kind == "attend":
            for n, j in enumerate(z_order):
                out_ref[spot, n, 96:104, :] = extra[2 * (z ^ j) + c_at].astype(BF16)

    def block_step(c_at, out_ref, spot, carry):
        one_block(spot, pick(order, spot), c_at, out_ref)
        return carry

    lax.fori_loop(0, 4, functools.partial(block_step, 1 - c, outs[0]), 0)
    lax.fori_loop(0, 4, functools.partial(block_step, c, outs[1]), 0)


def weight_grad(kind, order, z_order, me, left, g, sums=()):
    rows = 104 if kind == "attend" else 96
    return pl.pallas_call(
        functools.partial(weight_grad_body, kind, order, z_order),
        out_shape=(local(4, 4, rows, 768),) * 2,
        in_specs=[SM] + [VM] * (2 + len(sums)),
        out_specs=[VM] * 2,
        scratch_shapes=[pltpu.VMEM((384, left.shape[-1]), BF16)] + [pltpu.VMEM((8, 8, 768), F32)] * (kind == "attend"),
        compiler_params=limit(6),
        cost_estimate=FREE,
        name=f"weight_grad_{kind}",
    )(me, *stay(left, g, *sums))


def prepare_body(me_ref, *refs):
    vectors, weights = refs[:9], refs[9:15]
    first_ref, second_ref, pack_ref, *rows, sems = refs[15:]
    i = me_ref[0]
    part = vectors[0].shape[0]
    copies = [
        pltpu.make_async_copy(
            weights[4].at[:, pl.ds(pl.multiple_of(i * 768, 768), 768)], second_ref.at[pl.ds(0, 96), :], sems.at[0]
        ),
        pltpu.make_async_copy(weights[5].at[aligned_rows(i * 96, 96), :], second_ref.at[pl.ds(96, 96), :], sems.at[1]),
    ]
    for n in range(9):
        copies.append(pltpu.make_async_copy(vectors[n], rows[n], sems.at[3 + n]))
    for n in range(4):

        @pl.when(i == n)
        def _():
            pltpu.make_async_copy(weights[n], first_ref.at[pl.ds(0, 96), :], sems.at[2]).start()

    start_all(copies)
    pack_ref[...] = jnp.zeros_like(pack_ref)
    wait_all(copies[2:])
    for n in range(8):
        pack_ref[n : n + 1, :part] = rows[n][...].astype(F32).reshape(1, part)
    pack_ref[0:1, 128 : 128 + 4 * part] = rows[8][...].astype(F32).reshape(1, 4 * part)
    first_ref[96:104, :] = pack_ref[...].astype(BF16)
    pltpu.make_async_copy(weights[0], first_ref.at[pl.ds(0, 96), :], sems.at[2]).wait()
    wait_all(copies[:2])


def prepare(me, vectors, weights):
    return pl.pallas_call(
        prepare_body,
        out_shape=(local(104, 768), local(192, 768)),
        in_specs=[SM] + [HB] * 15,
        out_specs=[VM] * 2,
        scratch_shapes=[pltpu.VMEM((8, 768), F32)]
        + [pltpu.VMEM(v.shape, BF16) for v in vectors]
        + [pltpu.SemaphoreType.DMA((12,))],
        compiler_params=limit(2),
        cost_estimate=FREE,
        name="prepare",
    )(me, *far_off(*vectors, *weights))


def after(value, *others):
    def body(*refs):
        pass

    return pl.pallas_call(
        body,
        out_shape=jax.ShapeDtypeStruct(value.shape, value.dtype),
        in_specs=[HB] * (1 + len(others)),
        out_specs=HB,
        input_output_aliases={0: 0},
        compiler_params=limit(1),
        cost_estimate=FREE,
        name="after",
    )(value, *others)


def swap(value, axis, size, mask):
    return lax.ppermute(value, axis, [(n, n ^ mask) for n in range(size)])


def gather_z(piece, fsdp):
    return [swap(piece, "fsdp", fsdp, 2 * j) for j in (1, 2, 3)]


def combine(*outs, cost=FREE):
    arrays = []
    for _, parts in outs:
        for _, terms in parts:
            arrays += [a for a, _ in terms if not any(a is b for b in arrays)]

    def find(array):
        return next(n for n, b in enumerate(arrays) if b is array)

    def body(*refs):
        for out_ref, (lead, parts) in zip(refs[len(arrays) :], outs, strict=True):

            def tile(index):
                start = 0
                for rows, terms in parts:
                    found = [(find(array), at(*index)) for array, at in terms]
                    values = [refs[n][spot] for n, spot in found if spot is not None]
                    value = values[0] if len(values) == 1 else sum(v.astype(F32) for v in values).astype(BF16)
                    out_ref[(*index, slice(start, start + rows), slice(None))] = value
                    start += rows

            def step(front, last, carry):
                tile((*front, last))
                return carry

            if not lead:
                tile(())
            elif len(lead) == 1:
                lax.fori_loop(0, lead[0], functools.partial(step, ()), 0)
            else:
                for front in range(lead[0]):
                    lax.fori_loop(0, lead[1], functools.partial(step, (front,)), 0)

    return pl.pallas_call(
        body,
        out_shape=tuple(local(*lead, sum(rows for rows, _ in parts), 768) for lead, parts in outs),
        in_specs=[VM] * len(arrays),
        out_specs=[VM] * len(outs),
        compiler_params=limit(2),
        cost_estimate=cost,
        name="combine",
    )(*stay(*arrays))


def stack_three(parts):
    rows = parts[0].shape[0]

    def body(*refs):
        for n in range(3):
            refs[3][n] = refs[n][...]

    return pl.pallas_call(
        body,
        out_shape=local(3, rows, 768),
        in_specs=[VM] * 3,
        out_specs=VM,
        compiler_params=limit(2),
        cost_estimate=FREE,
        name="stack_three",
    )(*stay(*parts))


def rows_of(value, start, rows):
    (part,) = combine(((value.shape[0],), [(rows, [(value, lambda n: (n, slice(start, start + rows)))])]))
    return part


UPPER = slice(0, 48)


def held(pair, block, rows):
    return [(v, lambda b: (block, b, rows)) for v in pair]


def first_pair(pair, total):
    def sums(blocks, rows, size):
        terms = []
        for n, block in enumerate(blocks):
            for array, at in held(pair, block, rows):
                terms.append((array, lambda a, b, n=n, at=at: at(b) if a == n else None))
        return combine(((2, 4), [(size, terms)]))[0]

    return sums((1, 3), UPPER, 48), sums((2, 3), slice(48, total), total - 48)


def second_pair(pair, over_x, over_y, total):
    (x,) = combine(((4,), [(48, held(pair, 2, UPPER) + [(over_x, lambda b: (1, b))])]))
    (y,) = combine(((4,), [(total - 48, held(pair, 1, slice(48, total)) + [(over_y, lambda b: (1, b))])]))
    return x, y


def last_terms(pair, overs, onwards, total, tile):
    parts = []
    for rows, size, over, onward in (
        (UPPER, 48, overs[0], onwards[0]),
        (slice(48, total), total - 48, overs[1], onwards[1]),
    ):
        terms = [(array, lambda *n, at=at: at(tile(*n))) for array, at in held(pair, 0, rows)]
        terms += [(over, lambda *n: (0, tile(*n))), (onward, lambda *n: (tile(*n),))]
        parts.append((size, terms))
    return parts


def last_pair(pair, overs, onwards, cost=FREE):
    return combine(*[((2,), last_terms(pair, overs, onwards, 96, lambda b, k=k: k + b)) for k in (0, 2)], cost=cost)


def finish(terms):
    def body(*refs):
        terms, (own_ref, small_ref) = refs[:-2], refs[-2:]
        value = sum(r[...].astype(F32) for r in terms)
        own_ref[...] = value[:96].astype(BF16)
        small_ref[...] = value[96:]

    return pl.pallas_call(
        body,
        out_shape=(local(96, 768), local(8, 768, dtype=F32)),
        in_specs=[VM] * len(terms),
        out_specs=[VM] * 2,
        compiler_params=limit(2),
        cost_estimate=FREE,
        name="finish",
    )(*stay(*terms))


def spread(value, dp):
    return (value,) + tuple(swap(value, "dp", dp, m) for m in (1, 2, 3))


def pick(pieces, index):
    return jnp.where(index == 0, pieces[0], jnp.where(index == 1, pieces[1], jnp.where(index == 2, pieces[2], pieces[3])))


def in_order(pieces, i):
    return [pick(pieces, n ^ i) for n in range(4)]


def on_device(
    sizes,
    tokens,
    lengths,
    cotangent,
    query_weight,
    query_bias,
    key_weight,
    value_weight,
    value_bias,
    output_weight,
    output_bias,
    first_gain,
    first_shift,
    inner_weight,
    inner_bias,
    outer_weight,
    outer_bias,
    second_gain,
    second_shift,
):
    dp, fsdp = sizes
    docs, seq, width = tokens.shape
    blocks = inner_weight.shape[1] // width
    direct = dp == 4 and fsdp == 8 and docs == 1 and query_weight.shape == (96, 768) and blocks == 4
    i = lax.axis_index("dp")
    f = lax.axis_index("fsdp")
    me = jnp.stack([i, f // 2, f % 2, jnp.zeros_like(i)]).astype(jnp.int32)

    small = (query_bias, value_bias, output_bias, first_gain, first_shift, outer_bias, second_gain, second_shift, inner_bias)
    part = query_bias.shape[0]

    if direct:
        mine = (query_weight, key_weight, value_weight, output_weight)
        piece_a, piece_m = prepare(me, small, mine + (inner_weight, outer_weight))
        z_a = gather_z(piece_a, fsdp)
        z_m = gather_z(piece_m, fsdp)
        mine_a = stack_three(z_a)
        plane_a = (swap(mine_a, "dp", dp, 1), swap(mine_a, "dp", dp, 2))
        parts_a = (rows_of(plane_a[0], 0, 48), rows_of(plane_a[1], 48, 48))
        rest_a = (swap(parts_a[0], "dp", dp, 2), swap(parts_a[1], "dp", dp, 1))
        z_m[0] = after(z_m[0], *rest_a)
        mine_m = stack_three(z_m)
        plane_m = (swap(mine_m, "dp", dp, 1), swap(mine_m, "dp", dp, 2))
        near_a = bundle(1, mine, ((((0, 0)),),) * 4, (after(mine_a, mine_m),) + plane_a + (piece_a,))
        far_a = (swap(near_a, "fsdp", fsdp, 1),) + tuple(swap(v, "fsdp", fsdp, 1) for v in rest_a)

        def far_at(base, row=0):
            return [[(base + n, 0, row, 96, 0)] for n in range(3)]

        group_a = Pieces(
            mine,
            (mine_a,) + plane_a + rest_a + far_a + (piece_a,),
            [(n, 0, 0) for n in range(4)],
            [(5, n) for n in range(4)],
            far_at(0) + [[(3, 0, 0, 48, 0), (4, 0, 0, 48, 48)]],
            [[(5, 4 + 3 * n, 0, 96, 0)] for n in range(3)] + [[(6, 0, 0, 48, 0), (7, 0, 0, 48, 48)]],
            True,
            (8, 0, 5),
        )
        x = tokens.reshape(seq, width)
        q, k, v, att, left_a, lse, wa, vec, ib = attend_forward(group_a, fsdp, blocks, me, lengths, after(x, mine_m))
        plane_m = (after(plane_m[0], att), after(plane_m[1], att))
        parts_m = (rows_of(plane_m[0], 0, 96), rows_of(plane_m[1], 96, 96))
        rest_m = (swap(parts_m[0], "dp", dp, 2), swap(parts_m[1], "dp", dp, 1))
        spots = (tuple((0, 768 * n) for n in range(4)), tuple((96 * n, 0) for n in range(4)))
        near_m = bundle(2, (inner_weight, outer_weight), spots, (mine_m,) + plane_m)
        far_m = (swap(near_m, "fsdp", fsdp, 1),) + tuple(swap(v, "fsdp", fsdp, 1) for v in rest_m)
        four = range(4)
        early_i = Pieces(
            (inner_weight,),
            (mine_m,) + plane_m + (far_m[0],),
            [(0, 0, 768 * n) for n in four],
            [(3, n) for n in four],
            far_at(0),
            [[(3, 8 + 6 * n, 0, 96, 0)] for n in range(3)],
            True,
        )
        early_u = Pieces(
            (outer_weight,),
            (mine_m,) + plane_m + (far_m[0],),
            [(0, 96 * n, 0) for n in four],
            [(3, 4 + n) for n in four],
            far_at(0, 96),
            [[(3, 11 + 6 * n, 0, 96, 0)] for n in range(3)],
            False,
        )
        none = [None] * 3
        late_i = Pieces((), (rest_m[0], far_m[1]), (), (), none + [[(0, 0, 0, 96, 0)]], none + [[(1, 0, 0, 96, 0)]], True)
        late_u = Pieces((), (rest_m[1], far_m[2]), (), (), none + [[(0, 0, 0, 96, 0)]], none + [[(1, 0, 0, 96, 0)]], False)
        wi = fill(early_i, me, blocks, width, width)
        wu = fill(early_u, me, blocks * width, width)
        wi = fill(late_i, me, blocks, width, width, before=wi)
        wu = fill(late_u, me, blocks * width, width, before=wu)
    else:
        whole = tuple(
            lax.all_gather(w, "fsdp", axis=0, tiled=True)
            for w in (query_weight, key_weight, value_weight, output_weight, inner_weight, outer_weight)
        )
        packs = jnp.pad(jnp.stack(small[:8]), ((0, 0), (0, width - part)))
        packs = packs + jnp.pad(inner_bias[None], ((0, 7), (128, width - 128 - 4 * part)))
        packs = lax.all_gather(packs, "fsdp", axis=0, tiled=False)
        group_a = Whole(whole[:4], (packs,), [(n, 0, 0) for n in range(4)], True)
        group_i = Whole(whole[4:5], (), [(0, 0, width * n) for n in range(blocks)], True)
        group_u = Whole(whole[5:6], (), [(0, width * n, 0) for n in range(blocks)], False)
        x = tokens.reshape(seq, width)
        q, k, v, att, left_a, lse, wa, vec, ib = attend_forward(group_a, fsdp, blocks, me, lengths, x)
        wi = fill(group_i, me, blocks, width, width)
        wu = fill(group_u, me, blocks * width, width)

    cot = cotangent.reshape(seq, width)
    out, ssg, low, act_t, slope, norm, rstd, hid_t, sum_one = middle_forward(lengths, x, att, cot, vec, ib, wa, wi, wu)
    pairs = width // 128
    attend = functools.partial(attend_backward, length=lengths, q=q, k=k, v=v, lse=lse)
    if direct:
        sent_u, kept_u = weight_grad("outer", (0, 1, 2, 3), Z_ORDER, me, act_t, low)
        got_u = swap(sent_u, "fsdp", fsdp, 1)
        low = after(low, sent_u)
    igl, fsg, branch, att_g, ib_sum, sum_two = middle_backward(low, ssg, slope, norm, rstd, vec, wa, wi, wu)
    if direct:
        pair_u = (kept_u, got_u)
        first_u = first_pair(pair_u, 96)
        over_u = [swap(first_u[0], "dp", dp, 1), swap(first_u[1], "dp", dp, 2)]
        sent_i, kept_i = weight_grad("inner", (0, 1, 2, 3), Z_ORDER, me, hid_t, after(igl, *first_u))
        got_i = swap(sent_i, "fsdp", fsdp, 1)
        half = attend(0, pairs // 2, do=after(att_g, sent_i), branch=branch)
        pair_i = (kept_i, after(got_i, half[0]))
        first_i = first_pair(pair_i, 96)
        over_i = [swap(first_i[0], "dp", dp, 1), swap(first_i[1], "dp", dp, 2)]
        g, sum_three = attend(pairs // 2, pairs, do=after(att_g, *first_i), branch=branch, before=half)
    else:
        g, sum_three = attend(0, pairs, do=att_g, branch=branch)
        in_grad, _ = input_grad(g, fsg, wa)

    if direct:
        here = lambda: ()
        over_u = [after(v, g) for v in over_u]
        second_u = second_pair(pair_u, *over_u, 96)
        onward_u = [swap(second_u[0], "dp", dp, 2), swap(second_u[1], "dp", dp, 1)]

        left_a = after(left_a, *second_u)
        sent_a, kept_a = weight_grad(
            "attend", (0, 1, 2, 3), (0, 1, 2, 3), me, left_a, g, (sum_one, sum_two, sum_three, ib_sum)
        )
        in_grad, token = input_grad(g, after(fsg, kept_a), wa)

        over_i = [after(v, token) for v in over_i]
        second_i = second_pair(pair_i, *over_i, 96)
        onward_i = [swap(second_i[0], "dp", dp, 2), swap(second_i[1], "dp", dp, 1)]

        got_a = swap(after(sent_a, *second_i), "fsdp", fsdp, 1)

        onward_u = [after(v, *second_i) for v in onward_u]
        keep_u, send_u = last_pair(pair_u, over_u, onward_u, LONG)
        near_u = swap(send_u, "fsdp", fsdp, 2)

        pair_a = (kept_a, after(got_a, keep_u))
        first_a = first_pair(pair_a, 104)
        over_a = [swap(first_a[0], "dp", dp, 1), swap(first_a[1], "dp", dp, 2)]

        onward_i = [after(v, *first_a) for v in onward_i]
        keep_i, send_i = last_pair(pair_i, over_i, onward_i, LONG)
        near_i = swap(send_i, "fsdp", fsdp, 2)

        near_u = after(near_u, keep_i)
        (next_u,) = combine(((), [(96, [(keep_u, lambda: (1,)), (near_u, lambda: (1,))])]))
        last_u = swap(next_u, "fsdp", fsdp, 4)

        over_a = [after(v, next_u) for v in over_a]
        second_a = second_pair(pair_a, *over_a, 104)
        onward_a = [swap(second_a[0], "dp", dp, 2), swap(second_a[1], "dp", dp, 1)]

        near_i = after(near_i, *second_a)
        (next_i,) = combine(((), [(96, [(keep_i, lambda: (1,)), (near_i, lambda: (1,))])]), cost=LONG)
        last_i = swap(next_i, "fsdp", fsdp, 4)

        last_u = after(last_u, next_i)
        terms_u = [(keep_u, lambda: (0,)), (near_u, lambda: (0,)), (last_u, here)]
        (own_u,) = combine(((), [(96, terms_u)]))

        last_i = after(last_i, own_u)
        terms_i = [(keep_i, lambda: (0,)), (near_i, lambda: (0,)), (last_i, here)]
        (own_i,) = combine(((), [(96, terms_i)]))

        onward_a = [after(v, own_i) for v in onward_a]
        whole_a = combine(*[((), last_terms(pair_a, over_a, onward_a, 104, lambda j=j: j)) for j in range(4)])
        far_a = [swap(whole_a[j], "fsdp", fsdp, 2 * j) for j in (1, 2, 3)]

        (own_m,) = combine(((), [(96, [(after(own_i, whole_a[0]), here)]), (96, [(own_u, here)])]))
        every = spread(own_m, dp)

        far_a[0] = after(far_a[0], own_m)
        own_a, small_own = finish((whole_a[0], *far_a))
        all_a = spread(own_a, dp)
        small_grads = [small_own[n, :part] for n in range(8)] + [small_own[0, 128 : 128 + blocks * part]]
        all_i, all_u = [v[:96] for v in every], [v[96:] for v in every]
        q_g, k_g, v_g, o_g = (w.astype(F32) for w in in_order(all_a, i))
        i_g = jnp.concatenate(in_order(all_i, i), axis=1).astype(F32)
        u_g = jnp.concatenate(in_order(all_u, i), axis=0).astype(F32)
    else:
        vec_sum = jnp.concatenate([sum_three[:2], sum_two[2:5], sum_one[5:8]])
        vec_sum = vec_sum.reshape(8, fsdp, part).transpose(1, 0, 2).reshape(fsdp, 8 * part)
        ib_part = ib_sum.reshape(fsdp, blocks * part)
        small_sum = lax.psum(jnp.concatenate([vec_sum, ib_part], axis=1), ("dp", "fsdp"))
        small_own = lax.dynamic_index_in_dim(small_sum, f, 0, keepdims=False)
        small_grads = [small_own[n * part : (n + 1) * part] for n in range(8)] + [small_own[8 * part :]]
        x_t, att_t = left_a[0], left_a[1]
        locals_ = (
            dot_nn(x_t, g[0]),
            dot_nn(x_t, g[1]),
            dot_nn(x_t, g[2]),
            dot_nn(att_t, g[3]),
            jnp.concatenate([dot_nn(hid_t, igl[n]) for n in range(blocks)], axis=1),
            dot_nn(act_t, low),
        )
        owned = [lax.psum_scatter(w, "fsdp", scatter_dimension=0, tiled=True) for w in locals_]
        q_g, k_g, v_g, o_g, i_g, u_g = (lax.psum(w.astype(BF16), "dp").astype(F32) for w in owned)

    qb, vb, ob, g1, s1, ub, g2, s2, ibg = small_grads
    return (
        out.reshape(docs, seq, width),
        in_grad.reshape(docs, seq, width),
        q_g,
        qb,
        k_g,
        v_g,
        vb,
        o_g,
        ob,
        g1,
        s1,
        i_g,
        ibg,
        u_g,
        ub,
        g2,
        s2,
    )


def solution(mesh):
    rows, row = P("fsdp", None), P("fsdp")
    docs = P(("dp", "fsdp"), None, None)
    in_specs = (docs, P(("dp", "fsdp")), docs, rows, row, rows, rows, row, rows, row, row, row, rows, row, rows, row, row, row)
    out_specs = (docs, docs, rows, row, rows, rows, row, rows, row, row, row, rows, row, rows, row, row, row)
    sizes = (mesh.shape["dp"], mesh.shape["fsdp"])
    return jax.shard_map(
        functools.partial(on_device, sizes), mesh=mesh, in_specs=in_specs, out_specs=out_specs, check_vma=False
    )
```

```python
import functools
import math

import jax
import jax.numpy as jnp
from jax import lax
from jax.experimental import pallas as pl
from jax.experimental.pallas import tpu as pltpu
from jax.sharding import PartitionSpec as P

F32 = jnp.float32
BF16 = jnp.bfloat16
HD = 64
MASKED = -1e30
SCALE = HD ** -0.5
EPSILON = 1e-12
ROOT_HALF = math.sqrt(0.5)
INV_ROOT_TWO_PI = 1.0 / math.sqrt(2.0 * math.pi)

VM = pl.BlockSpec(memory_space=pltpu.VMEM)
SM = pl.BlockSpec(memory_space=pltpu.SMEM)
HB = pl.BlockSpec(memory_space=pl.ANY)
FREE = pl.CostEstimate(flops=0, bytes_accessed=0, transcendentals=0)

LONG = pl.CostEstimate(flops=60_000_000_000, bytes_accessed=0, transcendentals=0)


def shape(*dims, dtype=BF16):
    return jax.ShapeDtypeStruct(dims, dtype)


def local(*dims, dtype=BF16):
    return pltpu.VMEM(dims, dtype)


def stay(*values):
    return tuple(pltpu.with_memory_space_constraint(v, pltpu.VMEM) for v in values)


def far_off(*values):
    return tuple(pltpu.with_memory_space_constraint(v, pltpu.HBM) for v in values)


def limit(mebibytes):
    return pltpu.CompilerParams(vmem_limit_bytes=mebibytes << 20)


def dot_nn(a, b):
    return lax.dot_general(a, b, (((1,), (0,)), ((), ())), preferred_element_type=F32)


def dot_nt(a, b):
    return lax.dot_general(a, b, (((1,), (1,)), ((), ())), preferred_element_type=F32)


def flip(value):
    return value.T


def column_sum(value):
    return jnp.sum(value.astype(F32), axis=0, keepdims=True)


def row_mean(value):
    return jnp.mean(value, axis=-1, keepdims=True)


def aligned(start, size):
    return pl.ds(pl.multiple_of(start, size), size)


class Pieces:
    def __init__(self, held, arrays, own, sibling, far, far_sibling, stacked, packs=()):
        self.held, self.arrays, self.own, self.sibling, self.packs = held, arrays, own, sibling, packs
        self.far, self.far_sibling, self.stacked = far, far_sibling, stacked

    def count(self):
        return len(self.own)

    def place(self, target, block, z_at, c_at, offset, rows):
        if self.stacked:
            return target.at[block, aligned_rows((2 * z_at + c_at) * 96 + offset, rows), :]
        return target.at[aligned_rows((2 * z_at + c_at) * 384 + block * 96 + offset, rows), :]

    def copies(self, held, me_ref, target, sems, base):
        z, c = me_ref[1], me_ref[2]
        done = []
        for block, (position, row, lane) in enumerate(self.own):
            where = self.place(target, block, z, c, 0, 96)
            source = held[position].at[pl.ds(row, 96), pl.ds(lane, 768)]
            done.append(pltpu.make_async_copy(source, where, sems.at[base + block]))
        return done

    def fill(self, refs, me_ref, target, rest=(0, 1, 2, 3)):
        i, z, c = me_ref[0], me_ref[1], me_ref[2]
        for block, (position, tile) in enumerate(self.sibling if 0 in rest else ()):
            self.place(target, block, z, 1 - c, 0, 96)[...] = refs[position][tile]
        for c_at, far in ((c, self.far), (1 - c, self.far_sibling)):
            for away in rest:
                parts = far[away]
                for position, tile, row, rows, offset in parts:
                    for j in range(1, 4):
                        where = self.place(target, i ^ away, z ^ j, c_at, offset, rows)
                        where[...] = refs[position][tile + j - 1, row : row + rows, :]

    def vectors(self, refs, me_ref, target):
        z, c = me_ref[1], me_ref[2]
        own, mine, other = (refs[n] for n in self.packs)
        for j in range(4):
            target[2 * (z ^ j) + c] = (mine[j - 1, 96:104, :] if j else own[96:104, :]).astype(F32)
            target[2 * (z ^ j) + 1 - c] = other[13, 8 * j : 8 * j + 8, :].astype(F32)


def bundle_body(group_count, held, me_ref, *refs):
    sources, near = refs[: len(held)], refs[len(held) : -2]
    out_ref, sems = refs[-2:]
    own = [(n, row, lane) for n, spots in enumerate(held) for row, lane in spots]
    loads = []
    for tile, (n, row, lane) in enumerate(own):
        source = sources[n].at[pl.ds(row, 96), pl.ds(lane, 768)]
        loads.append(pltpu.make_async_copy(source, out_ref.at[tile], sems.at[tile]))
    start_all(loads)
    tile = len(own)
    for away in range(3):
        for group in range(group_count):
            for j in range(3):
                out_ref[tile] = near[away * group_count + group][j, :96, :]
                tile += 1
    if group_count == 1:
        out_ref[tile, 0:8, :] = near[3][96:104, :]
        for j in range(3):
            out_ref[tile, 8 * j + 8 : 8 * j + 16, :] = near[0][j, 96:104, :]
        out_ref[tile, 32:, :] = jnp.zeros((64, 768), BF16)
    wait_all(loads)


def bundle(group_count, sources, held, near):
    own = sum(len(spots) for spots in held)
    tiles = own + 9 * group_count + (group_count == 1)
    return pl.pallas_call(
        functools.partial(bundle_body, group_count, held),
        out_shape=local(tiles, 96, 768),
        in_specs=[SM] + [HB] * len(sources) + [VM] * len(near),
        out_specs=VM,
        scratch_shapes=[pltpu.SemaphoreType.DMA((own,))],
        compiler_params=limit(2),
        cost_estimate=FREE,
        name="bundle",
    )(jnp.zeros((1,), jnp.int32), *far_off(*sources), *stay(*near))


def aligned_rows(start, rows):
    return pl.ds(pl.multiple_of(start, 16), rows)


class Whole:
    def __init__(self, held, arrays, spots, stacked):
        self.held, self.arrays, self.spots, self.stacked = held, arrays, spots, stacked

    def count(self):
        return len(self.spots)

    def copies(self, held, me_ref, target, sems, base):
        done = []
        for block, (position, row, lane) in enumerate(self.spots):
            where = target.at[block] if self.stacked else target.at[pl.ds(block * 768, 768), :]
            source = held[position].at[pl.ds(row, 768), pl.ds(lane, 768)]
            done.append(pltpu.make_async_copy(source, where, sems.at[base + block]))
        return done

    def fill(self, refs, me_ref, target, rest=()):
        pass

    def vectors(self, refs, me_ref, target):
        target[...] = refs[0][...].astype(F32)


def start_all(copies):
    for copy in copies:
        copy.start()


def wait_all(copies):
    for copy in copies:
        copy.wait()


def pair_masks(dims, axis):
    spot = lax.broadcasted_iota(jnp.int32, dims, axis)
    return spot < HD, spot >= HD


def keep(mask, value):
    return jnp.where(mask, value, jnp.zeros_like(value))


def attend_forward_body(group, part, me_ref, len_ref, x_ref, *refs):
    held, refs = refs[: len(group.held)], refs[len(group.held) :]
    sources = refs[: len(group.arrays)]
    q_ref, k_ref, v_ref, att_ref, left_ref, lse_ref, w_ref, vec_ref, ib_ref, packed, sems = refs[len(group.arrays) :]
    seq, width = x_ref.shape
    tile = min(512, seq)
    loads = group.copies(held, me_ref, w_ref, sems, 0)
    start_all(loads)
    group.fill(sources, me_ref, w_ref)
    group.vectors(sources, me_ref, packed)
    for f in range(packed.shape[0]):
        pack = packed[f]
        vec_ref[:, f * part : (f + 1) * part] = pack[:, :part]
        row, lane = divmod(f * 4 * part, width)
        ib_ref[row : row + 1, lane : lane + 4 * part] = pack[:1, 128 : 128 + 4 * part]
    for p in range(width // 128):
        left_ref[0, p * 128 : (p + 1) * 128, :] = flip(x_ref[:, p * 128 : (p + 1) * 128])
    wait_all(loads)

    def project(r, carry):
        rows = aligned(r * tile, tile)
        x = x_ref[rows, :]
        q_ref[rows, :] = (dot_nn(x, w_ref[0]) + vec_ref[0:1, :]).astype(BF16)
        k_ref[rows, :] = dot_nn(x, w_ref[1]).astype(BF16)
        v_ref[rows, :] = (dot_nn(x, w_ref[2]) + vec_ref[1:2, :]).astype(BF16)
        return carry

    lax.fori_loop(0, seq // tile, project, 0)
    length = len_ref[0]

    def pair(p, carry):
        lanes = aligned(p * 128, 128)
        k_pair = k_ref[:, lanes]
        q_t = (q_ref[:, lanes].astype(F32) * SCALE).T.astype(BF16)
        v_t = flip(v_ref[:, lanes])
        masks = pair_masks((128, seq), 0)
        allowed = lax.broadcasted_iota(jnp.int32, (seq, seq), 0) < length
        for e in range(2):
            s = dot_nn(k_pair, keep(masks[e], q_t))
            s = jnp.where(allowed, s, MASKED)
            top = jnp.max(s, axis=0, keepdims=True)
            p_t = jnp.exp(s - top)
            total = jnp.sum(p_t, axis=0, keepdims=True)
            o_t = dot_nn(v_t[e * HD : (e + 1) * HD, :], p_t.astype(BF16)) / total
            left_ref[1, aligned(p * 128 + e * HD, HD), :] = o_t.astype(BF16)
            lse_ref[pl.ds(p * 2 + e, 1), :] = top + jnp.log(total)
        att_ref[:, lanes] = flip(left_ref[1, aligned(p * 128, 128), :])
        return carry

    lax.fori_loop(0, width // 128, pair, 0, unroll=2)


def attend_forward(group, shards, blocks, me, length, x):
    seq, width = x.shape
    heads = width // HD
    return pl.pallas_call(
        functools.partial(attend_forward_body, group, width // shards),
        out_shape=(local(seq, width),) * 4
        + (local(2, width, seq), local(-(-heads // 8) * 8, seq, dtype=F32), local(4, width, width))
        + (local(8, width, dtype=F32), local(blocks, width, dtype=F32)),
        in_specs=[SM, SM, VM] + [HB] * len(group.held) + [VM] * len(group.arrays),
        out_specs=[VM] * 9,
        scratch_shapes=[pltpu.VMEM((shards, 8, width), F32), pltpu.SemaphoreType.DMA((group.count(),))],
        compiler_params=limit(10),
        cost_estimate=FREE,
        name="attend_forward",
    )(me, length, x, *far_off(*group.held), *stay(*group.arrays))


def attend_backward_body(first, last, len_ref, q_ref, k_ref, v_ref, do_ref, lse_ref, branch_ref, *refs):
    g_ref, sum_ref = refs[-2:]
    seq, width = q_ref.shape
    length = len_ref[0]

    def pair(p, carry):
        lanes = aligned(p * 128, 128)
        q_pair = (q_ref[:, lanes].astype(F32) * SCALE).astype(BF16)
        k_pair = k_ref[:, lanes]
        v_pair = v_ref[:, lanes]
        do_pair = do_ref[:, lanes]
        q_t = flip(q_pair)
        k_t = (k_pair.astype(F32) * SCALE).T.astype(BF16)
        do_t = flip(do_pair)
        sub_masks = pair_masks((128, seq), 0)
        lane_masks = pair_masks((seq, 128), 1)
        allowed = lax.broadcasted_iota(jnp.int32, (seq, seq), 0) < length
        dk = jnp.zeros((seq, 128), F32)
        dv = jnp.zeros((seq, 128), F32)
        dq_t = []
        for e in range(2):
            s = dot_nn(k_pair, keep(sub_masks[e], q_t))
            s = jnp.where(allowed, s, MASKED)
            p_t = jnp.exp(s - lse_ref[pl.ds(p * 2 + e, 1), :])
            dp = dot_nn(v_pair, keep(sub_masks[e], do_t))
            dv = dv + dot_nn(p_t.astype(BF16), keep(lane_masks[e], do_pair))
            t = p_t * dp
            row = jnp.sum(t, axis=0, keepdims=True)
            ds = (t - p_t * row).astype(BF16)
            dk = dk + dot_nn(ds, keep(lane_masks[e], q_pair))
            dq_t.append(dot_nn(k_t[e * HD : (e + 1) * HD, :], ds))
        dq = jnp.concatenate(dq_t, axis=0).T.astype(BF16)
        dv = dv.astype(BF16)
        g_ref[0, :, lanes] = dq
        g_ref[1, :, lanes] = dk.astype(BF16)
        g_ref[2, :, lanes] = dv
        g_ref[3, :, lanes] = branch_ref[:, lanes]
        sum_ref[0:1, lanes] = column_sum(dq)
        sum_ref[1:2, lanes] = column_sum(dv)
        return carry

    lax.fori_loop(first, last, pair, 0, unroll=2)


def attend_backward(first, last, length, q, k, v, do, lse, branch, before=()):
    seq, width = q.shape
    return pl.pallas_call(
        functools.partial(attend_backward_body, first, last),
        out_shape=(local(4, seq, width), local(8, width, dtype=F32)),
        in_specs=[SM] + [VM] * 6 + [HB] * len(before),
        out_specs=[VM] * 2,
        input_output_aliases={7 + n: n for n in range(len(before))},
        compiler_params=limit(10),
        cost_estimate=FREE,
        name="attend_backward",
    )(length, *stay(q, k, v, do, lse, branch, *before))


def gelu_parts(inner):
    cumulative = 0.5 * (1.0 + lax.erf(inner * ROOT_HALF))
    density = jnp.exp(-0.5 * inner * inner) * INV_ROOT_TWO_PI
    return inner * cumulative, cumulative + inner * density


def fill_body(group, early, me_ref, *refs):
    held, near = refs[: len(group.held)], refs[len(group.held) : len(group.held) + len(group.arrays)]
    if not early:
        group.fill(near, me_ref, refs[-1], (3,))
        return
    target, sems = refs[-2:]
    loads = group.copies(held, me_ref, target, sems, 0)
    start_all(loads)
    group.fill(near, me_ref, target, (0, 1, 2))
    wait_all(loads)


def fill(group, me, *dims, before=None):
    early = before is None
    more = () if early else (before,)
    return pl.pallas_call(
        functools.partial(fill_body, group, early),
        out_shape=local(*dims),
        in_specs=[SM] + [HB] * len(group.held) + [VM] * len(group.arrays) + [HB] * len(more),
        out_specs=VM,
        scratch_shapes=[pltpu.SemaphoreType.DMA((group.count(),))] * early,
        input_output_aliases={} if early else {1 + len(group.held) + len(group.arrays): 0},
        compiler_params=limit(2),
        cost_estimate=FREE,
        name="fill",
    )(me, *far_off(*group.held), *stay(*group.arrays, *more))


def middle_forward_body(
    len_ref,
    x_ref,
    att_ref,
    cot_ref,
    vec_ref,
    ib_ref,
    wa,
    wi,
    wu,
    out_ref,
    ssg_ref,
    low_ref,
    actT_ref,
    slope_ref,
    norm_ref,
    rstd_ref,
    hidT_ref,
    sum_ref,
):
    seq, width = x_ref.shape
    blocks = wi.shape[0]
    tile = min(512, seq)
    length = len_ref[0]
    sum_ref[...] = jnp.zeros_like(sum_ref)

    def rows_step(r, carry):
        rows = aligned(r * tile, tile)
        first = x_ref[rows, :].astype(F32) + dot_nn(att_ref[rows, :], wa[3]) + vec_ref[2:3, :]
        center = first - row_mean(first)
        rstd = lax.rsqrt(row_mean(center * center) + EPSILON)
        normed = center * rstd
        norm_ref[rows, :] = normed
        rstd_ref[rows, :] = rstd
        hidden = normed * vec_ref[3:4, :] + vec_ref[4:5, :]
        low = hidden.astype(BF16)
        hidT_ref[:, rows] = low.astype(F32).T.astype(BF16)

        def block(f, second):
            inner = dot_nn(low, wi[f]) + ib_ref[pl.ds(f, 1), :]
            active, slope = gelu_parts(inner)
            active = active.astype(BF16)
            spot = aligned(f * width, width)
            slope_ref[rows, spot] = slope.astype(BF16)
            actT_ref[spot, rows] = flip(active)
            return second + dot_nn(active, wu[spot, :])

        second = lax.fori_loop(0, blocks, block, hidden + vec_ref[5:6, :], unroll=True)
        center = second - row_mean(second)
        rstd = lax.rsqrt(row_mean(center * center) + EPSILON)
        normed = center * rstd
        spot = r * tile + lax.broadcasted_iota(jnp.int32, (tile, width), 0)
        valid = spot < length
        result = normed * vec_ref[6:7, :] + vec_ref[7:8, :]
        out_ref[rows, :] = jnp.where(valid, result, 0.0).astype(BF16)
        grad = jnp.where(valid, cot_ref[rows, :].astype(F32), 0.0)
        sum_ref[7:8, :] += column_sum(grad)
        sum_ref[6:7, :] += column_sum(grad * normed)
        grad = grad * vec_ref[6:7, :]
        grad = rstd * (grad - row_mean(grad) - normed * row_mean(grad * normed))
        ssg_ref[rows, :] = grad
        low = grad.astype(BF16)
        low_ref[rows, :] = low
        sum_ref[5:6, :] += column_sum(low)
        return carry

    lax.fori_loop(0, seq // tile, rows_step, 0)


def middle_forward(length, x, att, cot, vec, ib, wa, wi, wu):
    seq, width = x.shape
    blocks = ib.shape[0]
    return pl.pallas_call(
        middle_forward_body,
        out_shape=(
            shape(seq, width),
            local(seq, width, dtype=F32),
            local(seq, width),
            local(blocks * width, seq),
            local(seq, blocks * width),
            local(seq, width, dtype=F32),
            local(seq, 1, dtype=F32),
            local(width, seq),
            local(8, width, dtype=F32),
        ),
        in_specs=[SM] + [VM] * 8,
        out_specs=[VM] * 9,
        compiler_params=limit(16),
        cost_estimate=FREE,
        name="middle_forward",
    )(length, x, *stay(att), cot, *stay(vec, ib, wa, wi, wu))


def middle_backward_body(
    low_ref, ssg_ref, slope_ref, norm_ref, rstd_ref, vec_ref, wa, wi, wu, igl_ref, fsg_ref, branch_ref, att_ref, ib_ref, sum_ref
):
    seq, width = low_ref.shape
    blocks = wi.shape[0]
    tile = min(512, seq)
    sum_ref[...] = jnp.zeros_like(sum_ref)
    ib_ref[...] = jnp.zeros_like(ib_ref)

    def rows_step(r, carry):
        rows = aligned(r * tile, tile)
        low = low_ref[rows, :]

        def block(f, grad):
            spot = aligned(f * width, width)
            inner = (dot_nt(low, wu[spot, :]) * slope_ref[rows, spot].astype(F32)).astype(BF16)
            igl_ref[f, rows, :] = inner
            ib_ref[pl.ds(f, 1), :] += column_sum(inner)
            return grad + dot_nt(inner, wi[f])

        grad = lax.fori_loop(0, blocks, block, ssg_ref[rows, :], unroll=True)
        normed = norm_ref[rows, :]
        sum_ref[4:5, :] += column_sum(grad)
        sum_ref[3:4, :] += column_sum(grad * normed)
        grad = grad * vec_ref[3:4, :]
        grad = rstd_ref[rows, :] * (grad - row_mean(grad) - normed * row_mean(grad * normed))
        fsg_ref[rows, :] = grad
        branch = grad.astype(BF16)
        branch_ref[rows, :] = branch
        sum_ref[2:3, :] += column_sum(branch)
        att_ref[rows, :] = dot_nt(branch, wa[3]).astype(BF16)
        return carry

    lax.fori_loop(0, seq // tile, rows_step, 0)


def middle_backward(low, ssg, slope, norm, rstd, vec, wa, wi, wu):
    seq, width = low.shape
    blocks = wi.shape[0]
    return pl.pallas_call(
        middle_backward_body,
        out_shape=(
            local(blocks, seq, width),
            local(seq, width, dtype=F32),
            local(seq, width),
            local(seq, width),
            local(blocks, width, dtype=F32),
            local(8, width, dtype=F32),
        ),
        in_specs=[VM] * 9,
        out_specs=[VM] * 6,
        compiler_params=limit(16),
        cost_estimate=FREE,
        name="middle_backward",
    )(*stay(low, ssg, slope, norm, rstd, vec, wa, wi, wu))


def input_grad_body(g_ref, fsg_ref, w_ref, out_ref, token_ref):
    seq, width = fsg_ref.shape
    token_ref[...] = jnp.zeros_like(token_ref)
    tile = min(512, seq)

    def rows_step(r, carry):
        rows = aligned(r * tile, tile)
        total = fsg_ref[rows, :]
        for n in range(3):
            total = total + dot_nt(g_ref[n, rows, :], w_ref[n])
        out_ref[rows, :] = total
        return carry

    lax.fori_loop(0, seq // tile, rows_step, 0)


def input_grad(g, fsg, wa):
    seq, width = fsg.shape
    return pl.pallas_call(
        input_grad_body,
        out_shape=(shape(seq, width, dtype=F32), local(8, 128, dtype=F32)),
        in_specs=[VM] * 3,
        out_specs=[VM] * 2,
        compiler_params=limit(12),
        cost_estimate=FREE,
        name="input_grad",
    )(*stay(g, fsg, wa))


Z_ORDER = (0, 2, 1, 3)


def weight_grad_body(kind, order, z_order, me_ref, left_ref, g_ref, *refs):
    sums, refs = (refs[:4], refs[4:]) if kind == "attend" else ((), refs)
    outs, left = refs[:2], refs[2]
    i, z, c = me_ref[0], me_ref[1], me_ref[2]
    part = 96
    if kind == "attend":
        extra = refs[3]
        one, two, three, ib = (r[...] for r in sums)
        row = lax.broadcasted_iota(jnp.int32, one.shape, 0)
        every = jnp.where(row < 2, three, jnp.where(row < 5, two, one))
        for f in range(8):
            extra[f] = jnp.zeros_like(extra[f])
            extra[f, :, :part] = every[:, f * part : (f + 1) * part]
            extra[f, 0:1, 128 : 128 + 4 * part] = ib[f // 2 : f // 2 + 1, f % 2 * 4 * part : (f % 2 + 1) * 4 * part]

    def block_step(spot, carry):
        block = i ^ pick(order, spot)
        for side, c_at in enumerate((1 - c, c)):
            for n, j in enumerate(z_order):
                f_at = 2 * (z ^ j) + c_at
                if kind == "outer":
                    rows = left_ref[aligned_rows(f_at * 384 + block * 96, 96), :]
                elif kind == "inner":
                    rows = left_ref[aligned_rows(f_at * 96, 96), :]
                else:
                    rows = left_ref[block // 3, aligned_rows(f_at * 96, 96), :]
                left[side * 384 + n * 96 : side * 384 + (n + 1) * 96, :] = rows
        right = g_ref[...] if kind == "outer" else g_ref[block]
        grads = dot_nn(left[...], right).reshape(2, 4, 96, 768).astype(BF16)
        for side, c_at in enumerate((1 - c, c)):
            outs[side][spot, :, :96, :] = grads[side]
            if kind == "attend":
                for n, j in enumerate(z_order):
                    outs[side][spot, n, 96:104, :] = extra[2 * (z ^ j) + c_at].astype(BF16)
        return carry

    lax.fori_loop(0, 4, block_step, 0, unroll=True)


def weight_grad(kind, order, z_order, me, left, g, sums=()):
    rows = 104 if kind == "attend" else 96
    return pl.pallas_call(
        functools.partial(weight_grad_body, kind, order, z_order),
        out_shape=(local(4, 4, rows, 768),) * 2,
        in_specs=[SM] + [VM] * (2 + len(sums)),
        out_specs=[VM] * 2,
        scratch_shapes=[pltpu.VMEM((768, left.shape[-1]), BF16)] + [pltpu.VMEM((8, 8, 768), F32)] * (kind == "attend"),
        compiler_params=limit(6),
        cost_estimate=FREE,
        name=f"weight_grad_{kind}",
    )(me, *stay(left, g, *sums))


def prepare_body(me_ref, *refs):
    vectors, weights = refs[:9], refs[9:15]
    first_ref, second_ref, pack_ref, *rows, sems = refs[15:]
    i = me_ref[0]
    part = vectors[0].shape[0]
    copies = [
        pltpu.make_async_copy(
            weights[4].at[:, pl.ds(pl.multiple_of(i * 768, 768), 768)], second_ref.at[pl.ds(0, 96), :], sems.at[0]
        ),
        pltpu.make_async_copy(weights[5].at[aligned_rows(i * 96, 96), :], second_ref.at[pl.ds(96, 96), :], sems.at[1]),
    ]
    for n in range(9):
        copies.append(pltpu.make_async_copy(vectors[n], rows[n], sems.at[3 + n]))
    for n in range(4):

        @pl.when(i == n)
        def _():
            pltpu.make_async_copy(weights[n], first_ref.at[pl.ds(0, 96), :], sems.at[2]).start()

    start_all(copies)
    pack_ref[...] = jnp.zeros_like(pack_ref)
    wait_all(copies[2:])
    for n in range(8):
        pack_ref[n : n + 1, :part] = rows[n][...].astype(F32).reshape(1, part)
    pack_ref[0:1, 128 : 128 + 4 * part] = rows[8][...].astype(F32).reshape(1, 4 * part)
    first_ref[96:104, :] = pack_ref[...].astype(BF16)
    pltpu.make_async_copy(weights[0], first_ref.at[pl.ds(0, 96), :], sems.at[2]).wait()
    wait_all(copies[:2])


def prepare(me, vectors, weights):
    return pl.pallas_call(
        prepare_body,
        out_shape=(local(104, 768), local(192, 768)),
        in_specs=[SM] + [HB] * 15,
        out_specs=[VM] * 2,
        scratch_shapes=[pltpu.VMEM((8, 768), F32)]
        + [pltpu.VMEM(v.shape, BF16) for v in vectors]
        + [pltpu.SemaphoreType.DMA((12,))],
        compiler_params=limit(2),
        cost_estimate=FREE,
        name="prepare",
    )(me, *far_off(*vectors, *weights))


def after(value, *others, cost=FREE):
    def body(*refs):
        pass

    return pl.pallas_call(
        body,
        out_shape=jax.ShapeDtypeStruct(value.shape, value.dtype),
        in_specs=[HB] * (1 + len(others)),
        out_specs=HB,
        input_output_aliases={0: 0},
        compiler_params=limit(1),
        cost_estimate=cost,
        name="after",
    )(value, *others)


def swap(value, axis, size, mask):
    return lax.ppermute(value, axis, [(n, n ^ mask) for n in range(size)])


def gather_z(piece, fsdp):
    return [swap(piece, "fsdp", fsdp, 2 * j) for j in (1, 2, 3)]


def combine(*outs, cost=FREE):
    arrays = []
    for _, parts in outs:
        for _, terms in parts:
            arrays += [a for a, _ in terms if not any(a is b for b in arrays)]

    def find(array):
        return next(n for n, b in enumerate(arrays) if b is array)

    def body(*refs):
        for out_ref, (lead, parts) in zip(refs[len(arrays) :], outs, strict=True):

            def tile(index):
                start = 0
                for rows, terms in parts:
                    found = [(find(array), at(*index)) for array, at in terms]
                    values = [refs[n][spot] for n, spot in found if spot is not None]
                    value = values[0] if len(values) == 1 else sum(v.astype(F32) for v in values).astype(BF16)
                    out_ref[(*index, slice(start, start + rows), slice(None))] = value
                    start += rows

            def step(front, last, carry):
                tile((*front, last))
                return carry

            if not lead:
                tile(())
            elif len(lead) == 1:
                lax.fori_loop(0, lead[0], functools.partial(step, ()), 0)
            else:
                for front in range(lead[0]):
                    lax.fori_loop(0, lead[1], functools.partial(step, (front,)), 0)

    return pl.pallas_call(
        body,
        out_shape=tuple(local(*lead, sum(rows for rows, _ in parts), 768) for lead, parts in outs),
        in_specs=[VM] * len(arrays),
        out_specs=[VM] * len(outs),
        compiler_params=limit(2),
        cost_estimate=cost,
        name="combine",
    )(*stay(*arrays))


def stack_three(parts):
    rows = parts[0].shape[0]

    def body(*refs):
        for n in range(3):
            refs[3][n] = refs[n][...]

    return pl.pallas_call(
        body,
        out_shape=local(3, rows, 768),
        in_specs=[VM] * 3,
        out_specs=VM,
        compiler_params=limit(2),
        cost_estimate=FREE,
        name="stack_three",
    )(*stay(*parts))


def rows_of(value, start, rows):
    (part,) = combine(((value.shape[0],), [(rows, [(value, lambda n: (n, slice(start, start + rows)))])]))
    return part


UPPER = slice(0, 48)


def held(pair, block, rows):
    return [(v, lambda b: (block, b, rows)) for v in pair]


def first_pair(pair, total):
    def out(blocks, rows, size):
        terms = []
        for n, block in enumerate(blocks):
            for array, at in held(pair, block, rows):
                terms.append((array, lambda a, b, n=n, at=at: at(b) if a == n else None))
        return (2, 4), [(size, terms)]

    return combine(out((1, 3), UPPER, 48), out((2, 3), slice(48, total), total - 48))


def second_pair(pair, over_x, over_y, total, cost=FREE):
    x = held(pair, 2, UPPER) + [(over_x, lambda b: (1, b))]
    y = held(pair, 1, slice(48, total)) + [(over_y, lambda b: (1, b))]
    return combine(((4,), [(48, x)]), ((4,), [(total - 48, y)]), cost=cost)


def last_terms(pair, overs, onwards, total, tile):
    parts = []
    for rows, size, over, onward in (
        (UPPER, 48, overs[0], onwards[0]),
        (slice(48, total), total - 48, overs[1], onwards[1]),
    ):
        terms = [(array, lambda *n, at=at: at(tile(*n))) for array, at in held(pair, 0, rows)]
        terms += [(over, lambda *n: (0, tile(*n))), (onward, lambda *n: (tile(*n),))]
        parts.append((size, terms))
    return parts


def last_pair(pair, overs, onwards, cost=FREE):
    return combine(*[((2,), last_terms(pair, overs, onwards, 96, lambda b, k=k: k + b)) for k in (0, 2)], cost=cost)


def finish(terms):
    def body(*refs):
        terms, (own_ref, small_ref) = refs[:-2], refs[-2:]
        value = sum(r[...].astype(F32) for r in terms)
        own_ref[...] = value[:96].astype(BF16)
        small_ref[...] = value[96:]

    return pl.pallas_call(
        body,
        out_shape=(local(96, 768), local(8, 768, dtype=F32)),
        in_specs=[VM] * len(terms),
        out_specs=[VM] * 2,
        compiler_params=limit(2),
        cost_estimate=FREE,
        name="finish",
    )(*stay(*terms))


def spread(value, dp):
    return (value,) + tuple(swap(value, "dp", dp, m) for m in (1, 2, 3))


def pick(pieces, index):
    return jnp.where(index == 0, pieces[0], jnp.where(index == 1, pieces[1], jnp.where(index == 2, pieces[2], pieces[3])))


def in_order(pieces, i):
    return [pick(pieces, n ^ i) for n in range(4)]


def on_device(
    sizes,
    tokens,
    lengths,
    cotangent,
    query_weight,
    query_bias,
    key_weight,
    value_weight,
    value_bias,
    output_weight,
    output_bias,
    first_gain,
    first_shift,
    inner_weight,
    inner_bias,
    outer_weight,
    outer_bias,
    second_gain,
    second_shift,
):
    dp, fsdp = sizes
    docs, seq, width = tokens.shape
    blocks = inner_weight.shape[1] // width
    direct = dp == 4 and fsdp == 8 and docs == 1 and query_weight.shape == (96, 768) and blocks == 4
    i = lax.axis_index("dp")
    f = lax.axis_index("fsdp")
    me = jnp.stack([i, f // 2, f % 2, jnp.zeros_like(i)]).astype(jnp.int32)

    small = (query_bias, value_bias, output_bias, first_gain, first_shift, outer_bias, second_gain, second_shift, inner_bias)
    part = query_bias.shape[0]

    if direct:
        mine = (query_weight, key_weight, value_weight, output_weight)
        piece_a, piece_m = prepare(me, small, mine + (inner_weight, outer_weight))
        z_a = gather_z(piece_a, fsdp)
        z_m = gather_z(piece_m, fsdp)
        mine_a = stack_three(z_a)
        plane_a = (swap(mine_a, "dp", dp, 1), swap(mine_a, "dp", dp, 2))
        parts_a = (rows_of(plane_a[0], 0, 48), rows_of(plane_a[1], 48, 48))
        rest_a = (swap(parts_a[0], "dp", dp, 2), swap(parts_a[1], "dp", dp, 1))
        z_m[0] = after(z_m[0], *rest_a)
        mine_m = stack_three(z_m)
        inner_m, outer_m = rows_of(mine_m, 0, 96), rows_of(mine_m, 96, 96)
        over_x = [swap(inner_m, "dp", dp, 1), None]
        over_y = [None, swap(outer_m, "dp", dp, 2)]
        over_x[1], over_y[0] = swap(outer_m, "dp", dp, 1), swap(inner_m, "dp", dp, 2)
        near_a = bundle(1, mine, ((((0, 0)),),) * 4, (after(mine_a, mine_m),) + plane_a + (piece_a,))
        far_a = (swap(near_a, "fsdp", fsdp, 1),) + tuple(swap(v, "fsdp", fsdp, 1) for v in rest_a)

        def far_at(base, row=0):
            return [[(base + n, 0, row, 96, 0)] for n in range(3)]

        group_a = Pieces(
            mine,
            (mine_a,) + plane_a + rest_a + far_a + (piece_a,),
            [(n, 0, 0) for n in range(4)],
            [(5, n) for n in range(4)],
            far_at(0) + [[(3, 0, 0, 48, 0), (4, 0, 0, 48, 48)]],
            [[(5, 4 + 3 * n, 0, 96, 0)] for n in range(3)] + [[(6, 0, 0, 48, 0), (7, 0, 0, 48, 48)]],
            True,
            (8, 0, 5),
        )
        x = tokens.reshape(seq, width)
        q, k, v, att, left_a, lse, wa, vec, ib = attend_forward(group_a, fsdp, blocks, me, lengths, after(x, mine_m))
        over_x[0], over_y[1] = after(over_x[0], att), after(over_y[1], att)
        rest_m = (swap(over_x[0], "dp", dp, 2), swap(over_y[1], "dp", dp, 1))
        spots = (tuple((0, 768 * n) for n in range(4)), tuple((96 * n, 0) for n in range(4)))
        planes = ((inner_m, outer_m), over_x, over_y)
        near_m = bundle(2, (inner_weight, outer_weight), spots, tuple(v for plane in planes for v in plane))
        far_m = swap(near_m, "fsdp", fsdp, 1)
        rest_m = [after(v, near_m, cost=LONG) for v in rest_m]
        far_rest = [swap(v, "fsdp", fsdp, 1) for v in rest_m]
        far_m = after(far_m, *rest_m)
        four = range(4)
        early_i = Pieces(
            (inner_weight,),
            (inner_m, over_x[0], over_y[0], far_m),
            [(0, 0, 768 * n) for n in four],
            [(3, n) for n in four],
            far_at(0),
            [[(3, 8 + 6 * n, 0, 96, 0)] for n in range(3)],
            True,
        )
        early_u = Pieces(
            (outer_weight,),
            (outer_m, over_x[1], over_y[1], far_m),
            [(0, 96 * n, 0) for n in four],
            [(3, 4 + n) for n in four],
            far_at(0),
            [[(3, 11 + 6 * n, 0, 96, 0)] for n in range(3)],
            False,
        )
        none = [None] * 3
        late_i = Pieces((), (rest_m[0], far_rest[0]), (), (), none + [[(0, 0, 0, 96, 0)]], none + [[(1, 0, 0, 96, 0)]], True)
        late_u = Pieces((), (rest_m[1], far_rest[1]), (), (), none + [[(0, 0, 0, 96, 0)]], none + [[(1, 0, 0, 96, 0)]], False)
        wi = fill(early_i, me, blocks, width, width)
        wu = fill(early_u, me, blocks * width, width)
        late_i.arrays = (rest_m[0], after(far_rest[0], wi, wu))
        wi = fill(late_i, me, blocks, width, width, before=wi)
        wu = fill(late_u, me, blocks * width, width, before=wu)
    else:
        whole = tuple(
            lax.all_gather(w, "fsdp", axis=0, tiled=True)
            for w in (query_weight, key_weight, value_weight, output_weight, inner_weight, outer_weight)
        )
        packs = jnp.pad(jnp.stack(small[:8]), ((0, 0), (0, width - part)))
        packs = packs + jnp.pad(inner_bias[None], ((0, 7), (128, width - 128 - 4 * part)))
        packs = lax.all_gather(packs, "fsdp", axis=0, tiled=False)
        group_a = Whole(whole[:4], (packs,), [(n, 0, 0) for n in range(4)], True)
        group_i = Whole(whole[4:5], (), [(0, 0, width * n) for n in range(blocks)], True)
        group_u = Whole(whole[5:6], (), [(0, width * n, 0) for n in range(blocks)], False)
        x = tokens.reshape(seq, width)
        q, k, v, att, left_a, lse, wa, vec, ib = attend_forward(group_a, fsdp, blocks, me, lengths, x)
        wi = fill(group_i, me, blocks, width, width)
        wu = fill(group_u, me, blocks * width, width)

    cot = cotangent.reshape(seq, width)
    out, ssg, low, act_t, slope, norm, rstd, hid_t, sum_one = middle_forward(lengths, x, att, cot, vec, ib, wa, wi, wu)
    pairs = width // 128
    attend = functools.partial(attend_backward, length=lengths, q=q, k=k, v=v, lse=lse)
    if direct:
        sent_u, kept_u = weight_grad("outer", (0, 1, 2, 3), Z_ORDER, me, act_t, low)
        got_u = swap(sent_u, "fsdp", fsdp, 1)
        low = after(low, sent_u)
    igl, fsg, branch, att_g, ib_sum, sum_two = middle_backward(low, ssg, slope, norm, rstd, vec, wa, wi, wu)
    if direct:
        pair_u = (kept_u, after(got_u, igl))
        first_u = first_pair(pair_u, 96)
        over_u = [swap(first_u[0], "dp", dp, 1), swap(first_u[1], "dp", dp, 2)]
        igl = after(igl, *first_u)
        sent_i, kept_i = weight_grad("inner", (0, 1, 2, 3), Z_ORDER, me, hid_t, igl)
        got_i = swap(sent_i, "fsdp", fsdp, 1)
        third = pairs // 3
        part_one = attend(0, third, do=after(att_g, sent_i), branch=branch)
        pair_i = (kept_i, after(got_i, part_one[0]))
        first_i = first_pair(pair_i, 96)
        over_i = [swap(first_i[0], "dp", dp, 1), swap(first_i[1], "dp", dp, 2)]
        g, sum_three = attend(third, pairs, do=after(att_g, *first_i), branch=branch, before=part_one)
    else:
        g, sum_three = attend(0, pairs, do=att_g, branch=branch)
        in_grad, _ = input_grad(g, fsg, wa)

    if direct:
        here = lambda: ()
        sent_a, kept_a = weight_grad(
            "attend", (0, 1, 2, 3), (0, 1, 2, 3), me, left_a, g, (sum_one, sum_two, sum_three, ib_sum)
        )
        over_u = [after(v, kept_a) for v in over_u]
        second_u = second_pair(pair_u, *over_u, 96)
        onward_u = [swap(second_u[0], "dp", dp, 2), swap(second_u[1], "dp", dp, 1)]

        in_grad, token = input_grad(g, after(fsg, *second_u), wa)
        over_i = [after(v, token) for v in over_i]
        second_i = second_pair(pair_i, *over_i, 96, LONG)
        onward_i = [swap(second_i[0], "dp", dp, 2), swap(second_i[1], "dp", dp, 1)]

        got_a = swap(sent_a, "fsdp", fsdp, 1)
        pair_a = (kept_a, after(got_a, *second_i))
        first_a = first_pair(pair_a, 104)
        over_a = [swap(first_a[0], "dp", dp, 1), swap(first_a[1], "dp", dp, 2)]

        onward_u = [after(v, *first_a) for v in onward_u]
        keep_u, send_u = last_pair(pair_u, over_u, onward_u)
        near_u = swap(send_u, "fsdp", fsdp, 2)

        onward_i = [after(v, keep_u) for v in onward_i]
        keep_i, send_i = last_pair(pair_i, over_i, onward_i, LONG)
        near_i = swap(send_i, "fsdp", fsdp, 2)

        near_u = after(near_u, keep_i)
        (next_u,) = combine(((), [(96, [(keep_u, lambda: (1,)), (near_u, lambda: (1,))])]))
        last_u = swap(next_u, "fsdp", fsdp, 4)

        over_a = [after(v, next_u) for v in over_a]
        second_a = second_pair(pair_a, *over_a, 104)
        onward_a = [swap(second_a[0], "dp", dp, 2), swap(second_a[1], "dp", dp, 1)]

        near_i = after(near_i, *second_a)
        (next_i,) = combine(((), [(96, [(keep_i, lambda: (1,)), (near_i, lambda: (1,))])]), cost=LONG)
        last_i = swap(next_i, "fsdp", fsdp, 4)

        last_u = after(last_u, next_i)
        terms_u = [(keep_u, lambda: (0,)), (near_u, lambda: (0,)), (last_u, here)]
        (own_u,) = combine(((), [(96, terms_u)]))

        last_i = after(last_i, own_u)
        terms_i = [(keep_i, lambda: (0,)), (near_i, lambda: (0,)), (last_i, here)]
        (own_i,) = combine(((), [(96, terms_i)]))

        onward_a = [after(v, own_i) for v in onward_a]
        whole_a = combine(*[((), last_terms(pair_a, over_a, onward_a, 104, lambda j=j: j)) for j in range(4)])
        far_a = [swap(whole_a[j], "fsdp", fsdp, 2 * j) for j in (1, 2, 3)]

        (own_m,) = combine(((), [(96, [(after(own_i, whole_a[0]), here)]), (96, [(own_u, here)])]))
        every = spread(own_m, dp)

        far_a[0] = after(far_a[0], own_m)
        own_a, small_own = finish((whole_a[0], *far_a))
        all_a = spread(own_a, dp)
        small_grads = [small_own[n, :part] for n in range(8)] + [small_own[0, 128 : 128 + blocks * part]]
        all_i, all_u = [v[:96] for v in every], [v[96:] for v in every]
        q_g, k_g, v_g, o_g = (w.astype(F32) for w in in_order(all_a, i))
        i_g = jnp.concatenate(in_order(all_i, i), axis=1).astype(F32)
        u_g = jnp.concatenate(in_order(all_u, i), axis=0).astype(F32)
    else:
        vec_sum = jnp.concatenate([sum_three[:2], sum_two[2:5], sum_one[5:8]])
        vec_sum = vec_sum.reshape(8, fsdp, part).transpose(1, 0, 2).reshape(fsdp, 8 * part)
        ib_part = ib_sum.reshape(fsdp, blocks * part)
        small_sum = lax.psum(jnp.concatenate([vec_sum, ib_part], axis=1), ("dp", "fsdp"))
        small_own = lax.dynamic_index_in_dim(small_sum, f, 0, keepdims=False)
        small_grads = [small_own[n * part : (n + 1) * part] for n in range(8)] + [small_own[8 * part :]]
        x_t, att_t = left_a[0], left_a[1]
        locals_ = (
            dot_nn(x_t, g[0]),
            dot_nn(x_t, g[1]),
            dot_nn(x_t, g[2]),
            dot_nn(att_t, g[3]),
            jnp.concatenate([dot_nn(hid_t, igl[n]) for n in range(blocks)], axis=1),
            dot_nn(act_t, low),
        )
        owned = [lax.psum_scatter(w, "fsdp", scatter_dimension=0, tiled=True) for w in locals_]
        q_g, k_g, v_g, o_g, i_g, u_g = (lax.psum(w.astype(BF16), "dp").astype(F32) for w in owned)

    qb, vb, ob, g1, s1, ub, g2, s2, ibg = small_grads
    return (
        out.reshape(docs, seq, width),
        in_grad.reshape(docs, seq, width),
        q_g,
        qb,
        k_g,
        v_g,
        vb,
        o_g,
        ob,
        g1,
        s1,
        i_g,
        ibg,
        u_g,
        ub,
        g2,
        s2,
    )


def solution(mesh):
    rows, row = P("fsdp", None), P("fsdp")
    docs = P(("dp", "fsdp"), None, None)
    in_specs = (docs, P(("dp", "fsdp")), docs, rows, row, rows, rows, row, rows, row, row, row, rows, row, rows, row, row, row)
    out_specs = (docs, docs, rows, row, rows, rows, row, rows, row, row, row, rows, row, rows, row, row, row)
    sizes = (mesh.shape["dp"], mesh.shape["fsdp"])
    return jax.shard_map(
        functools.partial(on_device, sizes), mesh=mesh, in_specs=in_specs, out_specs=out_specs, check_vma=False
    )
```

```python
import functools
import math

import jax
import jax.numpy as jnp
from jax import lax
from jax.experimental import pallas as pl
from jax.experimental.pallas import tpu as pltpu
from jax.sharding import PartitionSpec as P

F32 = jnp.float32
BF16 = jnp.bfloat16
HD = 64
MASKED = -1e30
SCALE = HD ** -0.5
EPSILON = 1e-12
ROOT_HALF = math.sqrt(0.5)
INV_ROOT_TWO_PI = 1.0 / math.sqrt(2.0 * math.pi)

VM = pl.BlockSpec(memory_space=pltpu.VMEM)
SM = pl.BlockSpec(memory_space=pltpu.SMEM)
HB = pl.BlockSpec(memory_space=pl.ANY)
FREE = pl.CostEstimate(flops=0, bytes_accessed=0, transcendentals=0)

LONG = pl.CostEstimate(flops=60_000_000_000, bytes_accessed=0, transcendentals=0)


def shape(*dims, dtype=BF16):
    return jax.ShapeDtypeStruct(dims, dtype)


def local(*dims, dtype=BF16):
    return pltpu.VMEM(dims, dtype)


def stay(*values):
    return tuple(pltpu.with_memory_space_constraint(v, pltpu.VMEM) for v in values)


def far_off(*values):
    return tuple(pltpu.with_memory_space_constraint(v, pltpu.HBM) for v in values)


def limit(mebibytes):
    return pltpu.CompilerParams(vmem_limit_bytes=mebibytes << 20)


def dot_nn(a, b):
    return lax.dot_general(a, b, (((1,), (0,)), ((), ())), preferred_element_type=F32)


def dot_nt(a, b):
    return lax.dot_general(a, b, (((1,), (1,)), ((), ())), preferred_element_type=F32)


def flip(value):
    return value.T


def column_sum(value):
    return jnp.sum(value.astype(F32), axis=0, keepdims=True)


def row_mean(value):
    return jnp.mean(value, axis=-1, keepdims=True)


def aligned(start, size):
    return pl.ds(pl.multiple_of(start, size), size)


class Pieces:
    def __init__(self, held, arrays, own, sibling, far, far_sibling, stacked, packs=()):
        self.held, self.arrays, self.own, self.sibling, self.packs = held, arrays, own, sibling, packs
        self.far, self.far_sibling, self.stacked = far, far_sibling, stacked

    def count(self):
        return len(self.own)

    def place(self, target, block, z_at, c_at, offset, rows):
        if self.stacked:
            return target.at[block, aligned_rows((2 * z_at + c_at) * 96 + offset, rows), :]
        return target.at[aligned_rows((2 * z_at + c_at) * 384 + block * 96 + offset, rows), :]

    def copies(self, held, me_ref, target, sems, base):
        z, c = me_ref[1], me_ref[2]
        done = []
        for block, (position, row, lane) in enumerate(self.own):
            where = self.place(target, block, z, c, 0, 96)
            source = held[position].at[pl.ds(row, 96), pl.ds(lane, 768)]
            done.append(pltpu.make_async_copy(source, where, sems.at[base + block]))
        return done

    def fill(self, refs, me_ref, target, rest=(0, 1, 2, 3)):
        i, z, c = me_ref[0], me_ref[1], me_ref[2]
        for block, (position, tile) in enumerate(self.sibling if 0 in rest else ()):
            self.place(target, block, z, 1 - c, 0, 96)[...] = refs[position][tile]
        for c_at, far in ((c, self.far), (1 - c, self.far_sibling)):
            for away in rest:
                parts = far[away]
                for position, tile, row, rows, offset in parts:

                    def copy(j, carry, position=position, tile=tile, row=row, rows=rows, offset=offset, away=away, c_at=c_at):
                        where = self.place(target, i ^ away, z ^ j, c_at, offset, rows)
                        where[...] = refs[position][tile + j - 1, row : row + rows, :]
                        return carry

                    lax.fori_loop(1, 4, copy, 0)

    def vectors(self, refs, me_ref, target):
        z, c = me_ref[1], me_ref[2]
        own, mine, other = (refs[n] for n in self.packs)
        for j in range(4):
            target[2 * (z ^ j) + c] = (mine[j - 1, 96:104, :] if j else own[96:104, :]).astype(F32)
            target[2 * (z ^ j) + 1 - c] = other[13, 8 * j : 8 * j + 8, :].astype(F32)


def bundle_body(group_count, held, me_ref, *refs):
    sources, near = refs[: len(held)], refs[len(held) : -2]
    out_ref, sems = refs[-2:]
    own = [(n, row, lane) for n, spots in enumerate(held) for row, lane in spots]
    loads = []
    for tile, (n, row, lane) in enumerate(own):
        source = sources[n].at[pl.ds(row, 96), pl.ds(lane, 768)]
        loads.append(pltpu.make_async_copy(source, out_ref.at[tile], sems.at[tile]))
    start_all(loads)
    tile = len(own)
    for away in range(3):
        for group in range(group_count):
            for j in range(3):
                out_ref[tile] = near[away * group_count + group][j, :96, :]
                tile += 1
    if group_count == 1:
        out_ref[tile, 0:8, :] = near[3][96:104, :]
        for j in range(3):
            out_ref[tile, 8 * j + 8 : 8 * j + 16, :] = near[0][j, 96:104, :]
        out_ref[tile, 32:, :] = jnp.zeros((64, 768), BF16)
    wait_all(loads)


def bundle(group_count, sources, held, near):
    own = sum(len(spots) for spots in held)
    tiles = own + 9 * group_count + (group_count == 1)
    return pl.pallas_call(
        functools.partial(bundle_body, group_count, held),
        out_shape=local(tiles, 96, 768),
        in_specs=[SM] + [HB] * len(sources) + [VM] * len(near),
        out_specs=VM,
        scratch_shapes=[pltpu.SemaphoreType.DMA((own,))],
        compiler_params=limit(2),
        cost_estimate=FREE,
        name="bundle",
    )(jnp.zeros((1,), jnp.int32), *far_off(*sources), *stay(*near))


def aligned_rows(start, rows):
    return pl.ds(pl.multiple_of(start, 16), rows)


class Whole:
    def __init__(self, held, arrays, spots, stacked):
        self.held, self.arrays, self.spots, self.stacked = held, arrays, spots, stacked

    def count(self):
        return len(self.spots)

    def copies(self, held, me_ref, target, sems, base):
        done = []
        for block, (position, row, lane) in enumerate(self.spots):
            where = target.at[block] if self.stacked else target.at[pl.ds(block * 768, 768), :]
            source = held[position].at[pl.ds(row, 768), pl.ds(lane, 768)]
            done.append(pltpu.make_async_copy(source, where, sems.at[base + block]))
        return done

    def fill(self, refs, me_ref, target, rest=()):
        pass

    def vectors(self, refs, me_ref, target):
        target[...] = refs[0][...].astype(F32)


def start_all(copies):
    for copy in copies:
        copy.start()


def wait_all(copies):
    for copy in copies:
        copy.wait()


def pair_masks(dims, axis):
    spot = lax.broadcasted_iota(jnp.int32, dims, axis)
    return spot < HD, spot >= HD


def keep(mask, value):
    return jnp.where(mask, value, jnp.zeros_like(value))


def attend_forward_body(group, part, me_ref, len_ref, x_ref, *refs):
    held, refs = refs[: len(group.held)], refs[len(group.held) :]
    sources = refs[: len(group.arrays)]
    q_ref, k_ref, v_ref, att_ref, left_ref, lse_ref, w_ref, vec_ref, ib_ref, packed, sems = refs[len(group.arrays) :]
    seq, width = x_ref.shape
    tile = min(512, seq)
    loads = group.copies(held, me_ref, w_ref, sems, 0)
    start_all(loads)
    group.fill(sources, me_ref, w_ref)
    group.vectors(sources, me_ref, packed)
    for f in range(packed.shape[0]):
        pack = packed[f]
        vec_ref[:, f * part : (f + 1) * part] = pack[:, :part]
        row, lane = divmod(f * 4 * part, width)
        ib_ref[row : row + 1, lane : lane + 4 * part] = pack[:1, 128 : 128 + 4 * part]
    for p in range(width // 128):
        left_ref[0, p * 128 : (p + 1) * 128, :] = flip(x_ref[:, p * 128 : (p + 1) * 128])
    wait_all(loads)

    def project(r, carry):
        rows = aligned(r * tile, tile)
        x = x_ref[rows, :]
        q_ref[rows, :] = (dot_nn(x, w_ref[0]) + vec_ref[0:1, :]).astype(BF16)
        k_ref[rows, :] = dot_nn(x, w_ref[1]).astype(BF16)
        v_ref[rows, :] = (dot_nn(x, w_ref[2]) + vec_ref[1:2, :]).astype(BF16)
        return carry

    lax.fori_loop(0, seq // tile, project, 0)
    length = len_ref[0]

    def pair(p, carry):
        lanes = aligned(p * 128, 128)
        k_pair = k_ref[:, lanes]
        q_t = (q_ref[:, lanes].astype(F32) * SCALE).T.astype(BF16)
        v_t = flip(v_ref[:, lanes])
        masks = pair_masks((128, seq), 0)
        allowed = lax.broadcasted_iota(jnp.int32, (seq, seq), 0) < length
        for e in range(2):
            s = dot_nn(k_pair, keep(masks[e], q_t))
            s = jnp.where(allowed, s, MASKED)
            top = jnp.max(s, axis=0, keepdims=True)
            p_t = jnp.exp(s - top)
            total = jnp.sum(p_t, axis=0, keepdims=True)
            o_t = dot_nn(v_t[e * HD : (e + 1) * HD, :], p_t.astype(BF16)) / total
            left_ref[1, aligned(p * 128 + e * HD, HD), :] = o_t.astype(BF16)
            lse_ref[pl.ds(p * 2 + e, 1), :] = top + jnp.log(total)
        att_ref[:, lanes] = flip(left_ref[1, aligned(p * 128, 128), :])
        return carry

    lax.fori_loop(0, width // 128, pair, 0, unroll=2)


def attend_forward(group, shards, blocks, me, length, x):
    seq, width = x.shape
    heads = width // HD
    return pl.pallas_call(
        functools.partial(attend_forward_body, group, width // shards),
        out_shape=(local(seq, width),) * 4
        + (local(2, width, seq), local(-(-heads // 8) * 8, seq, dtype=F32), local(4, width, width))
        + (local(8, width, dtype=F32), local(blocks, width, dtype=F32)),
        in_specs=[SM, SM, VM] + [HB] * len(group.held) + [VM] * len(group.arrays),
        out_specs=[VM] * 9,
        scratch_shapes=[pltpu.VMEM((shards, 8, width), F32), pltpu.SemaphoreType.DMA((group.count(),))],
        compiler_params=limit(10),
        cost_estimate=FREE,
        name="attend_forward",
    )(me, length, x, *far_off(*group.held), *stay(*group.arrays))


def attend_backward_body(first, last, len_ref, q_ref, k_ref, v_ref, do_ref, lse_ref, branch_ref, *refs):
    g_ref, sum_ref = refs[-2:]
    seq, width = q_ref.shape
    length = len_ref[0]

    def pair(p, carry):
        lanes = aligned(p * 128, 128)
        q_pair = (q_ref[:, lanes].astype(F32) * SCALE).astype(BF16)
        k_pair = k_ref[:, lanes]
        v_pair = v_ref[:, lanes]
        do_pair = do_ref[:, lanes]
        q_t = flip(q_pair)
        k_t = (k_pair.astype(F32) * SCALE).T.astype(BF16)
        do_t = flip(do_pair)
        sub_masks = pair_masks((128, seq), 0)
        lane_masks = pair_masks((seq, 128), 1)
        allowed = lax.broadcasted_iota(jnp.int32, (seq, seq), 0) < length
        dk = jnp.zeros((seq, 128), F32)
        dv = jnp.zeros((seq, 128), F32)
        dq_t = []
        for e in range(2):
            s = dot_nn(k_pair, keep(sub_masks[e], q_t))
            s = jnp.where(allowed, s, MASKED)
            p_t = jnp.exp(s - lse_ref[pl.ds(p * 2 + e, 1), :])
            dp = dot_nn(v_pair, keep(sub_masks[e], do_t))
            dv = dv + dot_nn(p_t.astype(BF16), keep(lane_masks[e], do_pair))
            t = p_t * dp
            row = jnp.sum(t, axis=0, keepdims=True)
            ds = (t - p_t * row).astype(BF16)
            dk = dk + dot_nn(ds, keep(lane_masks[e], q_pair))
            dq_t.append(dot_nn(k_t[e * HD : (e + 1) * HD, :], ds))
        dq = jnp.concatenate(dq_t, axis=0).T.astype(BF16)
        dv = dv.astype(BF16)
        g_ref[0, :, lanes] = dq
        g_ref[1, :, lanes] = dk.astype(BF16)
        g_ref[2, :, lanes] = dv
        g_ref[3, :, lanes] = branch_ref[:, lanes]
        sum_ref[0:1, lanes] = column_sum(dq)
        sum_ref[1:2, lanes] = column_sum(dv)
        return carry

    lax.fori_loop(first, last, pair, 0, unroll=2)


def attend_backward(first, last, length, q, k, v, do, lse, branch, before=()):
    seq, width = q.shape
    return pl.pallas_call(
        functools.partial(attend_backward_body, first, last),
        out_shape=(local(4, seq, width), local(8, width, dtype=F32)),
        in_specs=[SM] + [VM] * 6 + [HB] * len(before),
        out_specs=[VM] * 2,
        input_output_aliases={7 + n: n for n in range(len(before))},
        compiler_params=limit(10),
        cost_estimate=FREE,
        name="attend_backward",
    )(length, *stay(q, k, v, do, lse, branch, *before))


def gelu_parts(inner):
    cumulative = 0.5 * (1.0 + lax.erf(inner * ROOT_HALF))
    density = jnp.exp(-0.5 * inner * inner) * INV_ROOT_TWO_PI
    return inner * cumulative, cumulative + inner * density


def fill_body(group, early, me_ref, *refs):
    held, near = refs[: len(group.held)], refs[len(group.held) : len(group.held) + len(group.arrays)]
    if not early:
        group.fill(near, me_ref, refs[-1])
        return
    target, sems = refs[-2:]
    loads = group.copies(held, me_ref, target, sems, 0)
    start_all(loads)
    group.fill(near, me_ref, target)
    wait_all(loads)


def fill(group, me, *dims, before=None):
    early = before is None
    more = () if early else (before,)
    return pl.pallas_call(
        functools.partial(fill_body, group, early),
        out_shape=local(*dims),
        in_specs=[SM] + [HB] * len(group.held) + [VM] * len(group.arrays) + [HB] * len(more),
        out_specs=VM,
        scratch_shapes=[pltpu.SemaphoreType.DMA((group.count(),))] * early,
        input_output_aliases={} if early else {1 + len(group.held) + len(group.arrays): 0},
        compiler_params=limit(2),
        cost_estimate=FREE,
        name="fill",
    )(me, *far_off(*group.held), *stay(*group.arrays, *more))


def middle_forward_body(
    len_ref,
    x_ref,
    att_ref,
    cot_ref,
    vec_ref,
    ib_ref,
    wa,
    wi,
    wu,
    out_ref,
    ssg_ref,
    low_ref,
    actT_ref,
    slope_ref,
    norm_ref,
    rstd_ref,
    hidT_ref,
    sum_ref,
):
    seq, width = x_ref.shape
    blocks = wi.shape[0]
    tile = min(512, seq)
    length = len_ref[0]
    sum_ref[...] = jnp.zeros_like(sum_ref)

    def rows_step(r, carry):
        rows = aligned(r * tile, tile)
        first = x_ref[rows, :].astype(F32) + dot_nn(att_ref[rows, :], wa[3]) + vec_ref[2:3, :]
        center = first - row_mean(first)
        rstd = lax.rsqrt(row_mean(center * center) + EPSILON)
        normed = center * rstd
        norm_ref[rows, :] = normed
        rstd_ref[rows, :] = rstd
        hidden = normed * vec_ref[3:4, :] + vec_ref[4:5, :]
        low = hidden.astype(BF16)
        hidT_ref[:, rows] = low.astype(F32).T.astype(BF16)

        def block(f, second):
            inner = dot_nn(low, wi[f]) + ib_ref[pl.ds(f, 1), :]
            active, slope = gelu_parts(inner)
            active = active.astype(BF16)
            spot = aligned(f * width, width)
            slope_ref[rows, spot] = slope.astype(BF16)
            actT_ref[spot, rows] = flip(active)
            return second + dot_nn(active, wu[spot, :])

        second = lax.fori_loop(0, blocks, block, hidden + vec_ref[5:6, :], unroll=True)
        center = second - row_mean(second)
        rstd = lax.rsqrt(row_mean(center * center) + EPSILON)
        normed = center * rstd
        spot = r * tile + lax.broadcasted_iota(jnp.int32, (tile, width), 0)
        valid = spot < length
        result = normed * vec_ref[6:7, :] + vec_ref[7:8, :]
        out_ref[rows, :] = jnp.where(valid, result, 0.0).astype(BF16)
        grad = jnp.where(valid, cot_ref[rows, :].astype(F32), 0.0)
        sum_ref[7:8, :] += column_sum(grad)
        sum_ref[6:7, :] += column_sum(grad * normed)
        grad = grad * vec_ref[6:7, :]
        grad = rstd * (grad - row_mean(grad) - normed * row_mean(grad * normed))
        ssg_ref[rows, :] = grad
        low = grad.astype(BF16)
        low_ref[rows, :] = low
        sum_ref[5:6, :] += column_sum(low)
        return carry

    lax.fori_loop(0, seq // tile, rows_step, 0)


def middle_forward(length, x, att, cot, vec, ib, wa, wi, wu):
    seq, width = x.shape
    blocks = ib.shape[0]
    return pl.pallas_call(
        middle_forward_body,
        out_shape=(
            shape(seq, width),
            local(seq, width, dtype=F32),
            local(seq, width),
            local(blocks * width, seq),
            local(seq, blocks * width),
            local(seq, width, dtype=F32),
            local(seq, 1, dtype=F32),
            local(width, seq),
            local(8, width, dtype=F32),
        ),
        in_specs=[SM] + [VM] * 8,
        out_specs=[VM] * 9,
        compiler_params=limit(16),
        cost_estimate=FREE,
        name="middle_forward",
    )(length, x, *stay(att), cot, *stay(vec, ib, wa, wi, wu))


def middle_backward_body(
    low_ref, ssg_ref, slope_ref, norm_ref, rstd_ref, vec_ref, wa, wi, wu, igl_ref, fsg_ref, branch_ref, att_ref, ib_ref, sum_ref
):
    seq, width = low_ref.shape
    blocks = wi.shape[0]
    tile = min(512, seq)
    sum_ref[...] = jnp.zeros_like(sum_ref)
    ib_ref[...] = jnp.zeros_like(ib_ref)

    def rows_step(r, carry):
        rows = aligned(r * tile, tile)
        low = low_ref[rows, :]

        def block(f, grad):
            spot = aligned(f * width, width)
            inner = (dot_nt(low, wu[spot, :]) * slope_ref[rows, spot].astype(F32)).astype(BF16)
            igl_ref[f, rows, :] = inner
            ib_ref[pl.ds(f, 1), :] += column_sum(inner)
            return grad + dot_nt(inner, wi[f])

        grad = lax.fori_loop(0, blocks, block, ssg_ref[rows, :], unroll=True)
        normed = norm_ref[rows, :]
        sum_ref[4:5, :] += column_sum(grad)
        sum_ref[3:4, :] += column_sum(grad * normed)
        grad = grad * vec_ref[3:4, :]
        grad = rstd_ref[rows, :] * (grad - row_mean(grad) - normed * row_mean(grad * normed))
        fsg_ref[rows, :] = grad
        branch = grad.astype(BF16)
        branch_ref[rows, :] = branch
        sum_ref[2:3, :] += column_sum(branch)
        att_ref[rows, :] = dot_nt(branch, wa[3]).astype(BF16)
        return carry

    lax.fori_loop(0, seq // tile, rows_step, 0)


def middle_backward(low, ssg, slope, norm, rstd, vec, wa, wi, wu):
    seq, width = low.shape
    blocks = wi.shape[0]
    return pl.pallas_call(
        middle_backward_body,
        out_shape=(
            local(blocks, seq, width),
            local(seq, width, dtype=F32),
            local(seq, width),
            local(seq, width),
            local(blocks, width, dtype=F32),
            local(8, width, dtype=F32),
        ),
        in_specs=[VM] * 9,
        out_specs=[VM] * 6,
        compiler_params=limit(16),
        cost_estimate=FREE,
        name="middle_backward",
    )(*stay(low, ssg, slope, norm, rstd, vec, wa, wi, wu))


def input_grad_body(g_ref, fsg_ref, w_ref, out_ref, token_ref):
    seq, width = fsg_ref.shape
    token_ref[...] = jnp.zeros_like(token_ref)
    tile = min(512, seq)

    def rows_step(r, carry):
        rows = aligned(r * tile, tile)
        total = fsg_ref[rows, :]
        for n in range(3):
            total = total + dot_nt(g_ref[n, rows, :], w_ref[n])
        out_ref[rows, :] = total
        return carry

    lax.fori_loop(0, seq // tile, rows_step, 0)


def input_grad(g, fsg, wa):
    seq, width = fsg.shape
    return pl.pallas_call(
        input_grad_body,
        out_shape=(shape(seq, width, dtype=F32), local(8, 128, dtype=F32)),
        in_specs=[VM] * 3,
        out_specs=[VM] * 2,
        compiler_params=limit(12),
        cost_estimate=FREE,
        name="input_grad",
    )(*stay(g, fsg, wa))


Z_ORDER = (0, 2, 1, 3)


def weight_grad_body(kind, order, z_order, me_ref, left_ref, g_ref, *refs):
    sums, refs = (refs[:4], refs[4:]) if kind == "attend" else ((), refs)
    outs, left = refs[:2], refs[2]
    i, z, c = me_ref[0], me_ref[1], me_ref[2]
    part = 96
    if kind == "attend":
        extra = refs[3]
        one, two, three, ib = (r[...] for r in sums)
        row = lax.broadcasted_iota(jnp.int32, one.shape, 0)
        every = jnp.where(row < 2, three, jnp.where(row < 5, two, one))
        for f in range(8):
            extra[f] = jnp.zeros_like(extra[f])
            extra[f, :, :part] = every[:, f * part : (f + 1) * part]
            extra[f, 0:1, 128 : 128 + 4 * part] = ib[f // 2 : f // 2 + 1, f % 2 * 4 * part : (f % 2 + 1) * 4 * part]

    def block_step(spot, carry):
        block = i ^ pick(order, spot)
        for side, c_at in enumerate((1 - c, c)):
            for n, j in enumerate(z_order):
                f_at = 2 * (z ^ j) + c_at
                if kind == "outer":
                    rows = left_ref[aligned_rows(f_at * 384 + block * 96, 96), :]
                elif kind == "inner":
                    rows = left_ref[aligned_rows(f_at * 96, 96), :]
                else:
                    rows = left_ref[block // 3, aligned_rows(f_at * 96, 96), :]
                left[side * 384 + n * 96 : side * 384 + (n + 1) * 96, :] = rows
        right = g_ref[...] if kind == "outer" else g_ref[block]
        grads = dot_nn(left[...], right).reshape(2, 4, 96, 768).astype(BF16)
        for side, c_at in enumerate((1 - c, c)):
            outs[side][spot, :, :96, :] = grads[side]
            if kind == "attend":
                for n, j in enumerate(z_order):
                    outs[side][spot, n, 96:104, :] = extra[2 * (z ^ j) + c_at].astype(BF16)
        return carry

    lax.fori_loop(0, 4, block_step, 0, unroll=2)


def weight_grad(kind, order, z_order, me, left, g, sums=()):
    rows = 104 if kind == "attend" else 96
    return pl.pallas_call(
        functools.partial(weight_grad_body, kind, order, z_order),
        out_shape=(local(4, 4, rows, 768),) * 2,
        in_specs=[SM] + [VM] * (2 + len(sums)),
        out_specs=[VM] * 2,
        scratch_shapes=[pltpu.VMEM((768, left.shape[-1]), BF16)] + [pltpu.VMEM((8, 8, 768), F32)] * (kind == "attend"),
        compiler_params=limit(6),
        cost_estimate=FREE,
        name=f"weight_grad_{kind}",
    )(me, *stay(left, g, *sums))


def prepare_body(me_ref, *refs):
    vectors, weights = refs[:9], refs[9:15]
    first_ref, second_ref, pack_ref, *rows, sems = refs[15:]
    i = me_ref[0]
    part = vectors[0].shape[0]
    copies = [
        pltpu.make_async_copy(
            weights[4].at[:, pl.ds(pl.multiple_of(i * 768, 768), 768)], second_ref.at[pl.ds(0, 96), :], sems.at[0]
        ),
        pltpu.make_async_copy(weights[5].at[aligned_rows(i * 96, 96), :], second_ref.at[pl.ds(96, 96), :], sems.at[1]),
    ]
    for n in range(9):
        copies.append(pltpu.make_async_copy(vectors[n], rows[n], sems.at[3 + n]))
    for n in range(4):

        @pl.when(i == n)
        def _():
            pltpu.make_async_copy(weights[n], first_ref.at[pl.ds(0, 96), :], sems.at[2]).start()

    start_all(copies)
    pack_ref[...] = jnp.zeros_like(pack_ref)
    wait_all(copies[2:])
    for n in range(8):
        pack_ref[n : n + 1, :part] = rows[n][...].astype(F32).reshape(1, part)
    pack_ref[0:1, 128 : 128 + 4 * part] = rows[8][...].astype(F32).reshape(1, 4 * part)
    first_ref[96:104, :] = pack_ref[...].astype(BF16)
    pltpu.make_async_copy(weights[0], first_ref.at[pl.ds(0, 96), :], sems.at[2]).wait()
    wait_all(copies[:2])


def prepare(me, vectors, weights):
    return pl.pallas_call(
        prepare_body,
        out_shape=(local(104, 768), local(192, 768)),
        in_specs=[SM] + [HB] * 15,
        out_specs=[VM] * 2,
        scratch_shapes=[pltpu.VMEM((8, 768), F32)]
        + [pltpu.VMEM(v.shape, BF16) for v in vectors]
        + [pltpu.SemaphoreType.DMA((12,))],
        compiler_params=limit(2),
        cost_estimate=FREE,
        name="prepare",
    )(me, *far_off(*vectors, *weights))


def after(value, *others, cost=FREE):
    def body(*refs):
        pass

    return pl.pallas_call(
        body,
        out_shape=jax.ShapeDtypeStruct(value.shape, value.dtype),
        in_specs=[HB] * (1 + len(others)),
        out_specs=HB,
        input_output_aliases={0: 0},
        compiler_params=limit(1),
        cost_estimate=cost,
        name="after",
    )(value, *others)


def swap(value, axis, size, mask):
    return lax.ppermute(value, axis, [(n, n ^ mask) for n in range(size)])


def gather_z(piece, fsdp):
    return [swap(piece, "fsdp", fsdp, 2 * j) for j in (1, 2, 3)]


def combine(*outs, cost=FREE):
    arrays = []
    for _, parts in outs:
        for _, terms in parts:
            arrays += [a for a, _ in terms if not any(a is b for b in arrays)]

    def find(array):
        return next(n for n, b in enumerate(arrays) if b is array)

    def body(*refs):
        for out_ref, (lead, parts) in zip(refs[len(arrays) :], outs, strict=True):

            def tile(index):
                start = 0
                for rows, terms in parts:
                    found = [(find(array), at(*index)) for array, at in terms]
                    values = [refs[n][spot] for n, spot in found if spot is not None]
                    value = values[0] if len(values) == 1 else sum(v.astype(F32) for v in values).astype(BF16)
                    out_ref[(*index, slice(start, start + rows), slice(None))] = value
                    start += rows

            def step(front, last, carry):
                tile((*front, last))
                return carry

            if not lead:
                tile(())
            elif len(lead) == 1:
                lax.fori_loop(0, lead[0], functools.partial(step, ()), 0)
            else:
                for front in range(lead[0]):
                    lax.fori_loop(0, lead[1], functools.partial(step, (front,)), 0)

    return pl.pallas_call(
        body,
        out_shape=tuple(local(*lead, sum(rows for rows, _ in parts), 768) for lead, parts in outs),
        in_specs=[VM] * len(arrays),
        out_specs=[VM] * len(outs),
        compiler_params=limit(2),
        cost_estimate=cost,
        name="combine",
    )(*stay(*arrays))


def stack_three(parts):
    rows = parts[0].shape[0]

    def body(*refs):
        for n in range(3):
            refs[3][n] = refs[n][...]

    return pl.pallas_call(
        body,
        out_shape=local(3, rows, 768),
        in_specs=[VM] * 3,
        out_specs=VM,
        compiler_params=limit(2),
        cost_estimate=FREE,
        name="stack_three",
    )(*stay(*parts))


def rows_of(value, start, rows):
    (part,) = combine(((value.shape[0],), [(rows, [(value, lambda n: (n, slice(start, start + rows)))])]))
    return part


UPPER = slice(0, 48)


def held(pair, block, rows):
    return [(v, lambda b: (block, b, rows)) for v in pair]


def first_pair(pair, total):
    def out(blocks, rows, size):
        terms = []
        for n, block in enumerate(blocks):
            for array, at in held(pair, block, rows):
                terms.append((array, lambda a, b, n=n, at=at: at(b) if a == n else None))
        return (2, 4), [(size, terms)]

    return combine(out((1, 3), UPPER, 48), out((2, 3), slice(48, total), total - 48))


def second_pair(pair, over_x, over_y, total, cost=FREE):
    x = held(pair, 2, UPPER) + [(over_x, lambda b: (1, b))]
    y = held(pair, 1, slice(48, total)) + [(over_y, lambda b: (1, b))]
    return combine(((4,), [(48, x)]), ((4,), [(total - 48, y)]), cost=cost)


def last_terms(pair, overs, onwards, total, tile):
    parts = []
    for rows, size, over, onward in (
        (UPPER, 48, overs[0], onwards[0]),
        (slice(48, total), total - 48, overs[1], onwards[1]),
    ):
        terms = [(array, lambda *n, at=at: at(tile(*n))) for array, at in held(pair, 0, rows)]
        terms += [(over, lambda *n: (0, tile(*n))), (onward, lambda *n: (tile(*n),))]
        parts.append((size, terms))
    return parts


def last_pair(pair, overs, onwards, cost=FREE):
    return combine(*[((2,), last_terms(pair, overs, onwards, 96, lambda b, k=k: k + b)) for k in (0, 2)], cost=cost)


def finish(terms):
    def body(*refs):
        terms, (own_ref, small_ref) = refs[:-2], refs[-2:]
        value = sum(r[...].astype(F32) for r in terms)
        own_ref[...] = value[:96].astype(BF16)
        small_ref[...] = value[96:]

    return pl.pallas_call(
        body,
        out_shape=(local(96, 768), local(8, 768, dtype=F32)),
        in_specs=[VM] * len(terms),
        out_specs=[VM] * 2,
        compiler_params=limit(2),
        cost_estimate=FREE,
        name="finish",
    )(*stay(*terms))


def spread(value, dp):
    return (value,) + tuple(swap(value, "dp", dp, m) for m in (1, 2, 3))


def deliver_two(me, every):
    def body(me_ref, *refs):
        inner_ref, outer_ref = refs[4:]
        for away in range(4):
            block = me_ref[0] ^ away
            inner_ref[:, aligned(block * 768, 768)] = refs[away][:96, :].astype(F32)
            outer_ref[aligned(block * 96, 96), :] = refs[away][96:, :].astype(F32)

    return pl.pallas_call(
        body,
        out_shape=(shape(96, 3072, dtype=F32), shape(384, 768, dtype=F32)),
        in_specs=[SM] + [VM] * 4,
        out_specs=[VM] * 2,
        compiler_params=limit(6),
        cost_estimate=FREE,
        name="deliver_two",
    )(me, *stay(*every))


def deliver_four(me, every):
    def body(me_ref, *refs):
        outs, held_ref = refs[4:8], refs[8]
        for away in range(4):
            held_ref[me_ref[0] ^ away] = refs[away][...]
        for n in range(4):
            outs[n][...] = held_ref[n].astype(F32)

    return pl.pallas_call(
        body,
        out_shape=(shape(96, 768, dtype=F32),) * 4,
        in_specs=[SM] + [VM] * 4,
        out_specs=[VM] * 4,
        scratch_shapes=[pltpu.VMEM((4, 96, 768), BF16)],
        compiler_params=limit(4),
        cost_estimate=FREE,
        name="deliver_four",
    )(me, *stay(*every))


def pick(pieces, index):
    return jnp.where(index == 0, pieces[0], jnp.where(index == 1, pieces[1], jnp.where(index == 2, pieces[2], pieces[3])))


def on_device(
    sizes,
    tokens,
    lengths,
    cotangent,
    query_weight,
    query_bias,
    key_weight,
    value_weight,
    value_bias,
    output_weight,
    output_bias,
    first_gain,
    first_shift,
    inner_weight,
    inner_bias,
    outer_weight,
    outer_bias,
    second_gain,
    second_shift,
):
    dp, fsdp = sizes
    docs, seq, width = tokens.shape
    blocks = inner_weight.shape[1] // width
    direct = dp == 4 and fsdp == 8 and docs == 1 and query_weight.shape == (96, 768) and blocks == 4
    i = lax.axis_index("dp")
    f = lax.axis_index("fsdp")
    me = jnp.stack([i, f // 2, f % 2, jnp.zeros_like(i)]).astype(jnp.int32)

    small = (query_bias, value_bias, output_bias, first_gain, first_shift, outer_bias, second_gain, second_shift, inner_bias)
    part = query_bias.shape[0]

    if direct:
        mine = (query_weight, key_weight, value_weight, output_weight)
        piece_a, piece_m = prepare(me, small, mine + (inner_weight, outer_weight))
        z_a = gather_z(piece_a, fsdp)
        z_m = gather_z(piece_m, fsdp)
        mine_a = stack_three(z_a)
        plane_a = (swap(mine_a, "dp", dp, 1), swap(mine_a, "dp", dp, 2))
        parts_a = (rows_of(plane_a[0], 0, 48), rows_of(plane_a[1], 48, 48))
        rest_a = (swap(parts_a[0], "dp", dp, 2), swap(parts_a[1], "dp", dp, 1))
        z_m[0] = after(z_m[0], *rest_a)
        mine_m = stack_three(z_m)
        inner_m, outer_m = rows_of(mine_m, 0, 96), rows_of(mine_m, 96, 96)
        over_x = [swap(inner_m, "dp", dp, 1), None]
        over_y = [None, swap(outer_m, "dp", dp, 2)]
        over_x[1], over_y[0] = swap(outer_m, "dp", dp, 1), swap(inner_m, "dp", dp, 2)
        near_a = bundle(1, mine, ((((0, 0)),),) * 4, (after(mine_a, mine_m),) + plane_a + (piece_a,))
        far_a = (swap(near_a, "fsdp", fsdp, 1),) + tuple(swap(v, "fsdp", fsdp, 1) for v in rest_a)

        def far_at(base, row=0):
            return [[(base + n, 0, row, 96, 0)] for n in range(3)]

        group_a = Pieces(
            mine,
            (mine_a,) + plane_a + rest_a + far_a + (piece_a,),
            [(n, 0, 0) for n in range(4)],
            [(5, n) for n in range(4)],
            far_at(0) + [[(3, 0, 0, 48, 0), (4, 0, 0, 48, 48)]],
            [[(5, 4 + 3 * n, 0, 96, 0)] for n in range(3)] + [[(6, 0, 0, 48, 0), (7, 0, 0, 48, 48)]],
            True,
            (8, 0, 5),
        )
        x = tokens.reshape(seq, width)
        q, k, v, att, left_a, lse, wa, vec, ib = attend_forward(group_a, fsdp, blocks, me, lengths, after(x, mine_m))
        over_x[0], over_y[1] = after(over_x[0], att), after(over_y[1], att)
        rest_m = (swap(over_x[0], "dp", dp, 2), swap(over_y[1], "dp", dp, 1))
        spots = (tuple((0, 768 * n) for n in range(4)), tuple((96 * n, 0) for n in range(4)))

        def spots_of(n):
            return [(0, *spot) for spot in spots[n]]

        planes = ((inner_m, outer_m), over_x, over_y)
        near_m = bundle(2, (inner_weight, outer_weight), spots, tuple(v for plane in planes for v in plane))
        far_m = swap(near_m, "fsdp", fsdp, 1)
        empty = [[]]
        near_i = Pieces((inner_weight,), (inner_m, over_x[0], over_y[0]), spots_of(0), (), far_at(0) + empty, empty * 4, True)
        near_u = Pieces((outer_weight,), (outer_m, over_x[1], over_y[1]), spots_of(1), (), far_at(0) + empty, empty * 4, False)
        wi = fill(near_i, me, blocks, width, width)
        wu = fill(near_u, me, blocks * width, width)
        rest_m = [after(v, near_m, wi, wu, cost=LONG) for v in rest_m]
        far_rest = [swap(v, "fsdp", fsdp, 1) for v in rest_m]
        far_m = after(far_m, *rest_m)

        def from_sibling(first, tile, stacked):
            far = [[(0, tile + 6 * n, 0, 96, 0)] for n in range(3)] + empty
            return Pieces((), (far_m,), (), [(0, first + n) for n in range(4)], empty * 4, far, stacked)

        def late(n, stacked):
            arrays = (rest_m[n], far_rest[n])
            return Pieces((), arrays, (), (), empty * 3 + [[(0, 0, 0, 96, 0)]], empty * 3 + [[(1, 0, 0, 96, 0)]], stacked)

        wi = fill(from_sibling(0, 8, True), me, blocks, width, width, before=wi)
        wu = fill(from_sibling(4, 11, False), me, blocks * width, width, before=wu)
        far_rest[0] = after(far_rest[0], wi, wu)
        wi = fill(late(0, True), me, blocks, width, width, before=wi)
        wu = fill(late(1, False), me, blocks * width, width, before=wu)
    else:
        whole = tuple(
            lax.all_gather(w, "fsdp", axis=0, tiled=True)
            for w in (query_weight, key_weight, value_weight, output_weight, inner_weight, outer_weight)
        )
        packs = jnp.pad(jnp.stack(small[:8]), ((0, 0), (0, width - part)))
        packs = packs + jnp.pad(inner_bias[None], ((0, 7), (128, width - 128 - 4 * part)))
        packs = lax.all_gather(packs, "fsdp", axis=0, tiled=False)
        group_a = Whole(whole[:4], (packs,), [(n, 0, 0) for n in range(4)], True)
        group_i = Whole(whole[4:5], (), [(0, 0, width * n) for n in range(blocks)], True)
        group_u = Whole(whole[5:6], (), [(0, width * n, 0) for n in range(blocks)], False)
        x = tokens.reshape(seq, width)
        q, k, v, att, left_a, lse, wa, vec, ib = attend_forward(group_a, fsdp, blocks, me, lengths, x)
        wi = fill(group_i, me, blocks, width, width)
        wu = fill(group_u, me, blocks * width, width)

    cot = cotangent.reshape(seq, width)
    out, ssg, low, act_t, slope, norm, rstd, hid_t, sum_one = middle_forward(lengths, x, att, cot, vec, ib, wa, wi, wu)
    pairs = width // 128
    attend = functools.partial(attend_backward, length=lengths, q=q, k=k, v=v, lse=lse)
    if direct:
        sent_u, kept_u = weight_grad("outer", (0, 1, 2, 3), Z_ORDER, me, act_t, low)
        got_u = swap(sent_u, "fsdp", fsdp, 1)
        low = after(low, sent_u)
    igl, fsg, branch, att_g, ib_sum, sum_two = middle_backward(low, ssg, slope, norm, rstd, vec, wa, wi, wu)
    if direct:
        pair_u = (kept_u, after(got_u, igl))
        first_u = first_pair(pair_u, 96)
        over_u = [swap(first_u[0], "dp", dp, 1), swap(first_u[1], "dp", dp, 2)]
        igl = after(igl, *first_u)
        sent_i, kept_i = weight_grad("inner", (0, 1, 2, 3), Z_ORDER, me, hid_t, igl)
        got_i = swap(sent_i, "fsdp", fsdp, 1)
        third = pairs // 3
        part_one = attend(0, third, do=after(att_g, sent_i), branch=branch)
        pair_i = (kept_i, after(got_i, part_one[0]))
        first_i = first_pair(pair_i, 96)
        over_i = [swap(first_i[0], "dp", dp, 1), swap(first_i[1], "dp", dp, 2)]
        g, sum_three = attend(third, pairs, do=after(att_g, *first_i), branch=branch, before=part_one)
    else:
        g, sum_three = attend(0, pairs, do=att_g, branch=branch)
        in_grad, _ = input_grad(g, fsg, wa)

    if direct:
        here = lambda: ()
        sent_a, kept_a = weight_grad(
            "attend", (0, 1, 2, 3), (0, 1, 2, 3), me, left_a, g, (sum_one, sum_two, sum_three, ib_sum)
        )
        over_u = [after(v, kept_a) for v in over_u]
        second_u = second_pair(pair_u, *over_u, 96)
        onward_u = [swap(second_u[0], "dp", dp, 2), swap(second_u[1], "dp", dp, 1)]

        in_grad, token = input_grad(g, after(fsg, *second_u), wa)
        over_i = [after(v, token) for v in over_i]
        second_i = second_pair(pair_i, *over_i, 96, LONG)
        onward_i = [swap(second_i[0], "dp", dp, 2), swap(second_i[1], "dp", dp, 1)]

        got_a = swap(sent_a, "fsdp", fsdp, 1)
        pair_a = (kept_a, after(got_a, *second_i))
        first_a = first_pair(pair_a, 104)
        over_a = [swap(first_a[0], "dp", dp, 1), swap(first_a[1], "dp", dp, 2)]

        onward_u = [after(v, *first_a) for v in onward_u]
        keep_u, send_u = last_pair(pair_u, over_u, onward_u)
        near_u = swap(send_u, "fsdp", fsdp, 2)

        onward_i = [after(v, keep_u) for v in onward_i]
        keep_i, send_i = last_pair(pair_i, over_i, onward_i, LONG)
        near_i = swap(send_i, "fsdp", fsdp, 2)

        near_u = after(near_u, keep_i)
        (next_u,) = combine(((), [(96, [(keep_u, lambda: (1,)), (near_u, lambda: (1,))])]))
        last_u = swap(next_u, "fsdp", fsdp, 4)

        over_a = [after(v, next_u) for v in over_a]
        second_a = second_pair(pair_a, *over_a, 104)
        onward_a = [swap(second_a[0], "dp", dp, 2), swap(second_a[1], "dp", dp, 1)]

        near_i = after(near_i, *second_a)
        (next_i,) = combine(((), [(96, [(keep_i, lambda: (1,)), (near_i, lambda: (1,))])]), cost=LONG)
        last_i = swap(next_i, "fsdp", fsdp, 4)

        last_u = after(last_u, next_i)
        terms_u = [(keep_u, lambda: (0,)), (near_u, lambda: (0,)), (last_u, here)]
        (own_u,) = combine(((), [(96, terms_u)]))

        last_i = after(last_i, own_u)
        terms_i = [(keep_i, lambda: (0,)), (near_i, lambda: (0,)), (last_i, here)]
        (own_i,) = combine(((), [(96, terms_i)]))

        onward_a = [after(v, own_i) for v in onward_a]
        whole_a = combine(*[((), last_terms(pair_a, over_a, onward_a, 104, lambda j=j: j)) for j in range(4)])
        far_a = [swap(whole_a[j], "fsdp", fsdp, 2 * j) for j in (1, 2, 3)]

        (own_m,) = combine(((), [(96, [(after(own_i, whole_a[0]), here)]), (96, [(own_u, here)])]))
        every = spread(own_m, dp)

        far_a[0] = after(far_a[0], own_m)
        own_a, small_own = finish((whole_a[0], *far_a))
        all_a = spread(own_a, dp)
        small_grads = [small_own[n, :part] for n in range(8)] + [small_own[0, 128 : 128 + blocks * part]]
        i_g, u_g = deliver_two(me, every)
        q_g, k_g, v_g, o_g = deliver_four(me, all_a)
    else:
        vec_sum = jnp.concatenate([sum_three[:2], sum_two[2:5], sum_one[5:8]])
        vec_sum = vec_sum.reshape(8, fsdp, part).transpose(1, 0, 2).reshape(fsdp, 8 * part)
        ib_part = ib_sum.reshape(fsdp, blocks * part)
        small_sum = lax.psum(jnp.concatenate([vec_sum, ib_part], axis=1), ("dp", "fsdp"))
        small_own = lax.dynamic_index_in_dim(small_sum, f, 0, keepdims=False)
        small_grads = [small_own[n * part : (n + 1) * part] for n in range(8)] + [small_own[8 * part :]]
        x_t, att_t = left_a[0], left_a[1]
        locals_ = (
            dot_nn(x_t, g[0]),
            dot_nn(x_t, g[1]),
            dot_nn(x_t, g[2]),
            dot_nn(att_t, g[3]),
            jnp.concatenate([dot_nn(hid_t, igl[n]) for n in range(blocks)], axis=1),
            dot_nn(act_t, low),
        )
        owned = [lax.psum_scatter(w, "fsdp", scatter_dimension=0, tiled=True) for w in locals_]
        q_g, k_g, v_g, o_g, i_g, u_g = (lax.psum(w.astype(BF16), "dp").astype(F32) for w in owned)

    qb, vb, ob, g1, s1, ub, g2, s2, ibg = small_grads
    return (
        out.reshape(docs, seq, width),
        in_grad.reshape(docs, seq, width),
        q_g,
        qb,
        k_g,
        v_g,
        vb,
        o_g,
        ob,
        g1,
        s1,
        i_g,
        ibg,
        u_g,
        ub,
        g2,
        s2,
    )


def solution(mesh):
    rows, row = P("fsdp", None), P("fsdp")
    docs = P(("dp", "fsdp"), None, None)
    in_specs = (docs, P(("dp", "fsdp")), docs, rows, row, rows, rows, row, rows, row, row, row, rows, row, rows, row, row, row)
    out_specs = (docs, docs, rows, row, rows, rows, row, rows, row, row, row, rows, row, rows, row, row, row)
    sizes = (mesh.shape["dp"], mesh.shape["fsdp"])
    return jax.shard_map(
        functools.partial(on_device, sizes), mesh=mesh, in_specs=in_specs, out_specs=out_specs, check_vma=False
    )
```

```python
import functools
import math

import jax
import jax.numpy as jnp
from jax import lax
from jax.experimental import pallas as pl
from jax.experimental.pallas import tpu as pltpu
from jax.sharding import PartitionSpec as P

F32 = jnp.float32
BF16 = jnp.bfloat16
HD = 64
MASKED = -1e30
SCALE = HD ** -0.5
EPSILON = 1e-12
ROOT_HALF = math.sqrt(0.5)
INV_ROOT_TWO_PI = 1.0 / math.sqrt(2.0 * math.pi)

VM = pl.BlockSpec(memory_space=pltpu.VMEM)
SM = pl.BlockSpec(memory_space=pltpu.SMEM)
HB = pl.BlockSpec(memory_space=pl.ANY)
FREE = pl.CostEstimate(flops=0, bytes_accessed=0, transcendentals=0)

LONG = pl.CostEstimate(flops=60_000_000_000, bytes_accessed=0, transcendentals=0)


def shape(*dims, dtype=BF16):
    return jax.ShapeDtypeStruct(dims, dtype)


def local(*dims, dtype=BF16):
    return pltpu.VMEM(dims, dtype)


def stay(*values):
    return tuple(pltpu.with_memory_space_constraint(v, pltpu.VMEM) for v in values)


def far_off(*values):
    return tuple(pltpu.with_memory_space_constraint(v, pltpu.HBM) for v in values)


def limit(mebibytes):
    return pltpu.CompilerParams(vmem_limit_bytes=mebibytes << 20)


def dot_nn(a, b):
    return lax.dot_general(a, b, (((1,), (0,)), ((), ())), preferred_element_type=F32)


def dot_nt(a, b):
    return lax.dot_general(a, b, (((1,), (1,)), ((), ())), preferred_element_type=F32)


def flip(value):
    return value.T


def column_sum(value):
    return jnp.sum(value.astype(F32), axis=0, keepdims=True)


def row_mean(value):
    return jnp.mean(value, axis=-1, keepdims=True)


def aligned(start, size):
    return pl.ds(pl.multiple_of(start, size), size)


class Pieces:
    def __init__(self, held, arrays, own, sibling, far, far_sibling, stacked, packs=()):
        self.held, self.arrays, self.own, self.sibling, self.packs = held, arrays, own, sibling, packs
        self.far, self.far_sibling, self.stacked = far, far_sibling, stacked

    def count(self):
        return len(self.own)

    def place(self, target, block, z_at, c_at, offset, rows):
        if self.stacked:
            return target.at[block, aligned_rows((2 * z_at + c_at) * 96 + offset, rows), :]
        return target.at[aligned_rows((2 * z_at + c_at) * 384 + block * 96 + offset, rows), :]

    def copies(self, held, me_ref, target, sems, base):
        z, c = me_ref[1], me_ref[2]
        done = []
        for block, (position, row, lane) in enumerate(self.own):
            where = self.place(target, block, z, c, 0, 96)
            source = held[position].at[pl.ds(row, 96), pl.ds(lane, 768)]
            done.append(pltpu.make_async_copy(source, where, sems.at[base + block]))
        return done

    def fill(self, refs, me_ref, target, rest=(0, 1, 2, 3)):
        i, z, c = me_ref[0], me_ref[1], me_ref[2]
        for block, (position, tile) in enumerate(self.sibling if 0 in rest else ()):
            self.place(target, block, z, 1 - c, 0, 96)[...] = refs[position][tile]
        for c_at, far in ((c, self.far), (1 - c, self.far_sibling)):
            for away in rest:
                parts = far[away]
                for position, tile, row, rows, offset in parts:

                    def copy(j, carry, position=position, tile=tile, row=row, rows=rows, offset=offset, away=away, c_at=c_at):
                        where = self.place(target, i ^ away, z ^ j, c_at, offset, rows)
                        where[...] = refs[position][tile + j - 1, row : row + rows, :]
                        return carry

                    lax.fori_loop(1, 4, copy, 0)

    def vectors(self, refs, me_ref, target):
        z, c = me_ref[1], me_ref[2]
        own, mine, other = (refs[n] for n in self.packs)
        for j in range(4):
            target[2 * (z ^ j) + c] = (mine[j - 1, 96:104, :] if j else own[96:104, :]).astype(F32)
            target[2 * (z ^ j) + 1 - c] = other[13, 8 * j : 8 * j + 8, :].astype(F32)


def bundle_body(group_count, held, me_ref, *refs):
    sources, near = refs[: len(held)], refs[len(held) : -2]
    out_ref, sems = refs[-2:]
    own = [(n, row, lane) for n, spots in enumerate(held) for row, lane in spots]
    loads = []
    for tile, (n, row, lane) in enumerate(own):
        source = sources[n].at[pl.ds(row, 96), pl.ds(lane, 768)]
        loads.append(pltpu.make_async_copy(source, out_ref.at[tile], sems.at[tile]))
    start_all(loads)
    tile = len(own)
    for away in range(3):
        for group in range(group_count):
            for j in range(3):
                out_ref[tile] = near[away * group_count + group][j, :96, :]
                tile += 1
    if group_count == 1:
        out_ref[tile, 0:8, :] = near[3][96:104, :]
        for j in range(3):
            out_ref[tile, 8 * j + 8 : 8 * j + 16, :] = near[0][j, 96:104, :]
        out_ref[tile, 32:, :] = jnp.zeros((64, 768), BF16)
    wait_all(loads)


def bundle(group_count, sources, held, near):
    own = sum(len(spots) for spots in held)
    tiles = own + 9 * group_count + (group_count == 1)
    return pl.pallas_call(
        functools.partial(bundle_body, group_count, held),
        out_shape=local(tiles, 96, 768),
        in_specs=[SM] + [HB] * len(sources) + [VM] * len(near),
        out_specs=VM,
        scratch_shapes=[pltpu.SemaphoreType.DMA((own,))],
        compiler_params=limit(2),
        cost_estimate=FREE,
        name="bundle",
    )(jnp.zeros((1,), jnp.int32), *far_off(*sources), *stay(*near))


def aligned_rows(start, rows):
    return pl.ds(pl.multiple_of(start, 16), rows)


class Whole:
    def __init__(self, held, arrays, spots, stacked):
        self.held, self.arrays, self.spots, self.stacked = held, arrays, spots, stacked

    def count(self):
        return len(self.spots)

    def copies(self, held, me_ref, target, sems, base):
        done = []
        for block, (position, row, lane) in enumerate(self.spots):
            where = target.at[block] if self.stacked else target.at[pl.ds(block * 768, 768), :]
            source = held[position].at[pl.ds(row, 768), pl.ds(lane, 768)]
            done.append(pltpu.make_async_copy(source, where, sems.at[base + block]))
        return done

    def fill(self, refs, me_ref, target, rest=()):
        pass

    def vectors(self, refs, me_ref, target):
        target[...] = refs[0][...].astype(F32)


def start_all(copies):
    for copy in copies:
        copy.start()


def wait_all(copies):
    for copy in copies:
        copy.wait()


def pair_masks(dims, axis):
    spot = lax.broadcasted_iota(jnp.int32, dims, axis)
    return spot < HD, spot >= HD


def keep(mask, value):
    return jnp.where(mask, value, jnp.zeros_like(value))


def attend_forward_body(group, part, me_ref, len_ref, x_ref, *refs):
    held, refs = refs[: len(group.held)], refs[len(group.held) :]
    sources = refs[: len(group.arrays)]
    q_ref, k_ref, v_ref, att_ref, left_ref, lse_ref, w_ref, vec_ref, ib_ref, packed, sems = refs[len(group.arrays) :]
    seq, width = x_ref.shape
    tile = min(512, seq)
    loads = group.copies(held, me_ref, w_ref, sems, 0)
    start_all(loads)
    group.fill(sources, me_ref, w_ref)
    group.vectors(sources, me_ref, packed)
    for f in range(packed.shape[0]):
        pack = packed[f]
        vec_ref[:, f * part : (f + 1) * part] = pack[:, :part]
        row, lane = divmod(f * 4 * part, width)
        ib_ref[row : row + 1, lane : lane + 4 * part] = pack[:1, 128 : 128 + 4 * part]
    for p in range(width // 128):
        left_ref[0, p * 128 : (p + 1) * 128, :] = flip(x_ref[:, p * 128 : (p + 1) * 128])
    wait_all(loads)

    def project(r, carry):
        rows = aligned(r * tile, tile)
        x = x_ref[rows, :]
        q_ref[rows, :] = (dot_nn(x, w_ref[0]) + vec_ref[0:1, :]).astype(BF16)
        k_ref[rows, :] = dot_nn(x, w_ref[1]).astype(BF16)
        v_ref[rows, :] = (dot_nn(x, w_ref[2]) + vec_ref[1:2, :]).astype(BF16)
        return carry

    lax.fori_loop(0, seq // tile, project, 0)
    length = len_ref[0]

    def pair(p, carry):
        lanes = aligned(p * 128, 128)
        k_pair = k_ref[:, lanes]
        q_t = (q_ref[:, lanes].astype(F32) * SCALE).T.astype(BF16)
        v_t = flip(v_ref[:, lanes])
        masks = pair_masks((128, seq), 0)
        allowed = lax.broadcasted_iota(jnp.int32, (seq, seq), 0) < length
        for e in range(2):
            s = dot_nn(k_pair, keep(masks[e], q_t))
            s = jnp.where(allowed, s, MASKED)
            top = jnp.max(s, axis=0, keepdims=True)
            p_t = jnp.exp(s - top)
            total = jnp.sum(p_t, axis=0, keepdims=True)
            o_t = dot_nn(v_t[e * HD : (e + 1) * HD, :], p_t.astype(BF16)) / total
            left_ref[1, aligned(p * 128 + e * HD, HD), :] = o_t.astype(BF16)
            lse_ref[pl.ds(p * 2 + e, 1), :] = top + jnp.log(total)
        att_ref[:, lanes] = flip(left_ref[1, aligned(p * 128, 128), :])
        return carry

    lax.fori_loop(0, width // 128, pair, 0, unroll=2)


def attend_forward(group, shards, blocks, me, length, x):
    seq, width = x.shape
    heads = width // HD
    return pl.pallas_call(
        functools.partial(attend_forward_body, group, width // shards),
        out_shape=(local(seq, width),) * 4
        + (local(2, width, seq), local(-(-heads // 8) * 8, seq, dtype=F32), local(4, width, width))
        + (local(8, width, dtype=F32), local(blocks, width, dtype=F32)),
        in_specs=[SM, SM, VM] + [HB] * len(group.held) + [VM] * len(group.arrays),
        out_specs=[VM] * 9,
        scratch_shapes=[pltpu.VMEM((shards, 8, width), F32), pltpu.SemaphoreType.DMA((group.count(),))],
        compiler_params=limit(10),
        cost_estimate=FREE,
        name="attend_forward",
    )(me, length, x, *far_off(*group.held), *stay(*group.arrays))


def attend_backward_body(first, last, len_ref, q_ref, k_ref, v_ref, do_ref, lse_ref, branch_ref, *refs):
    g_ref, sum_ref = refs[-2:]
    seq, width = q_ref.shape
    length = len_ref[0]

    def pair(p, carry):
        lanes = aligned(p * 128, 128)
        q_pair = (q_ref[:, lanes].astype(F32) * SCALE).astype(BF16)
        k_pair = k_ref[:, lanes]
        v_pair = v_ref[:, lanes]
        do_pair = do_ref[:, lanes]
        q_t = flip(q_pair)
        k_t = (k_pair.astype(F32) * SCALE).T.astype(BF16)
        do_t = flip(do_pair)
        sub_masks = pair_masks((128, seq), 0)
        lane_masks = pair_masks((seq, 128), 1)
        allowed = lax.broadcasted_iota(jnp.int32, (seq, seq), 0) < length
        dk = jnp.zeros((seq, 128), F32)
        dv = jnp.zeros((seq, 128), F32)
        dq_t = []
        for e in range(2):
            s = dot_nn(k_pair, keep(sub_masks[e], q_t))
            s = jnp.where(allowed, s, MASKED)
            p_t = jnp.exp(s - lse_ref[pl.ds(p * 2 + e, 1), :])
            dp = dot_nn(v_pair, keep(sub_masks[e], do_t))
            dv = dv + dot_nn(p_t.astype(BF16), keep(lane_masks[e], do_pair))
            t = p_t * dp
            row = jnp.sum(t, axis=0, keepdims=True)
            ds = (t - p_t * row).astype(BF16)
            dk = dk + dot_nn(ds, keep(lane_masks[e], q_pair))
            dq_t.append(dot_nn(k_t[e * HD : (e + 1) * HD, :], ds))
        dq = jnp.concatenate(dq_t, axis=0).T.astype(BF16)
        dv = dv.astype(BF16)
        g_ref[0, :, lanes] = dq
        g_ref[1, :, lanes] = dk.astype(BF16)
        g_ref[2, :, lanes] = dv
        g_ref[3, :, lanes] = branch_ref[:, lanes]
        sum_ref[0:1, lanes] = column_sum(dq)
        sum_ref[1:2, lanes] = column_sum(dv)
        return carry

    lax.fori_loop(first, last, pair, 0, unroll=2)


def attend_backward(first, last, length, q, k, v, do, lse, branch, before=()):
    seq, width = q.shape
    return pl.pallas_call(
        functools.partial(attend_backward_body, first, last),
        out_shape=(local(4, seq, width), local(8, width, dtype=F32)),
        in_specs=[SM] + [VM] * 6 + [HB] * len(before),
        out_specs=[VM] * 2,
        input_output_aliases={7 + n: n for n in range(len(before))},
        compiler_params=limit(10),
        cost_estimate=FREE,
        name="attend_backward",
    )(length, *stay(q, k, v, do, lse, branch, *before))


def gelu_parts(inner):
    cumulative = 0.5 * (1.0 + lax.erf(inner * ROOT_HALF))
    density = jnp.exp(-0.5 * inner * inner) * INV_ROOT_TWO_PI
    return inner * cumulative, cumulative + inner * density


def fill_body(group, early, me_ref, *refs):
    held, near = refs[: len(group.held)], refs[len(group.held) : len(group.held) + len(group.arrays)]
    if not early:
        group.fill(near, me_ref, refs[-1])
        return
    target, sems = refs[-2:]
    loads = group.copies(held, me_ref, target, sems, 0)
    start_all(loads)
    group.fill(near, me_ref, target)
    wait_all(loads)


def fill(group, me, *dims, before=None):
    early = before is None
    more = () if early else (before,)
    return pl.pallas_call(
        functools.partial(fill_body, group, early),
        out_shape=local(*dims),
        in_specs=[SM] + [HB] * len(group.held) + [VM] * len(group.arrays) + [HB] * len(more),
        out_specs=VM,
        scratch_shapes=[pltpu.SemaphoreType.DMA((group.count(),))] * early,
        input_output_aliases={} if early else {1 + len(group.held) + len(group.arrays): 0},
        compiler_params=limit(2),
        cost_estimate=FREE,
        name="fill",
    )(me, *far_off(*group.held), *stay(*group.arrays, *more))


def middle_forward_body(
    len_ref,
    x_ref,
    att_ref,
    cot_ref,
    vec_ref,
    ib_ref,
    wa,
    wi,
    wu,
    out_ref,
    ssg_ref,
    low_ref,
    actT_ref,
    slope_ref,
    norm_ref,
    rstd_ref,
    hidT_ref,
    sum_ref,
):
    seq, width = x_ref.shape
    blocks = wi.shape[0]
    tile = min(512, seq)
    length = len_ref[0]
    sum_ref[...] = jnp.zeros_like(sum_ref)

    def rows_step(r, carry):
        rows = aligned(r * tile, tile)
        first = x_ref[rows, :].astype(F32) + dot_nn(att_ref[rows, :], wa[3]) + vec_ref[2:3, :]
        center = first - row_mean(first)
        rstd = lax.rsqrt(row_mean(center * center) + EPSILON)
        normed = center * rstd
        norm_ref[rows, :] = normed
        rstd_ref[rows, :] = rstd
        hidden = normed * vec_ref[3:4, :] + vec_ref[4:5, :]
        low = hidden.astype(BF16)
        hidT_ref[:, rows] = low.astype(F32).T.astype(BF16)

        def block(f, second):
            inner = dot_nn(low, wi[f]) + ib_ref[pl.ds(f, 1), :]
            active, slope = gelu_parts(inner)
            active = active.astype(BF16)
            spot = aligned(f * width, width)
            slope_ref[rows, spot] = slope.astype(BF16)
            actT_ref[spot, rows] = flip(active)
            return second + dot_nn(active, wu[spot, :])

        second = lax.fori_loop(0, blocks, block, hidden + vec_ref[5:6, :], unroll=True)
        center = second - row_mean(second)
        rstd = lax.rsqrt(row_mean(center * center) + EPSILON)
        normed = center * rstd
        spot = r * tile + lax.broadcasted_iota(jnp.int32, (tile, width), 0)
        valid = spot < length
        result = normed * vec_ref[6:7, :] + vec_ref[7:8, :]
        out_ref[rows, :] = jnp.where(valid, result, 0.0).astype(BF16)
        grad = jnp.where(valid, cot_ref[rows, :].astype(F32), 0.0)
        sum_ref[7:8, :] += column_sum(grad)
        sum_ref[6:7, :] += column_sum(grad * normed)
        grad = grad * vec_ref[6:7, :]
        grad = rstd * (grad - row_mean(grad) - normed * row_mean(grad * normed))
        ssg_ref[rows, :] = grad
        low = grad.astype(BF16)
        low_ref[rows, :] = low
        sum_ref[5:6, :] += column_sum(low)
        return carry

    lax.fori_loop(0, seq // tile, rows_step, 0)


def middle_forward(length, x, att, cot, vec, ib, wa, wi, wu):
    seq, width = x.shape
    blocks = ib.shape[0]
    return pl.pallas_call(
        middle_forward_body,
        out_shape=(
            shape(seq, width),
            local(seq, width, dtype=F32),
            local(seq, width),
            local(blocks * width, seq),
            local(seq, blocks * width),
            local(seq, width, dtype=F32),
            local(seq, 1, dtype=F32),
            local(width, seq),
            local(8, width, dtype=F32),
        ),
        in_specs=[SM] + [VM] * 8,
        out_specs=[VM] * 9,
        compiler_params=limit(16),
        cost_estimate=FREE,
        name="middle_forward",
    )(length, x, *stay(att), cot, *stay(vec, ib, wa, wi, wu))


def middle_backward_body(
    low_ref, ssg_ref, slope_ref, norm_ref, rstd_ref, vec_ref, wa, wi, wu, igl_ref, fsg_ref, branch_ref, att_ref, ib_ref, sum_ref
):
    seq, width = low_ref.shape
    blocks = wi.shape[0]
    tile = min(512, seq)
    sum_ref[...] = jnp.zeros_like(sum_ref)
    ib_ref[...] = jnp.zeros_like(ib_ref)

    def rows_step(r, carry):
        rows = aligned(r * tile, tile)
        low = low_ref[rows, :]

        def block(f, grad):
            spot = aligned(f * width, width)
            inner = (dot_nt(low, wu[spot, :]) * slope_ref[rows, spot].astype(F32)).astype(BF16)
            igl_ref[f, rows, :] = inner
            ib_ref[pl.ds(f, 1), :] += column_sum(inner)
            return grad + dot_nt(inner, wi[f])

        grad = lax.fori_loop(0, blocks, block, ssg_ref[rows, :], unroll=True)
        normed = norm_ref[rows, :]
        sum_ref[4:5, :] += column_sum(grad)
        sum_ref[3:4, :] += column_sum(grad * normed)
        grad = grad * vec_ref[3:4, :]
        grad = rstd_ref[rows, :] * (grad - row_mean(grad) - normed * row_mean(grad * normed))
        fsg_ref[rows, :] = grad
        branch = grad.astype(BF16)
        branch_ref[rows, :] = branch
        sum_ref[2:3, :] += column_sum(branch)
        att_ref[rows, :] = dot_nt(branch, wa[3]).astype(BF16)
        return carry

    lax.fori_loop(0, seq // tile, rows_step, 0)


def middle_backward(low, ssg, slope, norm, rstd, vec, wa, wi, wu):
    seq, width = low.shape
    blocks = wi.shape[0]
    return pl.pallas_call(
        middle_backward_body,
        out_shape=(
            local(blocks, seq, width),
            local(seq, width, dtype=F32),
            local(seq, width),
            local(seq, width),
            local(blocks, width, dtype=F32),
            local(8, width, dtype=F32),
        ),
        in_specs=[VM] * 9,
        out_specs=[VM] * 6,
        compiler_params=limit(16),
        cost_estimate=FREE,
        name="middle_backward",
    )(*stay(low, ssg, slope, norm, rstd, vec, wa, wi, wu))


def input_grad_body(g_ref, fsg_ref, w_ref, out_ref, token_ref):
    seq, width = fsg_ref.shape
    token_ref[...] = jnp.zeros_like(token_ref)
    tile = min(512, seq)

    def rows_step(r, carry):
        rows = aligned(r * tile, tile)
        total = fsg_ref[rows, :]
        for n in range(3):
            total = total + dot_nt(g_ref[n, rows, :], w_ref[n])
        out_ref[rows, :] = total
        return carry

    lax.fori_loop(0, seq // tile, rows_step, 0)


def input_grad(g, fsg, wa):
    seq, width = fsg.shape
    return pl.pallas_call(
        input_grad_body,
        out_shape=(shape(seq, width, dtype=F32), local(8, 128, dtype=F32)),
        in_specs=[VM] * 3,
        out_specs=[VM] * 2,
        compiler_params=limit(12),
        cost_estimate=FREE,
        name="input_grad",
    )(*stay(g, fsg, wa))


Z_ORDER = (0, 2, 1, 3)


def weight_grad_body(kind, order, z_order, me_ref, left_ref, g_ref, *refs):
    sums, refs = (refs[:4], refs[4:]) if kind == "attend" else ((), refs)
    outs, left = refs[:2], refs[2]
    i, z, c = me_ref[0], me_ref[1], me_ref[2]
    part = 96
    if kind == "attend":
        extra = refs[3]
        one, two, three, ib = (r[...] for r in sums)
        row = lax.broadcasted_iota(jnp.int32, one.shape, 0)
        every = jnp.where(row < 2, three, jnp.where(row < 5, two, one))
        for f in range(8):
            extra[f] = jnp.zeros_like(extra[f])
            extra[f, :, :part] = every[:, f * part : (f + 1) * part]
            extra[f, 0:1, 128 : 128 + 4 * part] = ib[f // 2 : f // 2 + 1, f % 2 * 4 * part : (f % 2 + 1) * 4 * part]

    def block_step(spot, carry):
        block = i ^ pick(order, spot)
        for side, c_at in enumerate((1 - c, c)):
            for n, j in enumerate(z_order):
                f_at = 2 * (z ^ j) + c_at
                if kind == "outer":
                    rows = left_ref[aligned_rows(f_at * 384 + block * 96, 96), :]
                elif kind == "inner":
                    rows = left_ref[aligned_rows(f_at * 96, 96), :]
                else:
                    rows = left_ref[block // 3, aligned_rows(f_at * 96, 96), :]
                left[side * 384 + n * 96 : side * 384 + (n + 1) * 96, :] = rows
        right = g_ref[...] if kind == "outer" else g_ref[block]
        grads = dot_nn(left[...], right).reshape(2, 4, 96, 768).astype(BF16)
        for side, c_at in enumerate((1 - c, c)):
            outs[side][spot, :, :96, :] = grads[side]
            if kind == "attend":
                for n, j in enumerate(z_order):
                    outs[side][spot, n, 96:104, :] = extra[2 * (z ^ j) + c_at].astype(BF16)
        return carry

    lax.fori_loop(0, 4, block_step, 0, unroll=2)


def weight_grad(kind, order, z_order, me, left, g, sums=()):
    rows = 104 if kind == "attend" else 96
    return pl.pallas_call(
        functools.partial(weight_grad_body, kind, order, z_order),
        out_shape=(local(4, 4, rows, 768),) * 2,
        in_specs=[SM] + [VM] * (2 + len(sums)),
        out_specs=[VM] * 2,
        scratch_shapes=[pltpu.VMEM((768, left.shape[-1]), BF16)] + [pltpu.VMEM((8, 8, 768), F32)] * (kind == "attend"),
        compiler_params=limit(6),
        cost_estimate=FREE,
        name=f"weight_grad_{kind}",
    )(me, *stay(left, g, *sums))


def prepare_body(me_ref, *refs):
    vectors, weights = refs[:9], refs[9:15]
    first_ref, second_ref, pack_ref, *rows, sems = refs[15:]
    i = me_ref[0]
    part = vectors[0].shape[0]
    copies = [
        pltpu.make_async_copy(
            weights[4].at[:, pl.ds(pl.multiple_of(i * 768, 768), 768)], second_ref.at[pl.ds(0, 96), :], sems.at[0]
        ),
        pltpu.make_async_copy(weights[5].at[aligned_rows(i * 96, 96), :], second_ref.at[pl.ds(96, 96), :], sems.at[1]),
    ]
    for n in range(9):
        copies.append(pltpu.make_async_copy(vectors[n], rows[n], sems.at[3 + n]))
    for n in range(4):

        @pl.when(i == n)
        def _():
            pltpu.make_async_copy(weights[n], first_ref.at[pl.ds(0, 96), :], sems.at[2]).start()

    start_all(copies)
    pack_ref[...] = jnp.zeros_like(pack_ref)
    wait_all(copies[2:])
    for n in range(8):
        pack_ref[n : n + 1, :part] = rows[n][...].astype(F32).reshape(1, part)
    pack_ref[0:1, 128 : 128 + 4 * part] = rows[8][...].astype(F32).reshape(1, 4 * part)
    first_ref[96:104, :] = pack_ref[...].astype(BF16)
    pltpu.make_async_copy(weights[0], first_ref.at[pl.ds(0, 96), :], sems.at[2]).wait()
    wait_all(copies[:2])


def prepare(me, vectors, weights):
    return pl.pallas_call(
        prepare_body,
        out_shape=(local(104, 768), local(192, 768)),
        in_specs=[SM] + [HB] * 15,
        out_specs=[VM] * 2,
        scratch_shapes=[pltpu.VMEM((8, 768), F32)]
        + [pltpu.VMEM(v.shape, BF16) for v in vectors]
        + [pltpu.SemaphoreType.DMA((12,))],
        compiler_params=limit(2),
        cost_estimate=FREE,
        name="prepare",
    )(me, *far_off(*vectors, *weights))


def after(value, *others, cost=FREE):
    def body(*refs):
        pass

    return pl.pallas_call(
        body,
        out_shape=jax.ShapeDtypeStruct(value.shape, value.dtype),
        in_specs=[HB] * (1 + len(others)),
        out_specs=HB,
        input_output_aliases={0: 0},
        compiler_params=limit(1),
        cost_estimate=cost,
        name="after",
    )(value, *others)


def swap(value, axis, size, mask):
    return lax.ppermute(value, axis, [(n, n ^ mask) for n in range(size)])


def combine(*outs, cost=FREE):
    arrays = []
    for _, parts in outs:
        for _, terms in parts:
            arrays += [a for a, _ in terms if not any(a is b for b in arrays)]

    def find(array):
        return next(n for n, b in enumerate(arrays) if b is array)

    def body(*refs):
        for out_ref, (lead, parts) in zip(refs[len(arrays) :], outs, strict=True):

            def tile(index):
                start = 0
                for rows, terms in parts:
                    found = [(find(array), at(*index)) for array, at in terms]
                    values = [refs[n][spot] for n, spot in found if spot is not None]
                    value = values[0] if len(values) == 1 else sum(v.astype(F32) for v in values).astype(BF16)
                    out_ref[(*index, slice(start, start + rows), slice(None))] = value
                    start += rows

            def step(front, last, carry):
                tile((*front, last))
                return carry

            if not lead:
                tile(())
            elif len(lead) == 1:
                lax.fori_loop(0, lead[0], functools.partial(step, ()), 0)
            else:
                for front in range(lead[0]):
                    lax.fori_loop(0, lead[1], functools.partial(step, (front,)), 0)

    return pl.pallas_call(
        body,
        out_shape=tuple(local(*lead, sum(rows for rows, _ in parts), 768) for lead, parts in outs),
        in_specs=[VM] * len(arrays),
        out_specs=[VM] * len(outs),
        compiler_params=limit(2),
        cost_estimate=cost,
        name="combine",
    )(*stay(*arrays))


def stack(rows, *tiles, cost=FREE):
    def body(*refs):
        for n, (_, place, first) in enumerate(tiles):
            part = pl.ds(first, rows)
            refs[-1][n] = refs[n][part, :] if place is None else refs[n][place, part, :]

    return pl.pallas_call(
        body,
        out_shape=local(len(tiles), rows, 768),
        in_specs=[VM] * len(tiles),
        out_specs=VM,
        compiler_params=limit(2),
        cost_estimate=cost,
        name="stack",
    )(*stay(*(array for array, _, _ in tiles)))


def pair_up(piece, fsdp, cost=FREE):
    other = swap(piece, "fsdp", fsdp, 4)
    return other, lambda ready: stack(piece.shape[0], (piece, None, 0), (ready, None, 0), cost=cost)


def rows_of(value, start, rows):
    (part,) = combine(((value.shape[0],), [(rows, [(value, lambda n: (n, slice(start, start + rows)))])]))
    return part


UPPER = slice(0, 48)


def held(pair, block, rows):
    return [(v, lambda b: (block, b, rows)) for v in pair]


def first_pair(pair, total):
    def out(blocks, rows, size):
        terms = []
        for n, block in enumerate(blocks):
            for array, at in held(pair, block, rows):
                terms.append((array, lambda a, b, n=n, at=at: at(b) if a == n else None))
        return (2, 4), [(size, terms)]

    return combine(out((1, 3), UPPER, 48), out((2, 3), slice(48, total), total - 48))


def second_pair(pair, over_x, over_y, total, cost=FREE):
    x = held(pair, 2, UPPER) + [(over_x, lambda b: (1, b))]
    y = held(pair, 1, slice(48, total)) + [(over_y, lambda b: (1, b))]
    return combine(((4,), [(48, x)]), ((4,), [(total - 48, y)]), cost=cost)


def last_terms(pair, overs, onwards, total, tile):
    parts = []
    for rows, size, over, onward in (
        (UPPER, 48, overs[0], onwards[0]),
        (slice(48, total), total - 48, overs[1], onwards[1]),
    ):
        terms = [(array, lambda *n, at=at: at(tile(*n))) for array, at in held(pair, 0, rows)]
        terms += [(over, lambda *n: (0, tile(*n))), (onward, lambda *n: (tile(*n),))]
        parts.append((size, terms))
    return parts


def last_pair(pair, overs, onwards, cost=FREE):
    return combine(*[((2,), last_terms(pair, overs, onwards, 96, lambda b, k=k: k + b)) for k in (0, 2)], cost=cost)


def finish(terms):
    def body(*refs):
        terms, (own_ref, small_ref) = refs[:-2], refs[-2:]
        value = sum(r[...].astype(F32) for r in terms)
        own_ref[...] = value[:96].astype(BF16)
        small_ref[...] = value[96:]

    return pl.pallas_call(
        body,
        out_shape=(local(96, 768), local(8, 768, dtype=F32)),
        in_specs=[VM] * len(terms),
        out_specs=[VM] * 2,
        compiler_params=limit(2),
        cost_estimate=FREE,
        name="finish",
    )(*stay(*terms))


def spread(value, dp):
    return (value,) + tuple(swap(value, "dp", dp, m) for m in (1, 2, 3))


def deliver_two(me, every):
    def body(me_ref, *refs):
        inner_ref, outer_ref = refs[4:]
        for away in range(4):
            block = me_ref[0] ^ away
            inner_ref[:, aligned(block * 768, 768)] = refs[away][:96, :].astype(F32)
            outer_ref[aligned(block * 96, 96), :] = refs[away][96:, :].astype(F32)

    return pl.pallas_call(
        body,
        out_shape=(shape(96, 3072, dtype=F32), shape(384, 768, dtype=F32)),
        in_specs=[SM] + [VM] * 4,
        out_specs=[VM] * 2,
        compiler_params=limit(6),
        cost_estimate=FREE,
        name="deliver_two",
    )(me, *stay(*every))


def deliver_four(me, every):
    def body(me_ref, *refs):
        outs, held_ref = refs[4:8], refs[8]
        for away in range(4):
            held_ref[me_ref[0] ^ away] = refs[away][...]
        for n in range(4):
            outs[n][...] = held_ref[n].astype(F32)

    return pl.pallas_call(
        body,
        out_shape=(shape(96, 768, dtype=F32),) * 4,
        in_specs=[SM] + [VM] * 4,
        out_specs=[VM] * 4,
        scratch_shapes=[pltpu.VMEM((4, 96, 768), BF16)],
        compiler_params=limit(4),
        cost_estimate=FREE,
        name="deliver_four",
    )(me, *stay(*every))


def pick(pieces, index):
    return jnp.where(index == 0, pieces[0], jnp.where(index == 1, pieces[1], jnp.where(index == 2, pieces[2], pieces[3])))


def on_device(
    sizes,
    tokens,
    lengths,
    cotangent,
    query_weight,
    query_bias,
    key_weight,
    value_weight,
    value_bias,
    output_weight,
    output_bias,
    first_gain,
    first_shift,
    inner_weight,
    inner_bias,
    outer_weight,
    outer_bias,
    second_gain,
    second_shift,
):
    dp, fsdp = sizes
    docs, seq, width = tokens.shape
    blocks = inner_weight.shape[1] // width
    direct = dp == 4 and fsdp == 8 and docs == 1 and query_weight.shape == (96, 768) and blocks == 4
    i = lax.axis_index("dp")
    f = lax.axis_index("fsdp")
    me = jnp.stack([i, f // 2, f % 2, jnp.zeros_like(i)]).astype(jnp.int32)

    small = (query_bias, value_bias, output_bias, first_gain, first_shift, outer_bias, second_gain, second_shift, inner_bias)
    part = query_bias.shape[0]

    if direct:
        mine = (query_weight, key_weight, value_weight, output_weight)
        piece_a, piece_m = prepare(me, small, mine + (inner_weight, outer_weight))
        other_a, with_a = pair_up(piece_a, fsdp)
        other_m, with_m = pair_up(piece_m, fsdp, LONG)
        pair_a = with_a(other_a)
        beside_a = swap(pair_a, "fsdp", fsdp, 2)
        mine_a = stack(104, (beside_a, 0, 0), (other_a, None, 0), (beside_a, 1, 0))
        other_m = after(other_m, mine_a)
        beside_m = swap(with_m(other_m), "fsdp", fsdp, 2)
        plane_a = (swap(mine_a, "dp", dp, 1), swap(mine_a, "dp", dp, 2))
        plane_a = tuple(after(v, other_m) for v in plane_a)
        parts_a = (rows_of(plane_a[0], 0, 48), rows_of(plane_a[1], 48, 48))
        rest_a = (swap(parts_a[0], "dp", dp, 2), swap(parts_a[1], "dp", dp, 1))
        beside_m = after(beside_m, *rest_a)
        inner_m, outer_m = (stack(96, (beside_m, 0, n), (other_m, None, n), (beside_m, 1, n)) for n in (0, 96))
        over_x = [swap(inner_m, "dp", dp, 1), None]
        over_y = [None, swap(outer_m, "dp", dp, 2)]
        over_x[1], over_y[0] = swap(outer_m, "dp", dp, 1), swap(inner_m, "dp", dp, 2)
        near_a = bundle(1, mine, ((((0, 0)),),) * 4, (after(mine_a, inner_m),) + plane_a + (piece_a,))
        far_a = (swap(near_a, "fsdp", fsdp, 1),) + tuple(swap(v, "fsdp", fsdp, 1) for v in rest_a)

        def far_at(base, row=0):
            return [[(base + n, 0, row, 96, 0)] for n in range(3)]

        group_a = Pieces(
            mine,
            (mine_a,) + plane_a + rest_a + far_a + (piece_a,),
            [(n, 0, 0) for n in range(4)],
            [(5, n) for n in range(4)],
            far_at(0) + [[(3, 0, 0, 48, 0), (4, 0, 0, 48, 48)]],
            [[(5, 4 + 3 * n, 0, 96, 0)] for n in range(3)] + [[(6, 0, 0, 48, 0), (7, 0, 0, 48, 48)]],
            True,
            (8, 0, 5),
        )
        x = tokens.reshape(seq, width)
        q, k, v, att, left_a, lse, wa, vec, ib = attend_forward(group_a, fsdp, blocks, me, lengths, after(x, inner_m))
        over_x[0], over_y[1] = after(over_x[0], att), after(over_y[1], att)
        rest_m = (swap(over_x[0], "dp", dp, 2), swap(over_y[1], "dp", dp, 1))
        spots = (tuple((0, 768 * n) for n in range(4)), tuple((96 * n, 0) for n in range(4)))

        def spots_of(n):
            return [(0, *spot) for spot in spots[n]]

        planes = ((inner_m, outer_m), over_x, over_y)
        near_m = bundle(2, (inner_weight, outer_weight), spots, tuple(v for plane in planes for v in plane))
        far_m = swap(near_m, "fsdp", fsdp, 1)
        empty = [[]]
        near_i = Pieces((inner_weight,), (inner_m, over_x[0], over_y[0]), spots_of(0), (), far_at(0) + empty, empty * 4, True)
        near_u = Pieces((outer_weight,), (outer_m, over_x[1], over_y[1]), spots_of(1), (), far_at(0) + empty, empty * 4, False)
        wi = fill(near_i, me, blocks, width, width)
        wu = fill(near_u, me, blocks * width, width)
        rest_m = [after(v, near_m, wi, wu, cost=LONG) for v in rest_m]
        far_rest = [swap(v, "fsdp", fsdp, 1) for v in rest_m]
        far_m = after(far_m, *rest_m)

        def from_sibling(first, tile, stacked):
            far = [[(0, tile + 6 * n, 0, 96, 0)] for n in range(3)] + empty
            return Pieces((), (far_m,), (), [(0, first + n) for n in range(4)], empty * 4, far, stacked)

        def late(n, stacked):
            arrays = (rest_m[n], far_rest[n])
            return Pieces((), arrays, (), (), empty * 3 + [[(0, 0, 0, 96, 0)]], empty * 3 + [[(1, 0, 0, 96, 0)]], stacked)

        wi = fill(from_sibling(0, 8, True), me, blocks, width, width, before=wi)
        wu = fill(from_sibling(4, 11, False), me, blocks * width, width, before=wu)
        far_rest[0] = after(far_rest[0], wi, wu)
        wi = fill(late(0, True), me, blocks, width, width, before=wi)
        wu = fill(late(1, False), me, blocks * width, width, before=wu)
    else:
        whole = tuple(
            lax.all_gather(w, "fsdp", axis=0, tiled=True)
            for w in (query_weight, key_weight, value_weight, output_weight, inner_weight, outer_weight)
        )
        packs = jnp.pad(jnp.stack(small[:8]), ((0, 0), (0, width - part)))
        packs = packs + jnp.pad(inner_bias[None], ((0, 7), (128, width - 128 - 4 * part)))
        packs = lax.all_gather(packs, "fsdp", axis=0, tiled=False)
        group_a = Whole(whole[:4], (packs,), [(n, 0, 0) for n in range(4)], True)
        group_i = Whole(whole[4:5], (), [(0, 0, width * n) for n in range(blocks)], True)
        group_u = Whole(whole[5:6], (), [(0, width * n, 0) for n in range(blocks)], False)
        x = tokens.reshape(seq, width)
        q, k, v, att, left_a, lse, wa, vec, ib = attend_forward(group_a, fsdp, blocks, me, lengths, x)
        wi = fill(group_i, me, blocks, width, width)
        wu = fill(group_u, me, blocks * width, width)

    cot = cotangent.reshape(seq, width)
    out, ssg, low, act_t, slope, norm, rstd, hid_t, sum_one = middle_forward(lengths, x, att, cot, vec, ib, wa, wi, wu)
    pairs = width // 128
    attend = functools.partial(attend_backward, length=lengths, q=q, k=k, v=v, lse=lse)
    if direct:
        sent_u, kept_u = weight_grad("outer", (0, 1, 2, 3), Z_ORDER, me, act_t, low)
        got_u = swap(sent_u, "fsdp", fsdp, 1)
        low = after(low, sent_u)
    igl, fsg, branch, att_g, ib_sum, sum_two = middle_backward(low, ssg, slope, norm, rstd, vec, wa, wi, wu)
    if direct:
        pair_u = (kept_u, after(got_u, igl))
        first_u = first_pair(pair_u, 96)
        over_u = [swap(first_u[0], "dp", dp, 1), swap(first_u[1], "dp", dp, 2)]
        igl = after(igl, *first_u)
        sent_i, kept_i = weight_grad("inner", (0, 1, 2, 3), Z_ORDER, me, hid_t, igl)
        got_i = swap(sent_i, "fsdp", fsdp, 1)
        third = pairs // 3
        part_one = attend(0, third, do=after(att_g, sent_i), branch=branch)
        pair_i = (kept_i, after(got_i, part_one[0]))
        first_i = first_pair(pair_i, 96)
        over_i = [swap(first_i[0], "dp", dp, 1), swap(first_i[1], "dp", dp, 2)]
        g, sum_three = attend(third, pairs, do=after(att_g, *first_i), branch=branch, before=part_one)
    else:
        g, sum_three = attend(0, pairs, do=att_g, branch=branch)
        in_grad, _ = input_grad(g, fsg, wa)

    if direct:
        here = lambda: ()
        sent_a, kept_a = weight_grad(
            "attend", (0, 1, 2, 3), (0, 1, 2, 3), me, left_a, g, (sum_one, sum_two, sum_three, ib_sum)
        )
        over_u = [after(v, kept_a) for v in over_u]
        second_u = second_pair(pair_u, *over_u, 96)
        onward_u = [swap(second_u[0], "dp", dp, 2), swap(second_u[1], "dp", dp, 1)]

        in_grad, token = input_grad(g, after(fsg, *second_u), wa)
        over_i = [after(v, token) for v in over_i]
        second_i = second_pair(pair_i, *over_i, 96, LONG)
        onward_i = [swap(second_i[0], "dp", dp, 2), swap(second_i[1], "dp", dp, 1)]

        got_a = swap(sent_a, "fsdp", fsdp, 1)
        pair_a = (kept_a, after(got_a, *second_i))
        first_a = first_pair(pair_a, 104)
        over_a = [swap(first_a[0], "dp", dp, 1), swap(first_a[1], "dp", dp, 2)]

        onward_u = [after(v, *first_a) for v in onward_u]
        keep_u, send_u = last_pair(pair_u, over_u, onward_u)
        near_u = swap(send_u, "fsdp", fsdp, 2)

        onward_i = [after(v, keep_u) for v in onward_i]
        keep_i, send_i = last_pair(pair_i, over_i, onward_i, LONG)
        near_i = swap(send_i, "fsdp", fsdp, 2)

        near_u = after(near_u, keep_i)
        (next_u,) = combine(((), [(96, [(keep_u, lambda: (1,)), (near_u, lambda: (1,))])]))
        last_u = swap(next_u, "fsdp", fsdp, 4)

        over_a = [after(v, next_u) for v in over_a]
        second_a = second_pair(pair_a, *over_a, 104)
        onward_a = [swap(second_a[0], "dp", dp, 2), swap(second_a[1], "dp", dp, 1)]

        near_i = after(near_i, *second_a)
        (next_i,) = combine(((), [(96, [(keep_i, lambda: (1,)), (near_i, lambda: (1,))])]), cost=LONG)
        last_i = swap(next_i, "fsdp", fsdp, 4)

        last_u = after(last_u, next_i)
        terms_u = [(keep_u, lambda: (0,)), (near_u, lambda: (0,)), (last_u, here)]
        (own_u,) = combine(((), [(96, terms_u)]))

        last_i = after(last_i, own_u)
        terms_i = [(keep_i, lambda: (0,)), (near_i, lambda: (0,)), (last_i, here)]
        (own_i,) = combine(((), [(96, terms_i)]))

        onward_a = [after(v, own_i) for v in onward_a]
        whole_a = combine(*[((), last_terms(pair_a, over_a, onward_a, 104, lambda j=j: j)) for j in range(4)])
        far_a = [swap(whole_a[j], "fsdp", fsdp, 2 * j) for j in (1, 2, 3)]

        (own_m,) = combine(((), [(96, [(after(own_i, whole_a[0]), here)]), (96, [(own_u, here)])]))
        every = spread(own_m, dp)

        far_a[0] = after(far_a[0], own_m)
        own_a, small_own = finish((whole_a[0], *far_a))
        all_a = spread(own_a, dp)
        small_grads = [small_own[n, :part] for n in range(8)] + [small_own[0, 128 : 128 + blocks * part]]
        i_g, u_g = deliver_two(me, every)
        q_g, k_g, v_g, o_g = deliver_four(me, all_a)
    else:
        vec_sum = jnp.concatenate([sum_three[:2], sum_two[2:5], sum_one[5:8]])
        vec_sum = vec_sum.reshape(8, fsdp, part).transpose(1, 0, 2).reshape(fsdp, 8 * part)
        ib_part = ib_sum.reshape(fsdp, blocks * part)
        small_sum = lax.psum(jnp.concatenate([vec_sum, ib_part], axis=1), ("dp", "fsdp"))
        small_own = lax.dynamic_index_in_dim(small_sum, f, 0, keepdims=False)
        small_grads = [small_own[n * part : (n + 1) * part] for n in range(8)] + [small_own[8 * part :]]
        x_t, att_t = left_a[0], left_a[1]
        locals_ = (
            dot_nn(x_t, g[0]),
            dot_nn(x_t, g[1]),
            dot_nn(x_t, g[2]),
            dot_nn(att_t, g[3]),
            jnp.concatenate([dot_nn(hid_t, igl[n]) for n in range(blocks)], axis=1),
            dot_nn(act_t, low),
        )
        owned = [lax.psum_scatter(w, "fsdp", scatter_dimension=0, tiled=True) for w in locals_]
        q_g, k_g, v_g, o_g, i_g, u_g = (lax.psum(w.astype(BF16), "dp").astype(F32) for w in owned)

    qb, vb, ob, g1, s1, ub, g2, s2, ibg = small_grads
    return (
        out.reshape(docs, seq, width),
        in_grad.reshape(docs, seq, width),
        q_g,
        qb,
        k_g,
        v_g,
        vb,
        o_g,
        ob,
        g1,
        s1,
        i_g,
        ibg,
        u_g,
        ub,
        g2,
        s2,
    )


def solution(mesh):
    rows, row = P("fsdp", None), P("fsdp")
    docs = P(("dp", "fsdp"), None, None)
    in_specs = (docs, P(("dp", "fsdp")), docs, rows, row, rows, rows, row, rows, row, row, row, rows, row, rows, row, row, row)
    out_specs = (docs, docs, rows, row, rows, rows, row, rows, row, row, row, rows, row, rows, row, row, row)
    sizes = (mesh.shape["dp"], mesh.shape["fsdp"])
    return jax.shard_map(
        functools.partial(on_device, sizes), mesh=mesh, in_specs=in_specs, out_specs=out_specs, check_vma=False
    )
```

```python
import functools
import math

import jax
import jax.numpy as jnp
from jax import lax
from jax.experimental import pallas as pl
from jax.experimental.pallas import tpu as pltpu
from jax.sharding import PartitionSpec as P

F32 = jnp.float32
BF16 = jnp.bfloat16
HD = 64
MASKED = -1e30
SCALE = HD ** -0.5
EPSILON = 1e-12
ROOT_HALF = math.sqrt(0.5)
INV_ROOT_TWO_PI = 1.0 / math.sqrt(2.0 * math.pi)

VM = pl.BlockSpec(memory_space=pltpu.VMEM)
SM = pl.BlockSpec(memory_space=pltpu.SMEM)
HB = pl.BlockSpec(memory_space=pl.ANY)
FREE = pl.CostEstimate(flops=0, bytes_accessed=0, transcendentals=0)

LONG = pl.CostEstimate(flops=60_000_000_000, bytes_accessed=0, transcendentals=0)


def shape(*dims, dtype=BF16):
    return jax.ShapeDtypeStruct(dims, dtype)


def local(*dims, dtype=BF16):
    return pltpu.VMEM(dims, dtype)


def stay(*values):
    return tuple(pltpu.with_memory_space_constraint(v, pltpu.VMEM) for v in values)


def far_off(*values):
    return tuple(pltpu.with_memory_space_constraint(v, pltpu.HBM) for v in values)


def limit(mebibytes):
    return pltpu.CompilerParams(vmem_limit_bytes=mebibytes << 20)


def dot_nn(a, b):
    return lax.dot_general(a, b, (((1,), (0,)), ((), ())), preferred_element_type=F32)


def dot_nt(a, b):
    return lax.dot_general(a, b, (((1,), (1,)), ((), ())), preferred_element_type=F32)


def flip(value):
    return value.T


def column_sum(value):
    return jnp.sum(value.astype(F32), axis=0, keepdims=True)


def row_mean(value):
    return jnp.mean(value, axis=-1, keepdims=True)


def aligned(start, size):
    return pl.ds(pl.multiple_of(start, size), size)


class Pieces:
    def __init__(self, held, arrays, own, sibling, far, far_sibling, stacked, packs=()):
        self.held, self.arrays, self.own, self.sibling, self.packs = held, arrays, own, sibling, packs
        self.far, self.far_sibling, self.stacked = far, far_sibling, stacked

    def count(self):
        return len(self.own)

    def place(self, target, block, z_at, c_at, offset, rows):
        if self.stacked:
            return target.at[block, aligned_rows((2 * z_at + c_at) * 96 + offset, rows), :]
        return target.at[aligned_rows((2 * z_at + c_at) * 384 + block * 96 + offset, rows), :]

    def copies(self, held, me_ref, target, sems, base):
        z, c = me_ref[1], me_ref[2]
        done = []
        for block, (position, row, lane) in enumerate(self.own):
            where = self.place(target, block, z, c, 0, 96)
            source = held[position].at[pl.ds(row, 96), pl.ds(lane, 768)]
            done.append(pltpu.make_async_copy(source, where, sems.at[base + block]))
        return done

    def fill(self, refs, me_ref, target, rest=(0, 1, 2, 3)):
        i, z, c = me_ref[0], me_ref[1], me_ref[2]
        for block, (position, tile) in enumerate(self.sibling if 0 in rest else ()):
            self.place(target, block, z, 1 - c, 0, 96)[...] = refs[position][tile]
        for c_at, far in ((c, self.far), (1 - c, self.far_sibling)):
            for away in rest:
                parts = far[away]
                for position, tile, row, rows, offset in parts:

                    def copy(j, carry, position=position, tile=tile, row=row, rows=rows, offset=offset, away=away, c_at=c_at):
                        where = self.place(target, i ^ away, z ^ j, c_at, offset, rows)
                        where[...] = refs[position][tile + j - 1, row : row + rows, :]
                        return carry

                    lax.fori_loop(1, 4, copy, 0)

    def vectors(self, refs, me_ref, target):
        z, c = me_ref[1], me_ref[2]
        own, mine, other = (refs[n] for n in self.packs)
        for j in range(4):
            target[2 * (z ^ j) + c] = (mine[j - 1, 96:104, :] if j else own[96:104, :]).astype(F32)
            target[2 * (z ^ j) + 1 - c] = other[13, 8 * j : 8 * j + 8, :].astype(F32)


def bundle_body(group_count, held, me_ref, *refs):
    sources, near = refs[: len(held)], refs[len(held) : -2]
    out_ref, sems = refs[-2:]
    own = [(n, row, lane) for n, spots in enumerate(held) for row, lane in spots]
    loads = []
    for tile, (n, row, lane) in enumerate(own):
        source = sources[n].at[pl.ds(row, 96), pl.ds(lane, 768)]
        loads.append(pltpu.make_async_copy(source, out_ref.at[tile], sems.at[tile]))
    start_all(loads)
    tile = len(own)
    for away in range(3):
        for group in range(group_count):
            for j in range(3):
                out_ref[tile] = near[away * group_count + group][j, :96, :]
                tile += 1
    if group_count == 1:
        out_ref[tile, 0:8, :] = near[3][96:104, :]
        for j in range(3):
            out_ref[tile, 8 * j + 8 : 8 * j + 16, :] = near[0][j, 96:104, :]
        out_ref[tile, 32:, :] = jnp.zeros((64, 768), BF16)
    wait_all(loads)


def bundle(group_count, sources, held, near):
    own = sum(len(spots) for spots in held)
    tiles = own + 9 * group_count + (group_count == 1)
    return pl.pallas_call(
        functools.partial(bundle_body, group_count, held),
        out_shape=local(tiles, 96, 768),
        in_specs=[SM] + [HB] * len(sources) + [VM] * len(near),
        out_specs=VM,
        scratch_shapes=[pltpu.SemaphoreType.DMA((own,))],
        compiler_params=limit(2),
        cost_estimate=FREE,
        name="bundle",
    )(jnp.zeros((1,), jnp.int32), *far_off(*sources), *stay(*near))


def aligned_rows(start, rows):
    return pl.ds(pl.multiple_of(start, 16), rows)


class Whole:
    def __init__(self, held, arrays, spots, stacked):
        self.held, self.arrays, self.spots, self.stacked = held, arrays, spots, stacked

    def count(self):
        return len(self.spots)

    def copies(self, held, me_ref, target, sems, base):
        done = []
        for block, (position, row, lane) in enumerate(self.spots):
            where = target.at[block] if self.stacked else target.at[pl.ds(block * 768, 768), :]
            source = held[position].at[pl.ds(row, 768), pl.ds(lane, 768)]
            done.append(pltpu.make_async_copy(source, where, sems.at[base + block]))
        return done

    def fill(self, refs, me_ref, target, rest=()):
        pass

    def vectors(self, refs, me_ref, target):
        target[...] = refs[0][...].astype(F32)


def start_all(copies):
    for copy in copies:
        copy.start()


def wait_all(copies):
    for copy in copies:
        copy.wait()


def pair_masks(dims, axis):
    spot = lax.broadcasted_iota(jnp.int32, dims, axis)
    return spot < HD, spot >= HD


def keep(mask, value):
    return jnp.where(mask, value, jnp.zeros_like(value))


def attend_forward_body(group, part, me_ref, len_ref, x_ref, *refs):
    held, refs = refs[: len(group.held)], refs[len(group.held) :]
    sources = refs[: len(group.arrays)]
    q_ref, k_ref, v_ref, att_ref, left_ref, lse_ref, w_ref, vec_ref, ib_ref, packed, sems = refs[len(group.arrays) :]
    seq, width = x_ref.shape
    tile = min(512, seq)
    loads = group.copies(held, me_ref, w_ref, sems, 0)
    start_all(loads)
    group.fill(sources, me_ref, w_ref)
    group.vectors(sources, me_ref, packed)
    for f in range(packed.shape[0]):
        pack = packed[f]
        vec_ref[:, f * part : (f + 1) * part] = pack[:, :part]
        row, lane = divmod(f * 4 * part, width)
        ib_ref[row : row + 1, lane : lane + 4 * part] = pack[:1, 128 : 128 + 4 * part]
    for p in range(width // 128):
        left_ref[0, p * 128 : (p + 1) * 128, :] = flip(x_ref[:, p * 128 : (p + 1) * 128])
    wait_all(loads)

    def project(r, carry):
        rows = aligned(r * tile, tile)
        x = x_ref[rows, :]
        q_ref[rows, :] = (dot_nn(x, w_ref[0]) + vec_ref[0:1, :]).astype(BF16)
        k_ref[rows, :] = dot_nn(x, w_ref[1]).astype(BF16)
        v_ref[rows, :] = (dot_nn(x, w_ref[2]) + vec_ref[1:2, :]).astype(BF16)
        return carry

    lax.fori_loop(0, seq // tile, project, 0)
    length = len_ref[0]

    def pair(p, carry):
        lanes = aligned(p * 128, 128)
        k_pair = k_ref[:, lanes]
        q_t = (q_ref[:, lanes].astype(F32) * SCALE).T.astype(BF16)
        v_t = flip(v_ref[:, lanes])
        masks = pair_masks((128, seq), 0)
        allowed = lax.broadcasted_iota(jnp.int32, (seq, seq), 0) < length
        for e in range(2):
            s = dot_nn(k_pair, keep(masks[e], q_t))
            s = jnp.where(allowed, s, MASKED)
            top = jnp.max(s, axis=0, keepdims=True)
            p_t = jnp.exp(s - top)
            total = jnp.sum(p_t, axis=0, keepdims=True)
            o_t = dot_nn(v_t[e * HD : (e + 1) * HD, :], p_t.astype(BF16)) * (1.0 / total)
            left_ref[1, aligned(p * 128 + e * HD, HD), :] = o_t.astype(BF16)
            lse_ref[pl.ds(p * 2 + e, 1), :] = top + jnp.log(total)
        att_ref[:, lanes] = flip(left_ref[1, aligned(p * 128, 128), :])
        return carry

    lax.fori_loop(0, width // 128, pair, 0, unroll=2)


def attend_forward(group, shards, blocks, me, length, x):
    seq, width = x.shape
    heads = width // HD
    return pl.pallas_call(
        functools.partial(attend_forward_body, group, width // shards),
        out_shape=(local(seq, width),) * 4
        + (local(2, width, seq), local(-(-heads // 8) * 8, seq, dtype=F32), local(4, width, width))
        + (local(8, width, dtype=F32), local(blocks, width, dtype=F32)),
        in_specs=[SM, SM, VM] + [HB] * len(group.held) + [VM] * len(group.arrays),
        out_specs=[VM] * 9,
        scratch_shapes=[pltpu.VMEM((shards, 8, width), F32), pltpu.SemaphoreType.DMA((group.count(),))],
        compiler_params=limit(10),
        cost_estimate=FREE,
        name="attend_forward",
    )(me, length, x, *far_off(*group.held), *stay(*group.arrays))


def attend_backward_body(first, last, len_ref, q_ref, k_ref, v_ref, do_ref, lse_ref, branch_ref, *refs):
    g_ref, sum_ref = refs[-2:]
    seq, width = q_ref.shape
    length = len_ref[0]

    def pair(p, carry):
        lanes = aligned(p * 128, 128)
        q_pair = (q_ref[:, lanes].astype(F32) * SCALE).astype(BF16)
        k_pair = k_ref[:, lanes]
        v_pair = v_ref[:, lanes]
        do_pair = do_ref[:, lanes]
        q_t = flip(q_pair)
        k_t = (k_pair.astype(F32) * SCALE).T.astype(BF16)
        do_t = flip(do_pair)
        sub_masks = pair_masks((128, seq), 0)
        lane_masks = pair_masks((seq, 128), 1)
        allowed = lax.broadcasted_iota(jnp.int32, (seq, seq), 0) < length
        dk = jnp.zeros((seq, 128), F32)
        dv = jnp.zeros((seq, 128), F32)
        dq_t = []
        for e in range(2):
            s = dot_nn(k_pair, keep(sub_masks[e], q_t))
            s = jnp.where(allowed, s, MASKED)
            p_t = jnp.exp(s - lse_ref[pl.ds(p * 2 + e, 1), :])
            dp = dot_nn(v_pair, keep(sub_masks[e], do_t))
            dv = dv + dot_nn(p_t.astype(BF16), keep(lane_masks[e], do_pair))
            t = p_t * dp
            row = jnp.sum(t, axis=0, keepdims=True)
            ds = (t - p_t * row).astype(BF16)
            dk = dk + dot_nn(ds, keep(lane_masks[e], q_pair))
            dq_t.append(dot_nn(k_t[e * HD : (e + 1) * HD, :], ds))
        dq = jnp.concatenate(dq_t, axis=0).T.astype(BF16)
        dv = dv.astype(BF16)
        g_ref[0, :, lanes] = dq
        g_ref[1, :, lanes] = dk.astype(BF16)
        g_ref[2, :, lanes] = dv
        g_ref[3, :, lanes] = branch_ref[:, lanes]
        sum_ref[0:1, lanes] = column_sum(dq)
        sum_ref[1:2, lanes] = column_sum(dv)
        return carry

    lax.fori_loop(first, last, pair, 0, unroll=2)


def attend_backward(first, last, length, q, k, v, do, lse, branch, before=()):
    seq, width = q.shape
    return pl.pallas_call(
        functools.partial(attend_backward_body, first, last),
        out_shape=(local(4, seq, width), local(8, width, dtype=F32)),
        in_specs=[SM] + [VM] * 6 + [HB] * len(before),
        out_specs=[VM] * 2,
        input_output_aliases={7 + n: n for n in range(len(before))},
        compiler_params=limit(10),
        cost_estimate=FREE,
        name="attend_backward",
    )(length, *stay(q, k, v, do, lse, branch, *before))


def gelu_parts(inner):
    cumulative = 0.5 * (1.0 + lax.erf(inner * ROOT_HALF))
    density = jnp.exp(-0.5 * inner * inner) * INV_ROOT_TWO_PI
    return inner * cumulative, cumulative + inner * density


def fill_body(group, early, me_ref, *refs):
    held, near = refs[: len(group.held)], refs[len(group.held) : len(group.held) + len(group.arrays)]
    if not early:
        group.fill(near, me_ref, refs[-1])
        return
    target, sems = refs[-2:]
    loads = group.copies(held, me_ref, target, sems, 0)
    start_all(loads)
    group.fill(near, me_ref, target)
    wait_all(loads)


def fill(group, me, *dims, before=None):
    early = before is None
    more = () if early else (before,)
    return pl.pallas_call(
        functools.partial(fill_body, group, early),
        out_shape=local(*dims),
        in_specs=[SM] + [HB] * len(group.held) + [VM] * len(group.arrays) + [HB] * len(more),
        out_specs=VM,
        scratch_shapes=[pltpu.SemaphoreType.DMA((group.count(),))] * early,
        input_output_aliases={} if early else {1 + len(group.held) + len(group.arrays): 0},
        compiler_params=limit(2),
        cost_estimate=FREE,
        name="fill",
    )(me, *far_off(*group.held), *stay(*group.arrays, *more))


def middle_forward_body(
    len_ref,
    x_ref,
    att_ref,
    cot_ref,
    vec_ref,
    ib_ref,
    wa,
    wi,
    wu,
    out_ref,
    ssg_ref,
    low_ref,
    actT_ref,
    slope_ref,
    norm_ref,
    rstd_ref,
    hidT_ref,
    sum_ref,
):
    seq, width = x_ref.shape
    blocks = wi.shape[0]
    tile = min(512, seq)
    length = len_ref[0]
    sum_ref[...] = jnp.zeros_like(sum_ref)

    def rows_step(r, carry):
        rows = aligned(r * tile, tile)
        first = x_ref[rows, :].astype(F32) + dot_nn(att_ref[rows, :], wa[3]) + vec_ref[2:3, :]
        center = first - row_mean(first)
        rstd = lax.rsqrt(row_mean(center * center) + EPSILON)
        normed = center * rstd
        norm_ref[rows, :] = normed
        rstd_ref[rows, :] = rstd
        hidden = normed * vec_ref[3:4, :] + vec_ref[4:5, :]
        low = hidden.astype(BF16)
        hidT_ref[:, rows] = low.astype(F32).T.astype(BF16)

        def block(f, second):
            inner = dot_nn(low, wi[f]) + ib_ref[pl.ds(f, 1), :]
            active, slope = gelu_parts(inner)
            active = active.astype(BF16)
            spot = aligned(f * width, width)
            slope_ref[rows, spot] = slope.astype(BF16)
            actT_ref[spot, rows] = flip(active)
            return second + dot_nn(active, wu[spot, :])

        second = lax.fori_loop(0, blocks, block, hidden + vec_ref[5:6, :], unroll=True)
        center = second - row_mean(second)
        rstd = lax.rsqrt(row_mean(center * center) + EPSILON)
        normed = center * rstd
        spot = r * tile + lax.broadcasted_iota(jnp.int32, (tile, width), 0)
        valid = spot < length
        result = normed * vec_ref[6:7, :] + vec_ref[7:8, :]
        out_ref[rows, :] = jnp.where(valid, result, 0.0).astype(BF16)
        grad = jnp.where(valid, cot_ref[rows, :].astype(F32), 0.0)
        sum_ref[7:8, :] += column_sum(grad)
        sum_ref[6:7, :] += column_sum(grad * normed)
        grad = grad * vec_ref[6:7, :]
        grad = rstd * (grad - row_mean(grad) - normed * row_mean(grad * normed))
        ssg_ref[rows, :] = grad
        low = grad.astype(BF16)
        low_ref[rows, :] = low
        sum_ref[5:6, :] += column_sum(low)
        return carry

    lax.fori_loop(0, seq // tile, rows_step, 0)


def middle_forward(length, x, att, cot, vec, ib, wa, wi, wu):
    seq, width = x.shape
    blocks = ib.shape[0]
    return pl.pallas_call(
        middle_forward_body,
        out_shape=(
            shape(seq, width),
            local(seq, width, dtype=F32),
            local(seq, width),
            local(blocks * width, seq),
            local(seq, blocks * width),
            local(seq, width, dtype=F32),
            local(seq, 1, dtype=F32),
            local(width, seq),
            local(8, width, dtype=F32),
        ),
        in_specs=[SM] + [VM] * 8,
        out_specs=[VM] * 9,
        compiler_params=limit(16),
        cost_estimate=FREE,
        name="middle_forward",
    )(length, x, *stay(att), cot, *stay(vec, ib, wa, wi, wu))


def middle_backward_body(
    low_ref, ssg_ref, slope_ref, norm_ref, rstd_ref, vec_ref, wa, wi, wu, igl_ref, fsg_ref, branch_ref, att_ref, ib_ref, sum_ref
):
    seq, width = low_ref.shape
    blocks = wi.shape[0]
    tile = min(512, seq)
    sum_ref[...] = jnp.zeros_like(sum_ref)
    ib_ref[...] = jnp.zeros_like(ib_ref)

    def rows_step(r, carry):
        rows = aligned(r * tile, tile)
        low = low_ref[rows, :]

        def block(f, grad):
            spot = aligned(f * width, width)
            inner = (dot_nt(low, wu[spot, :]) * slope_ref[rows, spot].astype(F32)).astype(BF16)
            igl_ref[f, rows, :] = inner
            ib_ref[pl.ds(f, 1), :] += column_sum(inner)
            return grad + dot_nt(inner, wi[f])

        grad = lax.fori_loop(0, blocks, block, ssg_ref[rows, :], unroll=True)
        normed = norm_ref[rows, :]
        sum_ref[4:5, :] += column_sum(grad)
        sum_ref[3:4, :] += column_sum(grad * normed)
        grad = grad * vec_ref[3:4, :]
        grad = rstd_ref[rows, :] * (grad - row_mean(grad) - normed * row_mean(grad * normed))
        fsg_ref[rows, :] = grad
        branch = grad.astype(BF16)
        branch_ref[rows, :] = branch
        sum_ref[2:3, :] += column_sum(branch)
        att_ref[rows, :] = dot_nt(branch, wa[3]).astype(BF16)
        return carry

    lax.fori_loop(0, seq // tile, rows_step, 0)


def middle_backward(low, ssg, slope, norm, rstd, vec, wa, wi, wu):
    seq, width = low.shape
    blocks = wi.shape[0]
    return pl.pallas_call(
        middle_backward_body,
        out_shape=(
            local(blocks, seq, width),
            local(seq, width, dtype=F32),
            local(seq, width),
            local(seq, width),
            local(blocks, width, dtype=F32),
            local(8, width, dtype=F32),
        ),
        in_specs=[VM] * 9,
        out_specs=[VM] * 6,
        compiler_params=limit(16),
        cost_estimate=FREE,
        name="middle_backward",
    )(*stay(low, ssg, slope, norm, rstd, vec, wa, wi, wu))


def input_grad_body(g_ref, fsg_ref, w_ref, out_ref, token_ref):
    seq, width = fsg_ref.shape
    token_ref[...] = jnp.zeros_like(token_ref)
    tile = min(512, seq)

    def rows_step(r, carry):
        rows = aligned(r * tile, tile)
        total = fsg_ref[rows, :]
        for n in range(3):
            total = total + dot_nt(g_ref[n, rows, :], w_ref[n])
        out_ref[rows, :] = total
        return carry

    lax.fori_loop(0, seq // tile, rows_step, 0)


def input_grad(g, fsg, wa):
    seq, width = fsg.shape
    return pl.pallas_call(
        input_grad_body,
        out_shape=(shape(seq, width, dtype=F32), local(8, 128, dtype=F32)),
        in_specs=[VM] * 3,
        out_specs=[VM] * 2,
        compiler_params=limit(12),
        cost_estimate=FREE,
        name="input_grad",
    )(*stay(g, fsg, wa))


Z_ORDER = (0, 2, 1, 3)


def weight_grad_body(kind, order, z_order, me_ref, left_ref, g_ref, *refs):
    sums, refs = (refs[:4], refs[4:]) if kind == "attend" else ((), refs)
    outs, left = refs[:2], refs[2]
    i, z, c = me_ref[0], me_ref[1], me_ref[2]
    part = 96
    if kind == "attend":
        extra = refs[3]
        one, two, three, ib = (r[...] for r in sums)
        row = lax.broadcasted_iota(jnp.int32, one.shape, 0)
        every = jnp.where(row < 2, three, jnp.where(row < 5, two, one))
        for f in range(8):
            extra[f] = jnp.zeros_like(extra[f])
            extra[f, :, :part] = every[:, f * part : (f + 1) * part]
            extra[f, 0:1, 128 : 128 + 4 * part] = ib[f // 2 : f // 2 + 1, f % 2 * 4 * part : (f % 2 + 1) * 4 * part]

    def gather(place, row_of, *lead):
        for side, c_at in enumerate((1 - c, c)):
            for n, j in enumerate(z_order):
                rows = left_ref[(*lead, aligned_rows(row_of(2 * (z ^ j) + c_at), 96), slice(None))]
                left[place, side * 384 + n * 96 : side * 384 + (n + 1) * 96, :] = rows

    if kind == "inner":
        gather(0, lambda f_at: f_at * 96)
    elif kind == "attend":
        gather(0, lambda f_at: f_at * 96, 0)
        gather(1, lambda f_at: f_at * 96, 1)

    def block_step(spot, carry):
        block = i ^ pick(order, spot)
        if kind == "outer":
            gather(0, lambda f_at: f_at * 384 + block * 96)
        right = g_ref[...] if kind == "outer" else g_ref[block]
        rows = left[block // 3] if kind == "attend" else left[0]
        grads = dot_nn(rows, right).reshape(2, 4, 96, 768).astype(BF16)
        for side, c_at in enumerate((1 - c, c)):
            outs[side][spot, :, :96, :] = grads[side]
            if kind == "attend":
                for n, j in enumerate(z_order):
                    outs[side][spot, n, 96:104, :] = extra[2 * (z ^ j) + c_at].astype(BF16)
        return carry

    lax.fori_loop(0, 4, block_step, 0, unroll=2)


def weight_grad(kind, order, z_order, me, left, g, sums=()):
    rows = 104 if kind == "attend" else 96
    return pl.pallas_call(
        functools.partial(weight_grad_body, kind, order, z_order),
        out_shape=(local(4, 4, rows, 768),) * 2,
        in_specs=[SM] + [VM] * (2 + len(sums)),
        out_specs=[VM] * 2,
        scratch_shapes=[pltpu.VMEM((1 + (kind == "attend"), 768, left.shape[-1]), BF16)] + [pltpu.VMEM((8, 8, 768), F32)] * (kind == "attend"),
        compiler_params=limit(6),
        cost_estimate=FREE,
        name=f"weight_grad_{kind}",
    )(me, *stay(left, g, *sums))


def prepare_body(me_ref, *refs):
    vectors, weights = refs[:9], refs[9:15]
    first_ref, second_ref, pack_ref, *rows, sems = refs[15:]
    i = me_ref[0]
    part = vectors[0].shape[0]
    copies = [
        pltpu.make_async_copy(
            weights[4].at[:, pl.ds(pl.multiple_of(i * 768, 768), 768)], second_ref.at[pl.ds(0, 96), :], sems.at[0]
        ),
        pltpu.make_async_copy(weights[5].at[aligned_rows(i * 96, 96), :], second_ref.at[pl.ds(96, 96), :], sems.at[1]),
    ]
    for n in range(9):
        copies.append(pltpu.make_async_copy(vectors[n], rows[n], sems.at[3 + n]))
    for n in range(4):

        @pl.when(i == n)
        def _():
            pltpu.make_async_copy(weights[n], first_ref.at[pl.ds(0, 96), :], sems.at[2]).start()

    start_all(copies)
    pack_ref[...] = jnp.zeros_like(pack_ref)
    wait_all(copies[2:])
    for n in range(8):
        pack_ref[n : n + 1, :part] = rows[n][...].astype(F32).reshape(1, part)
    pack_ref[0:1, 128 : 128 + 4 * part] = rows[8][...].astype(F32).reshape(1, 4 * part)
    first_ref[96:104, :] = pack_ref[...].astype(BF16)
    pltpu.make_async_copy(weights[0], first_ref.at[pl.ds(0, 96), :], sems.at[2]).wait()
    wait_all(copies[:2])


def prepare(me, vectors, weights):
    return pl.pallas_call(
        prepare_body,
        out_shape=(local(104, 768), local(192, 768)),
        in_specs=[SM] + [HB] * 15,
        out_specs=[VM] * 2,
        scratch_shapes=[pltpu.VMEM((8, 768), F32)]
        + [pltpu.VMEM(v.shape, BF16) for v in vectors]
        + [pltpu.SemaphoreType.DMA((12,))],
        compiler_params=limit(2),
        cost_estimate=FREE,
        name="prepare",
    )(me, *far_off(*vectors, *weights))


def after(value, *others, cost=FREE):
    def body(*refs):
        pass

    return pl.pallas_call(
        body,
        out_shape=jax.ShapeDtypeStruct(value.shape, value.dtype),
        in_specs=[HB] * (1 + len(others)),
        out_specs=HB,
        input_output_aliases={0: 0},
        compiler_params=limit(1),
        cost_estimate=cost,
        name="after",
    )(value, *others)


def swap(value, axis, size, mask):
    return lax.ppermute(value, axis, [(n, n ^ mask) for n in range(size)])


def combine(*outs, cost=FREE):
    arrays = []
    for _, parts in outs:
        for _, terms in parts:
            arrays += [a for a, _ in terms if not any(a is b for b in arrays)]

    def find(array):
        return next(n for n, b in enumerate(arrays) if b is array)

    def body(*refs):
        for out_ref, (lead, parts) in zip(refs[len(arrays) :], outs, strict=True):

            def tile(index):
                start = 0
                for rows, terms in parts:
                    found = [(find(array), at(*index)) for array, at in terms]
                    values = [refs[n][spot] for n, spot in found if spot is not None]
                    value = values[0] if len(values) == 1 else sum(v.astype(F32) for v in values).astype(BF16)
                    out_ref[(*index, slice(start, start + rows), slice(None))] = value
                    start += rows

            def step(front, last, carry):
                tile((*front, last))
                return carry

            if not lead:
                tile(())
            elif len(lead) == 1:
                lax.fori_loop(0, lead[0], functools.partial(step, ()), 0)
            else:
                for front in range(lead[0]):
                    lax.fori_loop(0, lead[1], functools.partial(step, (front,)), 0)

    return pl.pallas_call(
        body,
        out_shape=tuple(local(*lead, sum(rows for rows, _ in parts), 768) for lead, parts in outs),
        in_specs=[VM] * len(arrays),
        out_specs=[VM] * len(outs),
        compiler_params=limit(2),
        cost_estimate=cost,
        name="combine",
    )(*stay(*arrays))


def stack(rows, *tiles, cost=FREE):
    def body(*refs):
        for n, (_, place, first) in enumerate(tiles):
            part = pl.ds(first, rows)
            refs[-1][n] = refs[n][part, :] if place is None else refs[n][place, part, :]

    return pl.pallas_call(
        body,
        out_shape=local(len(tiles), rows, 768),
        in_specs=[VM] * len(tiles),
        out_specs=VM,
        compiler_params=limit(2),
        cost_estimate=cost,
        name="stack",
    )(*stay(*(array for array, _, _ in tiles)))


def pair_up(piece, fsdp, cost=FREE):
    other = swap(piece, "fsdp", fsdp, 4)
    return other, lambda ready: stack(piece.shape[0], (piece, None, 0), (ready, None, 0), cost=cost)


def rows_of(value, start, rows):
    (part,) = combine(((value.shape[0],), [(rows, [(value, lambda n: (n, slice(start, start + rows)))])]))
    return part


UPPER = slice(0, 48)


def held(pair, block, rows):
    return [(v, lambda b: (block, b, rows)) for v in pair]


def first_pair(pair, total):
    def out(blocks, rows, size):
        terms = []
        for n, block in enumerate(blocks):
            for array, at in held(pair, block, rows):
                terms.append((array, lambda a, b, n=n, at=at: at(b) if a == n else None))
        return (2, 4), [(size, terms)]

    return combine(out((1, 3), UPPER, 48), out((2, 3), slice(48, total), total - 48))


def second_pair(pair, over_x, over_y, total, cost=FREE):
    x = held(pair, 2, UPPER) + [(over_x, lambda b: (1, b))]
    y = held(pair, 1, slice(48, total)) + [(over_y, lambda b: (1, b))]
    return combine(((4,), [(48, x)]), ((4,), [(total - 48, y)]), cost=cost)


def last_terms(pair, overs, onwards, total, tile):
    parts = []
    for rows, size, over, onward in (
        (UPPER, 48, overs[0], onwards[0]),
        (slice(48, total), total - 48, overs[1], onwards[1]),
    ):
        terms = [(array, lambda *n, at=at: at(tile(*n))) for array, at in held(pair, 0, rows)]
        terms += [(over, lambda *n: (0, tile(*n))), (onward, lambda *n: (tile(*n),))]
        parts.append((size, terms))
    return parts


def last_pair(pair, overs, onwards, cost=FREE):
    return combine(*[((2,), last_terms(pair, overs, onwards, 96, lambda b, k=k: k + b)) for k in (0, 2)], cost=cost)


def finish(terms):
    def body(*refs):
        terms, (own_ref, small_ref) = refs[:-2], refs[-2:]
        value = sum(r[...].astype(F32) for r in terms)
        own_ref[...] = value[:96].astype(BF16)
        small_ref[...] = value[96:]

    return pl.pallas_call(
        body,
        out_shape=(local(96, 768), local(8, 768, dtype=F32)),
        in_specs=[VM] * len(terms),
        out_specs=[VM] * 2,
        compiler_params=limit(2),
        cost_estimate=FREE,
        name="finish",
    )(*stay(*terms))


def spread(value, dp):
    return (value,) + tuple(swap(value, "dp", dp, m) for m in (1, 2, 3))


def deliver_two(me, every):
    def body(me_ref, *refs):
        inner_ref, outer_ref = refs[4:]
        for away in range(4):
            block = me_ref[0] ^ away
            inner_ref[:, aligned(block * 768, 768)] = refs[away][:96, :].astype(F32)
            outer_ref[aligned(block * 96, 96), :] = refs[away][96:, :].astype(F32)

    return pl.pallas_call(
        body,
        out_shape=(shape(96, 3072, dtype=F32), shape(384, 768, dtype=F32)),
        in_specs=[SM] + [VM] * 4,
        out_specs=[VM] * 2,
        compiler_params=limit(6),
        cost_estimate=FREE,
        name="deliver_two",
    )(me, *stay(*every))


def deliver_four(me, every):
    def body(me_ref, *refs):
        outs, held_ref = refs[4:8], refs[8]
        for away in range(4):
            held_ref[me_ref[0] ^ away] = refs[away][...]
        for n in range(4):
            outs[n][...] = held_ref[n].astype(F32)

    return pl.pallas_call(
        body,
        out_shape=(shape(96, 768, dtype=F32),) * 4,
        in_specs=[SM] + [VM] * 4,
        out_specs=[VM] * 4,
        scratch_shapes=[pltpu.VMEM((4, 96, 768), BF16)],
        compiler_params=limit(4),
        cost_estimate=FREE,
        name="deliver_four",
    )(me, *stay(*every))


def pick(pieces, index):
    return jnp.where(index == 0, pieces[0], jnp.where(index == 1, pieces[1], jnp.where(index == 2, pieces[2], pieces[3])))


def on_device(
    sizes,
    tokens,
    lengths,
    cotangent,
    query_weight,
    query_bias,
    key_weight,
    value_weight,
    value_bias,
    output_weight,
    output_bias,
    first_gain,
    first_shift,
    inner_weight,
    inner_bias,
    outer_weight,
    outer_bias,
    second_gain,
    second_shift,
):
    dp, fsdp = sizes
    docs, seq, width = tokens.shape
    blocks = inner_weight.shape[1] // width
    direct = dp == 4 and fsdp == 8 and docs == 1 and query_weight.shape == (96, 768) and blocks == 4
    i = lax.axis_index("dp")
    f = lax.axis_index("fsdp")
    me = jnp.stack([i, f // 2, f % 2, jnp.zeros_like(i)]).astype(jnp.int32)

    small = (query_bias, value_bias, output_bias, first_gain, first_shift, outer_bias, second_gain, second_shift, inner_bias)
    part = query_bias.shape[0]

    if direct:
        mine = (query_weight, key_weight, value_weight, output_weight)
        piece_a, piece_m = prepare(me, small, mine + (inner_weight, outer_weight))
        other_a, with_a = pair_up(piece_a, fsdp)
        other_m, with_m = pair_up(piece_m, fsdp, LONG)
        pair_a = with_a(other_a)
        beside_a = swap(pair_a, "fsdp", fsdp, 2)
        mine_a = stack(104, (beside_a, 0, 0), (other_a, None, 0), (beside_a, 1, 0))
        other_m = after(other_m, mine_a)
        beside_m = swap(with_m(other_m), "fsdp", fsdp, 2)
        plane_a = (swap(mine_a, "dp", dp, 1), swap(mine_a, "dp", dp, 2))
        plane_a = tuple(after(v, other_m) for v in plane_a)
        parts_a = (rows_of(plane_a[0], 0, 48), rows_of(plane_a[1], 48, 48))
        rest_a = (swap(parts_a[0], "dp", dp, 2), swap(parts_a[1], "dp", dp, 1))
        beside_m = after(beside_m, *rest_a)
        inner_m, outer_m = (stack(96, (beside_m, 0, n), (other_m, None, n), (beside_m, 1, n)) for n in (0, 96))
        over_x = [swap(inner_m, "dp", dp, 1), None]
        over_y = [None, swap(outer_m, "dp", dp, 2)]
        over_x[1], over_y[0] = swap(outer_m, "dp", dp, 1), swap(inner_m, "dp", dp, 2)
        near_a = bundle(1, mine, ((((0, 0)),),) * 4, (after(mine_a, inner_m),) + plane_a + (piece_a,))
        far_a = (swap(near_a, "fsdp", fsdp, 1),) + tuple(swap(v, "fsdp", fsdp, 1) for v in rest_a)

        def far_at(base, row=0):
            return [[(base + n, 0, row, 96, 0)] for n in range(3)]

        group_a = Pieces(
            mine,
            (mine_a,) + plane_a + rest_a + far_a + (piece_a,),
            [(n, 0, 0) for n in range(4)],
            [(5, n) for n in range(4)],
            far_at(0) + [[(3, 0, 0, 48, 0), (4, 0, 0, 48, 48)]],
            [[(5, 4 + 3 * n, 0, 96, 0)] for n in range(3)] + [[(6, 0, 0, 48, 0), (7, 0, 0, 48, 48)]],
            True,
            (8, 0, 5),
        )
        x = tokens.reshape(seq, width)
        q, k, v, att, left_a, lse, wa, vec, ib = attend_forward(group_a, fsdp, blocks, me, lengths, after(x, inner_m))
        over_x[0], over_y[1] = after(over_x[0], att), after(over_y[1], att)
        rest_m = (swap(over_x[0], "dp", dp, 2), swap(over_y[1], "dp", dp, 1))
        spots = (tuple((0, 768 * n) for n in range(4)), tuple((96 * n, 0) for n in range(4)))

        def spots_of(n):
            return [(0, *spot) for spot in spots[n]]

        planes = ((inner_m, outer_m), over_x, over_y)
        near_m = bundle(2, (inner_weight, outer_weight), spots, tuple(v for plane in planes for v in plane))
        far_m = swap(near_m, "fsdp", fsdp, 1)
        empty = [[]]
        near_i = Pieces((inner_weight,), (inner_m, over_x[0], over_y[0]), spots_of(0), (), far_at(0) + empty, empty * 4, True)
        near_u = Pieces((outer_weight,), (outer_m, over_x[1], over_y[1]), spots_of(1), (), far_at(0) + empty, empty * 4, False)
        wi = fill(near_i, me, blocks, width, width)
        wu = fill(near_u, me, blocks * width, width)
        rest_m = [after(v, near_m, wi, wu, cost=LONG) for v in rest_m]
        far_rest = [swap(v, "fsdp", fsdp, 1) for v in rest_m]
        far_m = after(far_m, *rest_m)

        def from_sibling(first, tile, stacked):
            far = [[(0, tile + 6 * n, 0, 96, 0)] for n in range(3)] + empty
            return Pieces((), (far_m,), (), [(0, first + n) for n in range(4)], empty * 4, far, stacked)

        def late(n, stacked):
            arrays = (rest_m[n], far_rest[n])
            return Pieces((), arrays, (), (), empty * 3 + [[(0, 0, 0, 96, 0)]], empty * 3 + [[(1, 0, 0, 96, 0)]], stacked)

        wi = fill(from_sibling(0, 8, True), me, blocks, width, width, before=wi)
        wu = fill(from_sibling(4, 11, False), me, blocks * width, width, before=wu)
        far_rest[0] = after(far_rest[0], wi, wu)
        wi = fill(late(0, True), me, blocks, width, width, before=wi)
        wu = fill(late(1, False), me, blocks * width, width, before=wu)
    else:
        whole = tuple(
            lax.all_gather(w, "fsdp", axis=0, tiled=True)
            for w in (query_weight, key_weight, value_weight, output_weight, inner_weight, outer_weight)
        )
        packs = jnp.pad(jnp.stack(small[:8]), ((0, 0), (0, width - part)))
        packs = packs + jnp.pad(inner_bias[None], ((0, 7), (128, width - 128 - 4 * part)))
        packs = lax.all_gather(packs, "fsdp", axis=0, tiled=False)
        group_a = Whole(whole[:4], (packs,), [(n, 0, 0) for n in range(4)], True)
        group_i = Whole(whole[4:5], (), [(0, 0, width * n) for n in range(blocks)], True)
        group_u = Whole(whole[5:6], (), [(0, width * n, 0) for n in range(blocks)], False)
        x = tokens.reshape(seq, width)
        q, k, v, att, left_a, lse, wa, vec, ib = attend_forward(group_a, fsdp, blocks, me, lengths, x)
        wi = fill(group_i, me, blocks, width, width)
        wu = fill(group_u, me, blocks * width, width)

    cot = cotangent.reshape(seq, width)
    out, ssg, low, act_t, slope, norm, rstd, hid_t, sum_one = middle_forward(lengths, x, att, cot, vec, ib, wa, wi, wu)
    pairs = width // 128
    attend = functools.partial(attend_backward, length=lengths, q=q, k=k, v=v, lse=lse)
    if direct:
        sent_u, kept_u = weight_grad("outer", (0, 1, 2, 3), Z_ORDER, me, act_t, low)
        got_u = swap(sent_u, "fsdp", fsdp, 1)
        low = after(low, sent_u)
    igl, fsg, branch, att_g, ib_sum, sum_two = middle_backward(low, ssg, slope, norm, rstd, vec, wa, wi, wu)
    if direct:
        pair_u = (kept_u, after(got_u, igl))
        first_u = first_pair(pair_u, 96)
        over_u = [swap(first_u[0], "dp", dp, 1), swap(first_u[1], "dp", dp, 2)]
        igl = after(igl, *first_u)
        sent_i, kept_i = weight_grad("inner", (0, 1, 2, 3), Z_ORDER, me, hid_t, igl)
        got_i = swap(sent_i, "fsdp", fsdp, 1)
        third = pairs // 3
        part_one = attend(0, third, do=after(att_g, sent_i), branch=branch)
        pair_i = (kept_i, after(got_i, part_one[0]))
        first_i = first_pair(pair_i, 96)
        over_i = [swap(first_i[0], "dp", dp, 1), swap(first_i[1], "dp", dp, 2)]
        g, sum_three = attend(third, pairs, do=after(att_g, *first_i), branch=branch, before=part_one)
    else:
        g, sum_three = attend(0, pairs, do=att_g, branch=branch)
        in_grad, _ = input_grad(g, fsg, wa)

    if direct:
        here = lambda: ()
        sent_a, kept_a = weight_grad(
            "attend", (0, 1, 2, 3), (0, 1, 2, 3), me, left_a, g, (sum_one, sum_two, sum_three, ib_sum)
        )
        over_u = [after(v, kept_a) for v in over_u]
        second_u = second_pair(pair_u, *over_u, 96)
        onward_u = [swap(second_u[0], "dp", dp, 2), swap(second_u[1], "dp", dp, 1)]

        in_grad, token = input_grad(g, after(fsg, *second_u), wa)
        over_i = [after(v, token) for v in over_i]
        second_i = second_pair(pair_i, *over_i, 96, LONG)
        onward_i = [swap(second_i[0], "dp", dp, 2), swap(second_i[1], "dp", dp, 1)]

        got_a = swap(sent_a, "fsdp", fsdp, 1)
        pair_a = (kept_a, after(got_a, *second_i))
        first_a = first_pair(pair_a, 104)
        over_a = [swap(first_a[0], "dp", dp, 1), swap(first_a[1], "dp", dp, 2)]

        onward_u = [after(v, *first_a) for v in onward_u]
        keep_u, send_u = last_pair(pair_u, over_u, onward_u)
        near_u = swap(send_u, "fsdp", fsdp, 2)

        onward_i = [after(v, keep_u) for v in onward_i]
        keep_i, send_i = last_pair(pair_i, over_i, onward_i, LONG)
        near_i = swap(send_i, "fsdp", fsdp, 2)

        near_u = after(near_u, keep_i)
        (next_u,) = combine(((), [(96, [(keep_u, lambda: (1,)), (near_u, lambda: (1,))])]))
        last_u = swap(next_u, "fsdp", fsdp, 4)

        over_a = [after(v, next_u) for v in over_a]
        second_a = second_pair(pair_a, *over_a, 104)
        onward_a = [swap(second_a[0], "dp", dp, 2), swap(second_a[1], "dp", dp, 1)]

        near_i = after(near_i, *second_a)
        (next_i,) = combine(((), [(96, [(keep_i, lambda: (1,)), (near_i, lambda: (1,))])]), cost=LONG)
        last_i = swap(next_i, "fsdp", fsdp, 4)

        last_u = after(last_u, next_i)
        terms_u = [(keep_u, lambda: (0,)), (near_u, lambda: (0,)), (last_u, here)]
        (own_u,) = combine(((), [(96, terms_u)]))

        last_i = after(last_i, own_u)
        terms_i = [(keep_i, lambda: (0,)), (near_i, lambda: (0,)), (last_i, here)]
        (own_i,) = combine(((), [(96, terms_i)]))

        onward_a = [after(v, own_i) for v in onward_a]
        whole_a = combine(*[((), last_terms(pair_a, over_a, onward_a, 104, lambda j=j: j)) for j in range(4)])
        far_a = [swap(whole_a[j], "fsdp", fsdp, 2 * j) for j in (1, 2, 3)]

        (own_m,) = combine(((), [(96, [(after(own_i, whole_a[0]), here)]), (96, [(own_u, here)])]))
        every = spread(own_m, dp)

        far_a[0] = after(far_a[0], own_m)
        own_a, small_own = finish((whole_a[0], *far_a))
        all_a = spread(own_a, dp)
        small_grads = [small_own[n, :part] for n in range(8)] + [small_own[0, 128 : 128 + blocks * part]]
        i_g, u_g = deliver_two(me, every)
        q_g, k_g, v_g, o_g = deliver_four(me, all_a)
    else:
        vec_sum = jnp.concatenate([sum_three[:2], sum_two[2:5], sum_one[5:8]])
        vec_sum = vec_sum.reshape(8, fsdp, part).transpose(1, 0, 2).reshape(fsdp, 8 * part)
        ib_part = ib_sum.reshape(fsdp, blocks * part)
        small_sum = lax.psum(jnp.concatenate([vec_sum, ib_part], axis=1), ("dp", "fsdp"))
        small_own = lax.dynamic_index_in_dim(small_sum, f, 0, keepdims=False)
        small_grads = [small_own[n * part : (n + 1) * part] for n in range(8)] + [small_own[8 * part :]]
        x_t, att_t = left_a[0], left_a[1]
        locals_ = (
            dot_nn(x_t, g[0]),
            dot_nn(x_t, g[1]),
            dot_nn(x_t, g[2]),
            dot_nn(att_t, g[3]),
            jnp.concatenate([dot_nn(hid_t, igl[n]) for n in range(blocks)], axis=1),
            dot_nn(act_t, low),
        )
        owned = [lax.psum_scatter(w, "fsdp", scatter_dimension=0, tiled=True) for w in locals_]
        q_g, k_g, v_g, o_g, i_g, u_g = (lax.psum(w.astype(BF16), "dp").astype(F32) for w in owned)

    qb, vb, ob, g1, s1, ub, g2, s2, ibg = small_grads
    return (
        out.reshape(docs, seq, width),
        in_grad.reshape(docs, seq, width),
        q_g,
        qb,
        k_g,
        v_g,
        vb,
        o_g,
        ob,
        g1,
        s1,
        i_g,
        ibg,
        u_g,
        ub,
        g2,
        s2,
    )


def solution(mesh):
    rows, row = P("fsdp", None), P("fsdp")
    docs = P(("dp", "fsdp"), None, None)
    in_specs = (docs, P(("dp", "fsdp")), docs, rows, row, rows, rows, row, rows, row, row, row, rows, row, rows, row, row, row)
    out_specs = (docs, docs, rows, row, rows, rows, row, rows, row, row, row, rows, row, rows, row, row, row)
    sizes = (mesh.shape["dp"], mesh.shape["fsdp"])
    return jax.shard_map(
        functools.partial(on_device, sizes), mesh=mesh, in_specs=in_specs, out_specs=out_specs, check_vma=False
    )
```
